32 devices in a mesh: dp: 16 (over z, x, core), mp: 2 (over y).
Axes of the slice: x: 2, y: 2, z: 4, core: 2. Of those that a mesh axis runs over, the one named last changes fastest.
Arguments:
- tokens_in: bfloat16 [32768, 1024], P('dp'), may hold values from -6 to 6
- cotangent: bfloat16 [32768, 1024], P(('dp', 'mp')), may hold values from -6 to 6
- segment_ids: int32 [64, 512], P('dp'), may hold values from 0 to 3, never falling along the last dimension, each value on 1 to 256 neighbouring positions
- project_weight: float32 [3, 1024, 1024], P(None, 'dp', 'mp'), may hold values from -0.25 to 0.25
- project_momentum: float32 [3, 1024, 1024], P(None, 'dp', 'mp'), may hold values from -1536 to 1536
- project_squares: float32 [3, 1024, 1024], P(None, 'dp', 'mp'), may hold values from 32768 to 524288
- output_weight: float32 [1024, 1024], P('dp', 'mp'), may hold values from -0.75 to 0.75
- output_momentum: float32 [1024, 1024], P('dp', 'mp'), may hold values from -256 to 256
- output_squares: float32 [1024, 1024], P('dp', 'mp'), may hold values from 983.04 to 16384
- up_weight: float32 [1024, 4096], P('dp', 'mp'), may hold values from -0.1875 to 0.1875
- up_momentum: float32 [1024, 4096], P('dp', 'mp'), may hold values from -320 to 320
- up_squares: float32 [1024, 4096], P('dp', 'mp'), may hold values from 1638.4 to 26214.4
- down_weight: float32 [1024, 4096], P('dp', 'mp'), may hold values from -0.09375 to 0.09375
- down_momentum: float32 [1024, 4096], P('dp', 'mp'), may hold values from -640 to 640
- down_squares: float32 [1024, 4096], P('dp', 'mp'), may hold values from 6553.6 to 98304
- norm_params: float32 [4, 1024], P(None, ('dp', 'mp')), as said below
- norm_momentum: float32 [4, 1024], P(None, ('dp', 'mp')), may hold values from -1024 to 1024
- norm_squares: float32 [4, 1024], P(None, ('dp', 'mp')), may hold values from 16384 to 262144
Outputs:
- layer_out: bfloat16 [32768, 1024], P(('dp', 'mp'))
- input_grad: float32 [32768, 1024], P(('dp', 'mp'))
- project_grad: float32 [3, 1024, 1024], P(None, 'dp', 'mp')
- project_moment: float32 [3, 1024, 1024], P(None, 'dp', 'mp')
- project_square: float32 [3, 1024, 1024], P(None, 'dp', 'mp')
- project_updated: float32 [3, 1024, 1024], P(None, 'dp', 'mp')
- output_grad: float32 [1024, 1024], P('dp', 'mp')
- output_moment: float32 [1024, 1024], P('dp', 'mp')
- output_square: float32 [1024, 1024], P('dp', 'mp')
- output_updated: float32 [1024, 1024], P('dp', 'mp')
- up_grad: float32 [1024, 4096], P('dp', 'mp')
- up_moment: float32 [1024, 4096], P('dp', 'mp')
- up_square: float32 [1024, 4096], P('dp', 'mp')
- up_updated: float32 [1024, 4096], P('dp', 'mp')
- down_grad: float32 [1024, 4096], P('dp', 'mp')
- down_moment: float32 [1024, 4096], P('dp', 'mp')
- down_square: float32 [1024, 4096], P('dp', 'mp')
- down_updated: float32 [1024, 4096], P('dp', 'mp')
- norm_grad: float32 [4, 1024], P(None, ('dp', 'mp'))
- norm_moment: float32 [4, 1024], P(None, ('dp', 'mp'))
- norm_square: float32 [4, 1024], P(None, ('dp', 'mp'))
- norm_updated: float32 [4, 1024], P(None, ('dp', 'mp'))
The draws below stay inside these ranges and needn't reach their ends.
Inputs may be any that keep to these rules, and one draw needn't show every extreme that they name: `segment_ids`: along each row the segment number never falls; a segment holds 1 to 256 tokens, and in every row one holds exactly that many. `norm_params`: gains lie in 0.6 to 1.4 and shifts in -0.3 to 0.3.
All inputs are finite; a program needn't handle non-finite values.
Results may differ from the reference program's by a relative error of at most 0.02.
The reference program's roundings to bfloat16 on the way count: a program that leaves them out, or rounds other values in their place, can miss the bound.
Values may be sent and summed in bfloat16 or wider, within the bound.
A program may use at most 256 MiB of HBM per device.

```python
import math
import jax
import jax.numpy as jnp
import numpy as np
from jax import lax

D = 1024
HEADS = 16
HEAD_DIM = 64
FF = 4096
SEQ = 512
SEGS = 4
STEP = 3
ROWS_DEV = 4
ROWS = 64
TOKENS = 32768
N_DP = 16


def norm_table(key):
    gain_key, shift_key = jax.random.split(key)
    gains = jax.random.uniform(gain_key, (2, D), jnp.float32, 0.6, 1.4)
    shifts = jax.random.uniform(shift_key, (2, D), jnp.float32, -0.3, 0.3)
    return jnp.stack([gains[0], shifts[0], gains[1], shifts[1]])


def draw_norm_params(key, part):
    return norm_table(jax.random.fold_in(key, 11))


def block_levels(stream_key, extent, cuts, least, high):
    loudness, own = 1.0, jax.random.fold_in(stream_key, 6)
    for dim, blocks in cuts:
        draws = jnp.exp(jax.random.uniform(jax.random.fold_in(own, dim), (blocks,), jnp.float32, least / len(cuts), high / len(cuts)))
        loudness = loudness * jnp.repeat(draws, extent[dim] // blocks).reshape([-1 if axis == dim else 1 for axis in range(len(extent))])
    return loudness


def length_profile(count, total, most, lean):
    weights = [(1 << 20) // math.isqrt(grade ** lean) + 1 for grade in range(2, count + 1)]
    surplus, given = total - most - (count - 1), [1] * (count - 1)
    while surplus > 0:
        candidates = [i for i in range(count - 1) if given[i] < most]
        pool, remaining = sum([weights[i] for i in candidates]), surplus
        for i in candidates:
            extra = min(most - given[i], max(1, remaining * weights[i] // pool), surplus)
            given[i] = given[i] + extra
            surplus = surplus - extra
    return np.array([most] + given)


def ragged_sizes(own_key, count, total, limit, skew):
    if count == 2:
        one = jax.random.randint(own_key, (), max(1, total - limit), min(limit, total - 1) + 1)
        return jnp.stack([one, total - one])
    tallies = jnp.asarray(length_profile(count, total, limit, skew), jnp.int32)
    pairs = (count - 1) // 2
    giver, sink = tallies[1:1 + 2 * pairs:2], tallies[2:2 + 2 * pairs:2]
    margin = jnp.minimum(giver - 1, limit - sink)
    moved = jax.random.randint(jax.random.fold_in(own_key, 1), (pairs,), 0, 1 << 20) % (margin + 1)
    tallies = tallies.at[1:1 + 2 * pairs:2].set(giver - moved).at[2:2 + 2 * pairs:2].set(sink + moved)
    return tallies[jax.random.permutation(jax.random.fold_in(own_key, 2), count)]


def scatter_about(own_key, dims, deviation, bound, cuts=(), kind=jnp.bfloat16):
    loudness = block_levels(own_key, dims, cuts, -0.22, 0.18) if cuts else 1.0
    values = jax.random.normal(own_key, dims, jnp.float32) * deviation * loudness
    return jnp.minimum(jnp.maximum(values, -bound), bound).astype(kind)


def setup_inputs(seed: int = 0) -> dict:
    key_of = jax.random.split(jax.random.key(seed), 19)
    tokens_in = scatter_about(key_of[0], (TOKENS, D), 1.0, 6.0, ((0, 16),))
    cotangent = scatter_about(key_of[1], (TOKENS, D), 1.0, 6.0, ((0, 32),))
    segment_ids = jax.vmap(lambda own: jnp.searchsorted(jnp.cumsum(ragged_sizes(own, SEGS, SEQ, SEQ // 2, 1)), jnp.arange(SEQ), side="right"))(jax.random.split(key_of[2], ROWS)).reshape((ROWS, SEQ)).astype(jnp.int32)
    project_weight = scatter_about(key_of[3], (3, D, D), (D // 2) ** -0.5, 0.25, ((1, 16), (2, 2)), jnp.float32)
    project_momentum = scatter_about(key_of[4], (3, D, D), (1.4 * TOKENS ** 0.5), 1536.0, ((1, 16), (2, 2)), jnp.float32)
    project_squares = jnp.clip(jnp.exp(math.log(524288.0) - 2.7725887 * jax.random.uniform(key_of[5], (3, D, D), jnp.float32) ** block_levels(key_of[5], (3, D, D), ((1, 16), (2, 2)), -0.2, 0.2)), 32768.0, 524288.0)
    output_weight = scatter_about(key_of[6], (D, D), (D // 16) ** -0.5, 0.75, ((0, 16), (1, 2)), jnp.float32)
    output_momentum = scatter_about(key_of[7], (D, D), (0.25 * TOKENS ** 0.5), 256.0, ((0, 16), (1, 2)), jnp.float32)
    output_squares = jnp.clip(jnp.exp(math.log(16384.0) - 2.8134107 * jax.random.uniform(key_of[8], (D, D), jnp.float32) ** block_levels(key_of[8], (D, D), ((0, 16), (1, 2)), -0.2, 0.2)), 983.04, 16384.0)
    up_weight = scatter_about(key_of[9], (D, FF), D ** -0.5, 0.1875, ((0, 16), (1, 2)), jnp.float32)
    up_momentum = scatter_about(key_of[10], (D, FF), (0.3 * TOKENS ** 0.5), 320.0, ((0, 16), (1, 2)), jnp.float32)
    up_squares = jnp.clip(jnp.exp(math.log(26214.4) - 2.7725887 * jax.random.uniform(key_of[11], (D, FF), jnp.float32) ** block_levels(key_of[11], (D, FF), ((0, 16), (1, 2)), -0.2, 0.2)), 1638.4, 26214.4)
    down_weight = scatter_about(key_of[12], (D, FF), FF ** -0.5, 0.09375, ((0, 16), (1, 2)), jnp.float32)
    down_momentum = scatter_about(key_of[13], (D, FF), (0.6 * TOKENS ** 0.5), 640.0, ((0, 16), (1, 2)), jnp.float32)
    down_squares = jnp.clip(jnp.exp(math.log(98304.0) - 2.7080502 * jax.random.uniform(key_of[14], (D, FF), jnp.float32) ** block_levels(key_of[14], (D, FF), ((0, 16), (1, 2)), -0.2, 0.2)), 6553.6, 98304.0)
    norm_params = draw_norm_params(jax.random.fold_in(key_of[18], 71), 0)
    norm_momentum = scatter_about(key_of[16], (4, D), (TOKENS ** 0.5), 1024.0, ((1, 32),), jnp.float32)
    norm_squares = jnp.clip(jnp.exp(math.log(262144.0) - 2.7725887 * jax.random.uniform(key_of[17], (4, D), jnp.float32) ** block_levels(key_of[17], (4, D), ((1, 32),), -0.2, 0.2)), 16384.0, 262144.0)
    return dict(tokens_in=tokens_in, cotangent=cotangent, segment_ids=segment_ids, project_weight=project_weight, project_momentum=project_momentum, project_squares=project_squares, output_weight=output_weight, output_momentum=output_momentum, output_squares=output_squares, up_weight=up_weight, up_momentum=up_momentum, up_squares=up_squares, down_weight=down_weight, down_momentum=down_momentum, down_squares=down_squares, norm_params=norm_params, norm_momentum=norm_momentum, norm_squares=norm_squares)


HIGHEST = lax.Precision.HIGHEST
EPS_NORM = 1e-12
NEG_FILL = -1e+30
BETA_ONE = 0.5
BETA_TWO = 0.5
ADAM_EPS = 1e-08
DECAY_RATE = 0.01

@jax.custom_vjp
def low(v):
    return lax.optimization_barrier(v.astype(jnp.bfloat16)).astype(jnp.float32)

@jax.custom_vjp
def low_back(v):
    return v

def low_keep(v):
    return (low(v), None)

def low_pass(kept, grad):
    return (grad,)

def back_keep(v):
    return (v, None)

def back_low(kept, grad):
    return (low(grad),)
low.defvjp(low_keep, low_pass)
low_back.defvjp(back_keep, back_low)

def layer_norm(values, norm_gain, norm_shift):
    center = values - lax.optimization_barrier(jnp.mean(values, axis=-1, keepdims=True))
    spread = lax.optimization_barrier(jnp.mean(center * center, axis=-1, keepdims=True))
    return center * lax.rsqrt(spread + EPS_NORM) * norm_gain + norm_shift

def exact_gelu(values):
    return jax.nn.gelu(values, approximate=False)

def row_attend(packed):
    query_rows, key_rows, value_rows, row_segments = packed
    scores = jnp.einsum('qhd,khd->hqk', query_rows, key_rows, precision=HIGHEST) * HEAD_DIM ** (-0.5)
    scores = low_back(scores)
    same_doc = row_segments[:, None] == row_segments[None, :]
    scores = jnp.where(same_doc[None], scores, NEG_FILL)
    row_probs = low(jax.nn.softmax(scores, axis=-1))
    mixed = jnp.einsum('hqk,khd->qhd', row_probs, value_rows, precision=HIGHEST)
    return mixed.reshape(SEQ, D)

def layer_forward(token_rows, segments, proj_master, out_master, up_master, down_master, norm_master):
    proj_copy = low(proj_master)
    out_copy = low(out_master)
    up_copy = low(up_master)
    down_copy = low(down_master)
    norm_copy = low(norm_master)
    projected = low_back(low(jnp.einsum('tc,scn->stn', token_rows, proj_copy, precision=HIGHEST)))
    heads_split = projected.reshape(3, ROWS_DEV, SEQ, HEADS, HEAD_DIM)
    context = lax.map(jax.checkpoint(row_attend), (heads_split[0], heads_split[1], heads_split[2], segments))
    context = low_back(low(context.reshape(ROWS_DEV * SEQ, D)))
    attended = low_back(jnp.einsum('tn,dn->td', context, out_copy, precision=HIGHEST))
    hidden_one = layer_norm(token_rows + attended, norm_copy[0], norm_copy[1])
    pre_act = low_back(jnp.dot(low(hidden_one), up_copy, precision=HIGHEST, preferred_element_type=jnp.float32))
    activated = low(exact_gelu(pre_act))
    ffn_out = low_back(jnp.einsum('tf,df->td', activated, down_copy, precision=HIGHEST))
    return layer_norm(hidden_one + ffn_out, norm_copy[2], norm_copy[3])

def adam_step(gradient, weight, first_old, second, step_rate):
    correct_one = 1.0 - BETA_ONE ** STEP
    correct_two = 1.0 - BETA_TWO ** STEP
    moment = BETA_ONE * first_old + (1.0 - BETA_ONE) * gradient
    square = BETA_TWO * second + (1.0 - BETA_TWO) * gradient * gradient
    normed = moment / correct_one / (jnp.sqrt(square / correct_two) + ADAM_EPS)
    updated = weight - step_rate * (normed + DECAY_RATE * weight)
    return (gradient, moment, square, updated)

def reference(tokens_in, cotangent, segment_ids, project_weight, project_momentum, project_squares, output_weight, output_momentum, output_squares, up_weight, up_momentum, up_squares, down_weight, down_momentum, down_squares, norm_params, norm_momentum, norm_squares):
    masters = (project_weight, output_weight, up_weight, down_weight, norm_params)
    group_tokens = ROWS_DEV * SEQ
    token_groups = tokens_in.astype(jnp.float32).reshape(N_DP, group_tokens, D)
    grad_groups = cotangent.astype(jnp.float32).reshape(N_DP, group_tokens, D)
    segment_groups = segment_ids.reshape(N_DP, ROWS_DEV, SEQ)

    def one_group(totals, packed):
        tokens, grad_rows, segments = packed

        def forward(token_rows, proj_master, out_master, up_master, down_master, norm_master):
            return layer_forward(token_rows, segments, proj_master, out_master, up_master, down_master, norm_master)
        result, backward = jax.vjp(forward, tokens, *masters)
        pulled = backward(grad_rows)
        totals = tuple((former + latter for former, latter in zip(totals, pulled[1:])))
        return (totals, (result, pulled[0]))
    initial = tuple((jnp.zeros_like(member) for member in masters))
    grad_sums, (results, input_grads) = lax.scan(one_group, initial, (token_groups, grad_groups, segment_groups))
    layer_out = results.reshape(ROWS * SEQ, D).astype(jnp.bfloat16)
    input_grad = input_grads.reshape(ROWS * SEQ, D)
    proj_new = adam_step(grad_sums[0], project_weight, project_momentum, project_squares, D ** (-0.5))
    out_new = adam_step(grad_sums[1], output_weight, output_momentum, output_squares, 4.0 * D ** (-0.5))
    up_new = adam_step(grad_sums[2], up_weight, up_momentum, up_squares, D ** (-0.5))
    down_new = adam_step(grad_sums[3], down_weight, down_momentum, down_squares, FF ** (-0.5))
    norm_new = adam_step(grad_sums[4], norm_params, norm_momentum, norm_squares, 0.3)
    return (layer_out, input_grad, proj_new[0], proj_new[1], proj_new[2], proj_new[3], out_new[0], out_new[1], out_new[2], out_new[3], up_new[0], up_new[1], up_new[2], up_new[3], down_new[0], down_new[1], down_new[2], down_new[3], norm_new[0], norm_new[1], norm_new[2], norm_new[3])
```

```python
import functools

import jax
import jax.numpy as jnp
from jax import lax
from jax.experimental import pallas as pl
from jax.experimental.pallas import tpu as pltpu
from jax.sharding import PartitionSpec as P

D = 1024
HEAD_DIM = 64
FF = 4096
STEP = 3


EPS_NORM = 1e-12
NEG_FILL = -1e30
BETA_ONE = 0.5
BETA_TWO = 0.5
ADAM_EPS = 1e-08
DECAY_RATE = 0.01


def layer_norm(values, norm_gain, norm_shift):
    center = values - jnp.mean(values, axis=-1, keepdims=True)
    spread = jnp.mean(center * center, axis=-1, keepdims=True)
    return center * lax.rsqrt(spread + EPS_NORM) * norm_gain + norm_shift


def exact_gelu(values):
    return jax.nn.gelu(values, approximate=False)


def adam_step(gradient, weight, first_old, second, step_rate):
    correct_one = 1.0 - BETA_ONE**STEP
    correct_two = 1.0 - BETA_TWO**STEP
    moment = BETA_ONE * first_old + (1.0 - BETA_ONE) * gradient
    square = BETA_TWO * second + (1.0 - BETA_TWO) * gradient * gradient
    normed = moment / correct_one / (jnp.sqrt(square / correct_two) + ADAM_EPS)
    updated = weight - step_rate * (normed + DECAY_RATE * weight)
    return (gradient, moment, square, updated)


def local_plain(
    tokens_in,
    cotangent,
    segment_ids,
    project_weight,
    project_momentum,
    project_squares,
    output_weight,
    output_momentum,
    output_squares,
    up_weight,
    up_momentum,
    up_squares,
    down_weight,
    down_momentum,
    down_squares,
    norm_params,
    norm_momentum,
    norm_squares,
):
    gathered = (
        lax.all_gather(project_weight.astype(jnp.bfloat16), "dp", axis=1, tiled=True),
        lax.all_gather(output_weight.astype(jnp.bfloat16), "dp", axis=0, tiled=True),
        lax.all_gather(up_weight.astype(jnp.bfloat16), "dp", axis=0, tiled=True),
        lax.all_gather(down_weight.astype(jnp.bfloat16), "dp", axis=0, tiled=True),
    )
    proj_copy, out_copy, up_copy, down_copy = gathered
    norm_full = lax.all_gather(
        norm_params.astype(jnp.bfloat16), ("dp", "mp"), axis=1, tiled=True
    ).astype(jnp.float32)
    rows_here = segment_ids.shape[0]
    seq_len = segment_ids.shape[1]
    local_width = proj_copy.shape[2]
    heads_here = local_width // HEAD_DIM
    score_scale = HEAD_DIM ** (-0.5)
    projected = jnp.einsum(
        "tc,scn->stn", tokens_in, proj_copy, preferred_element_type=jnp.float32
    ).astype(jnp.bfloat16)
    heads_split = projected.reshape(3, rows_here, seq_len, heads_here, HEAD_DIM)

    def masked_scores(query_rows, key_rows, row_segments):
        scores = (
            jnp.einsum("qhd,khd->hqk", query_rows, key_rows, preferred_element_type=jnp.float32)
            * score_scale
        )
        same_doc = row_segments[:, None] == row_segments[None, :]
        return jnp.where(same_doc[None], scores, NEG_FILL)

    def row_forward(packed):
        query_rows, key_rows, value_rows, row_segments = packed
        scores = masked_scores(query_rows, key_rows, row_segments)
        row_max = jnp.max(scores, axis=-1, keepdims=True)
        row_exp = jnp.exp(scores - row_max)
        row_total = jnp.sum(row_exp, axis=-1, keepdims=True)
        row_probs = (row_exp / row_total).astype(jnp.bfloat16)
        mixed = jnp.einsum(
            "hqk,khd->qhd", row_probs, value_rows, preferred_element_type=jnp.float32
        )
        row_lse = (row_max + jnp.log(row_total))[..., 0]
        return (mixed.astype(jnp.bfloat16).reshape(seq_len, local_width), row_lse)

    context_rows, lse_rows = lax.map(
        row_forward, (heads_split[0], heads_split[1], heads_split[2], segment_ids)
    )
    context = context_rows.reshape(rows_here * seq_len, local_width)
    attn_part = jnp.einsum("tn,dn->td", context, out_copy, preferred_element_type=jnp.float32)
    attn_share = lax.psum_scatter(
        attn_part.astype(jnp.bfloat16), "mp", scatter_dimension=0, tiled=True
    ).astype(jnp.float32)
    share_rows = attn_share.shape[0]
    share_start = lax.axis_index("mp") * share_rows
    token_share = lax.dynamic_slice_in_dim(tokens_in, share_start, share_rows, 0).astype(
        jnp.float32
    )
    hidden_one, norm_one_back = jax.vjp(
        layer_norm, token_share + attn_share, norm_full[0], norm_full[1]
    )
    hidden_low = lax.all_gather(hidden_one.astype(jnp.bfloat16), "mp", axis=0, tiled=True)
    pre_act = jnp.dot(hidden_low, up_copy, preferred_element_type=jnp.float32)
    act_full, gelu_back = jax.vjp(exact_gelu, pre_act)
    act_low = act_full.astype(jnp.bfloat16)
    ffn_part = jnp.einsum("tf,df->td", act_low, down_copy, preferred_element_type=jnp.float32)
    ffn_share = lax.psum_scatter(
        ffn_part.astype(jnp.bfloat16), "mp", scatter_dimension=0, tiled=True
    ).astype(jnp.float32)
    result, norm_two_back = jax.vjp(layer_norm, hidden_one + ffn_share, norm_full[2], norm_full[3])
    layer_out = result.astype(jnp.bfloat16)
    regathered = (
        lax.all_gather(project_weight.astype(jnp.bfloat16), "dp", axis=1, tiled=True),
        lax.all_gather(output_weight.astype(jnp.bfloat16), "dp", axis=0, tiled=True),
        lax.all_gather(up_weight.astype(jnp.bfloat16), "dp", axis=0, tiled=True),
        lax.all_gather(down_weight.astype(jnp.bfloat16), "dp", axis=0, tiled=True),
    )
    proj_copy, out_copy, up_copy, down_copy = regathered
    d_resid_two, d_gain_two, d_shift_two = norm_two_back(cotangent.astype(jnp.float32))
    d_ffn = lax.all_gather(d_resid_two.astype(jnp.bfloat16), "mp", axis=0, tiled=True)
    down_grad = jnp.einsum("td,tf->df", d_ffn, act_low, preferred_element_type=jnp.float32)
    d_act = jnp.dot(d_ffn, down_copy, preferred_element_type=jnp.float32)
    d_pre = gelu_back(d_act)[0].astype(jnp.bfloat16)
    up_grad = jnp.einsum("tc,tf->cf", hidden_low, d_pre, preferred_element_type=jnp.float32)
    d_hidden_part = jnp.einsum("tf,cf->tc", d_pre, up_copy, preferred_element_type=jnp.float32)
    d_hidden = d_resid_two + lax.psum_scatter(
        d_hidden_part.astype(jnp.bfloat16), "mp", scatter_dimension=0, tiled=True
    ).astype(jnp.float32)
    d_resid_one, d_gain_one, d_shift_one = norm_one_back(d_hidden)
    d_attn = lax.all_gather(d_resid_one.astype(jnp.bfloat16), "mp", axis=0, tiled=True)
    output_grad = jnp.einsum("td,tn->dn", d_attn, context, preferred_element_type=jnp.float32)
    d_context = jnp.dot(d_attn, out_copy, preferred_element_type=jnp.float32).astype(jnp.bfloat16)

    def row_backward(packed):
        query_rows, key_rows, value_rows, row_segments, row_lse, row_grad = packed
        scores = masked_scores(query_rows, key_rows, row_segments)
        row_probs = jnp.exp(scores - row_lse[..., None])
        grad_heads = row_grad.reshape(seq_len, heads_here, HEAD_DIM)
        d_probs = jnp.einsum(
            "qhd,khd->hqk", grad_heads, value_rows, preferred_element_type=jnp.float32
        )
        row_inner = jnp.sum(d_probs * row_probs, axis=-1, keepdims=True)
        d_scores = (row_probs * (d_probs - row_inner)).astype(jnp.bfloat16)
        d_value = jnp.einsum(
            "hqk,qhd->khd",
            row_probs.astype(jnp.bfloat16),
            grad_heads,
            preferred_element_type=jnp.float32,
        )
        d_query = (
            jnp.einsum("hqk,khd->qhd", d_scores, key_rows, preferred_element_type=jnp.float32)
            * score_scale
        )
        d_key = (
            jnp.einsum("hqk,qhd->khd", d_scores, query_rows, preferred_element_type=jnp.float32)
            * score_scale
        )
        return (
            d_query.astype(jnp.bfloat16).reshape(seq_len, local_width),
            d_key.astype(jnp.bfloat16).reshape(seq_len, local_width),
            d_value.astype(jnp.bfloat16).reshape(seq_len, local_width),
        )

    grad_context_rows = d_context.reshape(rows_here, seq_len, local_width)
    d_rows = lax.map(
        row_backward,
        (heads_split[0], heads_split[1], heads_split[2], segment_ids, lse_rows, grad_context_rows),
    )
    d_proj = jnp.stack(d_rows).reshape(3, rows_here * seq_len, local_width)
    project_grad = jnp.einsum("tc,stn->scn", tokens_in, d_proj, preferred_element_type=jnp.float32)
    d_input_part = jnp.einsum("stn,scn->tc", d_proj, proj_copy, preferred_element_type=jnp.float32)
    input_grad = d_resid_one + lax.psum_scatter(
        d_input_part.astype(jnp.bfloat16), "mp", scatter_dimension=0, tiled=True
    ).astype(jnp.float32)
    norm_local = jnp.stack([d_gain_one, d_shift_one, d_gain_two, d_shift_two])
    norm_red = lax.psum_scatter(norm_local, ("dp", "mp"), scatter_dimension=1, tiled=True)
    proj_red, out_red, up_red, down_red = (
        lax.psum_scatter(
            project_grad.astype(jnp.bfloat16), "dp", scatter_dimension=1, tiled=True
        ).astype(jnp.float32),
        lax.psum_scatter(
            output_grad.astype(jnp.bfloat16), "dp", scatter_dimension=0, tiled=True
        ).astype(jnp.float32),
        lax.psum_scatter(
            up_grad.astype(jnp.bfloat16), "dp", scatter_dimension=0, tiled=True
        ).astype(jnp.float32),
        lax.psum_scatter(
            down_grad.astype(jnp.bfloat16), "dp", scatter_dimension=0, tiled=True
        ).astype(jnp.float32),
    )
    proj_new = adam_step(proj_red, project_weight, project_momentum, project_squares, D ** (-0.5))
    out_new = adam_step(out_red, output_weight, output_momentum, output_squares, 4.0 * D ** (-0.5))
    up_new = adam_step(up_red, up_weight, up_momentum, up_squares, D ** (-0.5))
    down_new = adam_step(down_red, down_weight, down_momentum, down_squares, FF ** (-0.5))
    norm_new = adam_step(norm_red, norm_params, norm_momentum, norm_squares, 0.3)
    return (
        layer_out,
        input_grad,
        proj_new[0],
        proj_new[1],
        proj_new[2],
        proj_new[3],
        out_new[0],
        out_new[1],
        out_new[2],
        out_new[3],
        up_new[0],
        up_new[1],
        up_new[2],
        up_new[3],
        down_new[0],
        down_new[1],
        down_new[2],
        down_new[3],
        norm_new[0],
        norm_new[1],
        norm_new[2],
        norm_new[3],
    )


MESH = pl.DeviceIdType.MESH
BF16 = jnp.bfloat16
F32 = jnp.float32
ANY = pl.BlockSpec(memory_space=pl.ANY)
VMEM = pl.BlockSpec(memory_space=pltpu.VMEM)
DMA = pltpu.SemaphoreType.DMA

HOP_X, HOP_Y, HOP_C, OWN = (0, 1, 0, 0), (0, 0, 0, 1), (0, 0, 1, 0), (0, 0, 0, 0)


def hop_z(mask):
    return (mask, 0, 0, 0)


def position():
    dp = lax.axis_index("dp")
    return (dp // 4, (dp // 2) % 2, dp % 2, lax.axis_index("mp"))


def moved(me, hop):
    return tuple(m ^ h if h else m for m, h in zip(me, hop))


def device_at(me, hop):
    z, x, c, y = moved(me, hop)
    return (z * 4 + x * 2 + c, y)


def entry_barrier(me, nz):
    barrier = pltpu.get_barrier_semaphore()
    hops = [HOP_X, HOP_Y, HOP_C] + [hop_z(a) for a in range(1, nz)]
    for hop in hops:
        pl.semaphore_signal(barrier, inc=1, device_id=device_at(me, hop), device_id_type=MESH)
    pl.semaphore_wait(barrier, len(hops))


def view_rows(ref, pos):
    z, x, c, y = pos
    half = ref.shape[4] // 2
    return ref.at[z, x, c, :, pl.ds(pl.multiple_of(y * half, half), half)]


def view_stack(ref, pos):
    z, x, c, y = pos
    half = ref.shape[5] // 2
    return ref.at[:, z, x, c, :, pl.ds(pl.multiple_of(y * half, half), half)]


class Gather:
    def __init__(self, me, nz, own, out, view, send_sem, recv_sem, base):
        self.me, self.nz, self.own, self.out, self.view = me, nz, own, out, view
        self.send_sem, self.recv_sem, self.base = send_sem, recv_sem, base
        self.sent = []

    def slot(self, rel):
        a, b, d, e = rel
        return self.base + ((a * 2 + b) * 2 + d) * 2 + e

    def piece(self, rel):
        return self.view(self.out, moved(self.me, rel))

    def copy(self, rel, hop):
        arrives = tuple(r ^ h for r, h in zip(rel, hop))
        return pltpu.make_async_remote_copy(
            src_ref=self.own if rel == OWN else self.piece(rel),
            dst_ref=self.piece(rel),
            send_sem=self.send_sem.at[self.slot(arrives)],
            recv_sem=self.recv_sem.at[self.slot(arrives)],
            device_id=device_at(self.me, hop),
            device_id_type=MESH,
        )

    def send(self, rel, hop):
        copy = self.copy(rel, hop)
        copy.start()
        self.sent.append(copy)

    def wait(self, rel):
        pltpu.make_async_remote_copy(
            src_ref=self.own,
            dst_ref=self.piece(rel),
            send_sem=self.send_sem.at[self.slot(rel)],
            recv_sem=self.recv_sem.at[self.slot(rel)],
            device_id=device_at(self.me, HOP_C),
            device_id_type=MESH,
        ).wait_recv()

    def run(self, steps):
        for kind, rel, hop in steps:
            if kind == "send":
                self.send(rel, hop)
            else:
                self.wait(rel)

    def steps_first(self):
        out = [("send", OWN, HOP_X), ("send", OWN, HOP_Y)]
        out += [("send", OWN, hop_z(a)) for a in range(1, self.nz)]
        return out + [("send", OWN, HOP_C)]

    def steps_square(self, a):
        out = [("wait", (a, 1, 0, 0), None), ("wait", (a, 0, 0, 1), None)]
        if a < self.nz // 2:
            out.append(("send", (a, 1, 0, 0), HOP_Y))
        else:
            out.append(("send", (a, 0, 0, 1), HOP_X))
        return out + [("send", (a, 1, 0, 0), HOP_C), ("send", (a, 0, 0, 1), HOP_C)]

    def steps_level(self, a):
        piece = hop_z(a)
        return [("wait", piece, None)] + [("send", piece, hop) for hop in (HOP_X, HOP_Y, HOP_C)]

    def steps_middle(self):
        out = []
        for a in range(1, self.nz):
            out += self.steps_level(a) + self.steps_square(a - 1)
        return out + self.steps_square(self.nz - 1)

    def steps_diagonal(self):
        out = []
        for a in range(self.nz):
            out += [("wait", (a, 1, 0, 1), None), ("send", (a, 1, 0, 1), HOP_C)]
        return out

    def steps_last(self):
        return [("wait", (a, b, 1, e), None) for a in range(self.nz) for b in range(2) for e in range(2)]

    def drain(self):
        for copy in self.sent:
            copy.wait_send()


def sum_hops(nz):
    hops, mask = [HOP_C, HOP_X, HOP_Y], 1
    while mask < nz:
        hops.append(hop_z(mask))
        mask *= 2
    return hops


class SmallSum:
    def __init__(self, me, nz, parts, came, send_sem, recv_sem):
        self.me, self.hops, self.parts, self.came = me, sum_hops(nz), parts, came
        self.send_sem, self.recv_sem = send_sem, recv_sem

    def copy(self, i):
        return pltpu.make_async_remote_copy(
            src_ref=self.parts.at[i],
            dst_ref=self.came.at[i],
            send_sem=self.send_sem.at[i],
            recv_sem=self.recv_sem.at[i],
            device_id=device_at(self.me, self.hops[i]),
            device_id_type=MESH,
        )

    def start(self, i):
        self.copy(i).start()

    def finish(self, i):
        self.copy(i).wait()
        self.parts[i + 1] = self.parts[i] + self.came[i]


def gather_kernel(nz, proj, out, up, down, norm, proj_all, out_all, up_all, down_all, norm_all,
                  send_sem, recv_sem, local_sem, parts, came, sum_send, sum_recv):
    me = position()
    entry_barrier(me, nz)
    n = 8 * nz
    small = SmallSum(me, nz, parts, came, sum_send, sum_recv)
    parts[0] = norm[...]
    owns, fulls = (proj, out, up, down), (proj_all, out_all, up_all, down_all)
    views = (view_stack, view_rows, view_rows, view_rows)
    gathers = [
        Gather(me, nz, owns[i], fulls[i], views[i], send_sem, recv_sem, n * i) for i in range(4)
    ]
    locals_ = [pltpu.make_async_copy(g.own, g.piece(OWN), local_sem.at[i]) for i, g in enumerate(gathers)]
    for copy in locals_:
        copy.start()
    for i in range(len(small.hops)):
        small.start(i)
        small.finish(i)
    norm_all[...] = parts[len(small.hops)]
    gathers[0].run(gathers[0].steps_first())
    for i, g in enumerate(gathers):
        g.run(g.steps_middle())
        if i + 1 < len(gathers):
            gathers[i + 1].run(gathers[i + 1].steps_first())
        g.run(g.steps_diagonal())
        g.run(g.steps_last())
    for copy in locals_:
        copy.wait()
    for g in gathers:
        g.drain()


def gather_weights(nz, proj, out, up, down, norm):
    n_sum = len(sum_hops(nz))
    full = lambda s: jax.ShapeDtypeStruct((nz, 2, 2, s.shape[0], s.shape[1] * 2), BF16)
    results = pl.pallas_call(
        functools.partial(gather_kernel, nz),
        out_shape=[
            jax.ShapeDtypeStruct((3, nz, 2, 2, proj.shape[1], proj.shape[2] * 2), BF16),
            full(out),
            full(up),
            full(down),
            jax.ShapeDtypeStruct(norm.shape, F32),
        ],
        in_specs=[ANY] * 4 + [VMEM],
        out_specs=[ANY] * 4 + [VMEM],
        scratch_shapes=[
            DMA((32 * nz,)),
            DMA((32 * nz,)),
            DMA((4,)),
            pltpu.VMEM((n_sum + 1,) + norm.shape, F32),
            pltpu.VMEM((n_sum,) + norm.shape, F32),
            DMA((n_sum,)),
            DMA((n_sum,)),
        ],
        compiler_params=pltpu.CompilerParams(collective_id=0, has_side_effects=True),
        name="gather_weights",
    )(proj, out, up, down, norm)
    proj_all, out_all, up_all, down_all, norm_all = results
    return (
        proj_all.reshape(3, D, -1),
        out_all.reshape(D, -1),
        up_all.reshape(D, -1),
        down_all.reshape(D, -1),
        norm_all,
    )


def blocks_of(ref, rows=16):
    return ref.shape[-2] // rows


def add_blocks(dst, terms, rows=16):
    lead = range(dst.shape[0]) if len(dst.shape) == 3 else (None,)

    def body(i, carry):
        start = pl.multiple_of(i * rows, rows)
        for s in lead:
            idx = (pl.ds(start, rows), slice(None)) if s is None else (s, pl.ds(start, rows), slice(None))
            total = terms[0][idx].astype(F32)
            for term in terms[1:]:
                total = total + term[idx].astype(F32)
            dst[idx] = total.astype(dst.dtype)
        return carry

    lax.fori_loop(0, dst.shape[-2] // rows, body, 0)


class Scatter:
    def __init__(self, me, nz, grad, result, view, held, from_c, from_d, from_x, from_y, from_z,
                 load_sem, send_sem, recv_sem, base):
        self.me, self.nz, self.grad, self.result, self.view = me, nz, grad, result, view
        self.held, self.from_c, self.from_d = held, from_c, from_d
        self.from_x, self.from_y, self.from_z = from_x, from_y, from_z
        self.load_sem, self.send_sem, self.recv_sem, self.base = load_sem, send_sem, recv_sem, base
        self.sent = []

    def index(self, a, b, e):
        return (a * 2 + b) * 2 + e

    def remote(self, src, dst, slot, hop):
        sem = self.base * 8 * self.nz + slot
        return pltpu.make_async_remote_copy(
            src_ref=src, dst_ref=dst, send_sem=self.send_sem.at[sem], recv_sem=self.recv_sem.at[sem],
            device_id=device_at(self.me, hop), device_id_type=MESH,
        )

    def send(self, src, dst, slot, hop):
        copy = self.remote(src, dst, slot, hop)
        copy.start()
        self.sent.append(copy)

    def wait(self, dst, slot):
        self.remote(dst, dst, slot, HOP_C).wait_recv()

    def load(self, a, b, e):
        i = self.index(a, b, e)
        return pltpu.make_async_copy(
            self.view(self.grad, moved(self.me, (a, b, 0, e))), self.held.at[i],
            self.load_sem.at[self.base * 4 * self.nz + i],
        )

    def stage_core(self, a):
        for b, e in ((1, 1), (1, 0), (0, 1), (0, 0)):
            i = self.index(a, b, e)
            self.send(self.view(self.grad, moved(self.me, (a, b, 1, e))), self.from_c.at[i], i, HOP_C)
            self.load(a, b, e).start()

    def slot_of(self, kind, a):
        return 4 * self.nz + self.nz * "dxyz".index(kind) + a

    def stage_diagonal(self, a):
        for b, e in ((1, 1), (1, 0), (0, 1), (0, 0)):
            i = self.index(a, b, e)
            self.load(a, b, e).wait()
            self.wait(self.from_c.at[i], i)
            add_blocks(self.held.at[i], [self.held.at[i], self.from_c.at[i]])
            if (b, e) == (1, 1):
                hop = HOP_Y if a < self.nz // 2 else HOP_X
                self.send(self.held.at[i], self.from_d.at[a], self.slot_of("d", a), hop)
            elif (b, e) == (1, 0) and a >= self.nz // 2:
                self.send(self.held.at[i], self.from_x.at[a], self.slot_of("x", a), HOP_X)
            elif (b, e) == (0, 1) and a < self.nz // 2:
                self.send(self.held.at[i], self.from_y.at[a], self.slot_of("y", a), HOP_Y)

    def stage_square(self, a):
        self.wait(self.from_d.at[a], self.slot_of("d", a))
        if a < self.nz // 2:
            i = self.index(a, 1, 0)
            add_blocks(self.held.at[i], [self.held.at[i], self.from_d.at[a]])
            self.send(self.held.at[i], self.from_x.at[a], self.slot_of("x", a), HOP_X)
        else:
            i = self.index(a, 0, 1)
            add_blocks(self.held.at[i], [self.held.at[i], self.from_d.at[a]])
            self.send(self.held.at[i], self.from_y.at[a], self.slot_of("y", a), HOP_Y)

    def stage_column(self, a):
        self.wait(self.from_x.at[a], self.slot_of("x", a))
        self.wait(self.from_y.at[a], self.slot_of("y", a))
        i = self.index(a, 0, 0)
        terms = [self.held.at[i], self.from_x.at[a], self.from_y.at[a]]
        if a:
            add_blocks(self.held.at[i], terms)
            self.send(self.held.at[i], self.from_z.at[a], self.slot_of("z", a), hop_z(a))
        else:
            for other in range(1, self.nz):
                self.wait(self.from_z.at[other], self.slot_of("z", other))
                terms.append(self.from_z.at[other])
            add_blocks(self.result, terms)

    def order(self):
        half = self.nz // 2
        out = []
        for k in range(half):
            out += [self.nz - 1 - k, half - 1 - k]
        return out

    def stages(self):
        order = self.order()
        calls = [(self.stage_core, a) for a in order]
        kinds = (self.stage_diagonal, self.stage_square, self.stage_column)
        for t in range(len(order) + 2):
            for lag, kind in enumerate(kinds):
                if 0 <= t - lag < len(order):
                    calls.append((kind, order[t - lag]))
        return calls

    def drain(self):
        for copy in self.sent:
            copy.wait_send()


def scatter_kernel(nz, *refs):
    grads, norm = refs[:4], refs[4]
    results, norm_all = refs[5:9], refs[9]
    buffers, rest = refs[10:34], refs[34:]
    load_sem, send_sem, recv_sem, parts, came, sum_send, sum_recv = rest
    me = position()
    entry_barrier(me, nz)
    views = (view_rows, view_rows, view_rows, view_stack)
    scatters = [
        Scatter(me, nz, grads[i], results[i], views[i], *buffers[6 * i : 6 * i + 6],
                load_sem, send_sem, recv_sem, i)
        for i in range(4)
    ]
    small = SmallSum(me, nz, parts, came, sum_send, sum_recv)
    parts[0] = norm[...]
    for i in range(len(small.hops)):
        small.start(i)
        small.finish(i)
    norm_all[...] = parts[len(small.hops)]
    for s in scatters:
        for call, a in s.stages():
            call(a)
    for s in scatters:
        s.drain()


def scatter_grads(nz, down, up, out, proj, norm):
    grads = [g.reshape(nz, 2, 2, D // (4 * nz), g.shape[1]) for g in (down, up, out)]
    grads.append(proj.reshape(3, nz, 2, 2, D // (4 * nz), proj.shape[2]))
    shapes, buffers = [], []
    for g in grads:
        piece = (g.shape[-2], g.shape[-1] // 2)
        if g.ndim == 6:
            piece = (3,) + piece
        shapes.append(jax.ShapeDtypeStruct(piece, F32))
        for count in (4 * nz, 4 * nz, nz, nz, nz, nz):
            buffers.append(pltpu.VMEM((count,) + piece, BF16))
    n_sum = len(sum_hops(nz))
    return pl.pallas_call(
        functools.partial(scatter_kernel, nz),
        out_shape=shapes + [jax.ShapeDtypeStruct(norm.shape, F32)],
        in_specs=[ANY] * 4 + [VMEM],
        out_specs=[VMEM] * 5,
        scratch_shapes=buffers
        + [
            DMA((16 * nz,)),
            DMA((32 * nz,)),
            DMA((32 * nz,)),
            pltpu.VMEM((n_sum + 1,) + norm.shape, F32),
            pltpu.VMEM((n_sum,) + norm.shape, F32),
            DMA((n_sum,)),
            DMA((n_sum,)),
        ],
        compiler_params=pltpu.CompilerParams(
            collective_id=1, has_side_effects=True, vmem_limit_bytes=56 << 20
        ),
        name="scatter_grads",
    )(*grads, norm)


def dot_f32(spec, a, b):
    return jnp.einsum(spec, a, b, preferred_element_type=F32)


def local_rows(
    tokens_in,
    cotangent,
    segment_ids,
    project_weight,
    project_momentum,
    project_squares,
    output_weight,
    output_momentum,
    output_squares,
    up_weight,
    up_momentum,
    up_squares,
    down_weight,
    down_momentum,
    down_squares,
    norm_params,
    norm_momentum,
    norm_squares,
):
    nz = lax.axis_size("dp") // 4
    dp, mp = lax.axis_index("dp"), lax.axis_index("mp")
    norm_cols = norm_params.shape[1]
    norm_start = (dp * 2 + mp) * norm_cols
    norm_wide = lax.dynamic_update_slice(
        jnp.zeros((8, D), F32), norm_params.astype(BF16).astype(F32), (0, norm_start)
    )
    proj_w, out_w, up_w, down_w, norm_full = gather_weights(
        nz,
        project_weight.astype(BF16),
        output_weight.astype(BF16),
        up_weight.astype(BF16),
        down_weight.astype(BF16),
        norm_wide,
    )
    rows_here = segment_ids.shape[0] // 2
    seq_len = segment_ids.shape[1]
    tokens_here = rows_here * seq_len
    heads = D // HEAD_DIM
    score_scale = HEAD_DIM ** (-0.5)
    tokens = lax.dynamic_slice_in_dim(tokens_in, mp * tokens_here, tokens_here, 0)
    segments = lax.dynamic_slice_in_dim(segment_ids, mp * rows_here, rows_here, 0)
    projected = dot_f32("tc,scn->stn", tokens, proj_w).astype(BF16)
    heads_split = projected.reshape(3, rows_here, seq_len, heads, HEAD_DIM)

    def masked_scores(query_rows, key_rows, row_segments):
        scores = dot_f32("qhd,khd->hqk", query_rows, key_rows) * score_scale
        same_doc = row_segments[:, None] == row_segments[None, :]
        return jnp.where(same_doc[None], scores, NEG_FILL)

    def row_forward(packed):
        query_rows, key_rows, value_rows, row_segments = packed
        scores = masked_scores(query_rows, key_rows, row_segments)
        row_max = jnp.max(scores, axis=-1, keepdims=True)
        row_exp = jnp.exp(scores - row_max)
        row_total = jnp.sum(row_exp, axis=-1, keepdims=True)
        row_probs = (row_exp / row_total).astype(BF16)
        mixed = dot_f32("hqk,khd->qhd", row_probs, value_rows)
        row_lse = (row_max + jnp.log(row_total))[..., 0]
        return (mixed.astype(BF16).reshape(seq_len, D), row_lse)

    context_rows, lse_rows = lax.map(
        row_forward, (heads_split[0], heads_split[1], heads_split[2], segments)
    )
    context = context_rows.reshape(tokens_here, D)
    attended = dot_f32("tn,dn->td", context, out_w)
    hidden_one, norm_one_back = jax.vjp(
        layer_norm, tokens.astype(F32) + attended, norm_full[0], norm_full[1]
    )
    hidden_low = hidden_one.astype(BF16)
    pre_act = jnp.dot(hidden_low, up_w, preferred_element_type=F32)
    act_full, gelu_back = jax.vjp(exact_gelu, pre_act)
    act_low = act_full.astype(BF16)
    ffn_out = dot_f32("tf,df->td", act_low, down_w)
    result, norm_two_back = jax.vjp(layer_norm, hidden_one + ffn_out, norm_full[2], norm_full[3])
    layer_out = result.astype(BF16)
    d_resid_two, d_gain_two, d_shift_two = norm_two_back(cotangent.astype(F32))
    d_ffn = d_resid_two.astype(BF16)
    down_grad = dot_f32("td,tf->df", d_ffn, act_low).astype(BF16)
    d_act = jnp.dot(d_ffn, down_w, preferred_element_type=F32)
    d_pre = gelu_back(d_act)[0].astype(BF16)
    up_grad = dot_f32("tc,tf->cf", hidden_low, d_pre).astype(BF16)
    d_hidden = d_resid_two + dot_f32("tf,cf->tc", d_pre, up_w)
    d_resid_one, d_gain_one, d_shift_one = norm_one_back(d_hidden)
    d_attn = d_resid_one.astype(BF16)
    output_grad = dot_f32("td,tn->dn", d_attn, context).astype(BF16)
    d_context = jnp.dot(d_attn, out_w, preferred_element_type=F32).astype(BF16)

    def row_backward(packed):
        query_rows, key_rows, value_rows, row_segments, row_lse, row_grad = packed
        scores = masked_scores(query_rows, key_rows, row_segments)
        row_probs = jnp.exp(scores - row_lse[..., None])
        grad_heads = row_grad.reshape(seq_len, heads, HEAD_DIM)
        d_probs = dot_f32("qhd,khd->hqk", grad_heads, value_rows)
        row_inner = jnp.sum(d_probs * row_probs, axis=-1, keepdims=True)
        d_scores = (row_probs * (d_probs - row_inner)).astype(BF16)
        d_value = dot_f32("hqk,qhd->khd", row_probs.astype(BF16), grad_heads)
        d_query = dot_f32("hqk,khd->qhd", d_scores, key_rows) * score_scale
        d_key = dot_f32("hqk,qhd->khd", d_scores, query_rows) * score_scale
        return tuple(g.astype(BF16).reshape(seq_len, D) for g in (d_query, d_key, d_value))

    d_rows = lax.map(
        row_backward,
        (
            heads_split[0],
            heads_split[1],
            heads_split[2],
            segments,
            lse_rows,
            d_context.reshape(rows_here, seq_len, D),
        ),
    )
    d_proj = jnp.stack(d_rows).reshape(3, tokens_here, D)
    project_grad = dot_f32("tc,stn->scn", tokens, d_proj).astype(BF16)
    input_grad = d_resid_one + dot_f32("stn,scn->tc", d_proj, proj_w)
    norm_local = jnp.stack([d_gain_one, d_shift_one, d_gain_two, d_shift_two])
    norm_local = jnp.concatenate([norm_local, jnp.zeros_like(norm_local)])
    down_red, up_red, out_red, proj_red, norm_sum = scatter_grads(
        nz, down_grad, up_grad, output_grad, project_grad, norm_local
    )
    norm_red = lax.dynamic_slice(norm_sum, (0, norm_start), (4, norm_cols))
    return (
        layer_out,
        input_grad,
        *adam_step(proj_red, project_weight, project_momentum, project_squares, D ** (-0.5)),
        *adam_step(out_red, output_weight, output_momentum, output_squares, 4.0 * D ** (-0.5)),
        *adam_step(up_red, up_weight, up_momentum, up_squares, D ** (-0.5)),
        *adam_step(down_red, down_weight, down_momentum, down_squares, FF ** (-0.5)),
        *adam_step(norm_red, norm_params, norm_momentum, norm_squares, 0.3),
    )


def by_rows(mesh):
    dp, mp = mesh.shape["dp"], mesh.shape["mp"]
    return mp == 2 and dp >= 8 and dp & (dp - 1) == 0 and D % (64 * dp) == 0


def solution(mesh):
    body = local_rows if by_rows(mesh) else local_plain
    return jax.shard_map(
        body,
        mesh=mesh,
        in_specs=(
            P("dp", None),
            P(("dp", "mp"), None),
            P("dp", None),
            P(None, "dp", "mp"),
            P(None, "dp", "mp"),
            P(None, "dp", "mp"),
            P("dp", "mp"),
            P("dp", "mp"),
            P("dp", "mp"),
            P("dp", "mp"),
            P("dp", "mp"),
            P("dp", "mp"),
            P("dp", "mp"),
            P("dp", "mp"),
            P("dp", "mp"),
            P(None, ("dp", "mp")),
            P(None, ("dp", "mp")),
            P(None, ("dp", "mp")),
        ),
        out_specs=(
            P(("dp", "mp"), None),
            P(("dp", "mp"), None),
            P(None, "dp", "mp"),
            P(None, "dp", "mp"),
            P(None, "dp", "mp"),
            P(None, "dp", "mp"),
            P("dp", "mp"),
            P("dp", "mp"),
            P("dp", "mp"),
            P("dp", "mp"),
            P("dp", "mp"),
            P("dp", "mp"),
            P("dp", "mp"),
            P("dp", "mp"),
            P("dp", "mp"),
            P("dp", "mp"),
            P("dp", "mp"),
            P("dp", "mp"),
            P(None, ("dp", "mp")),
            P(None, ("dp", "mp")),
            P(None, ("dp", "mp")),
            P(None, ("dp", "mp")),
        ),
        check_vma=False,
    )
```

```python
import functools

import jax
import jax.numpy as jnp
from jax import lax
from jax.experimental import pallas as pl
from jax.experimental.pallas import tpu as pltpu
from jax.sharding import PartitionSpec as P

D = 1024
HEAD_DIM = 64
FF = 4096
STEP = 3


EPS_NORM = 1e-12
NEG_FILL = -1e30
BETA_ONE = 0.5
BETA_TWO = 0.5
ADAM_EPS = 1e-08
DECAY_RATE = 0.01


def layer_norm(values, norm_gain, norm_shift):
    center = values - jnp.mean(values, axis=-1, keepdims=True)
    spread = jnp.mean(center * center, axis=-1, keepdims=True)
    return center * lax.rsqrt(spread + EPS_NORM) * norm_gain + norm_shift


def exact_gelu(values):
    return jax.nn.gelu(values, approximate=False)


def adam_step(gradient, weight, first_old, second, step_rate):
    correct_one = 1.0 - BETA_ONE**STEP
    correct_two = 1.0 - BETA_TWO**STEP
    moment = BETA_ONE * first_old + (1.0 - BETA_ONE) * gradient
    square = BETA_TWO * second + (1.0 - BETA_TWO) * gradient * gradient
    normed = moment / correct_one / (jnp.sqrt(square / correct_two) + ADAM_EPS)
    updated = weight - step_rate * (normed + DECAY_RATE * weight)
    return (gradient, moment, square, updated)


def local_plain(
    tokens_in,
    cotangent,
    segment_ids,
    project_weight,
    project_momentum,
    project_squares,
    output_weight,
    output_momentum,
    output_squares,
    up_weight,
    up_momentum,
    up_squares,
    down_weight,
    down_momentum,
    down_squares,
    norm_params,
    norm_momentum,
    norm_squares,
):
    gathered = (
        lax.all_gather(project_weight.astype(jnp.bfloat16), "dp", axis=1, tiled=True),
        lax.all_gather(output_weight.astype(jnp.bfloat16), "dp", axis=0, tiled=True),
        lax.all_gather(up_weight.astype(jnp.bfloat16), "dp", axis=0, tiled=True),
        lax.all_gather(down_weight.astype(jnp.bfloat16), "dp", axis=0, tiled=True),
    )
    proj_copy, out_copy, up_copy, down_copy = gathered
    norm_full = lax.all_gather(
        norm_params.astype(jnp.bfloat16), ("dp", "mp"), axis=1, tiled=True
    ).astype(jnp.float32)
    rows_here = segment_ids.shape[0]
    seq_len = segment_ids.shape[1]
    local_width = proj_copy.shape[2]
    heads_here = local_width // HEAD_DIM
    score_scale = HEAD_DIM ** (-0.5)
    projected = jnp.einsum(
        "tc,scn->stn", tokens_in, proj_copy, preferred_element_type=jnp.float32
    ).astype(jnp.bfloat16)
    heads_split = projected.reshape(3, rows_here, seq_len, heads_here, HEAD_DIM)

    def masked_scores(query_rows, key_rows, row_segments):
        scores = (
            jnp.einsum("qhd,khd->hqk", query_rows, key_rows, preferred_element_type=jnp.float32)
            * score_scale
        )
        same_doc = row_segments[:, None] == row_segments[None, :]
        return jnp.where(same_doc[None], scores, NEG_FILL)

    def row_forward(packed):
        query_rows, key_rows, value_rows, row_segments = packed
        scores = masked_scores(query_rows, key_rows, row_segments)
        row_max = jnp.max(scores, axis=-1, keepdims=True)
        row_exp = jnp.exp(scores - row_max)
        row_total = jnp.sum(row_exp, axis=-1, keepdims=True)
        row_probs = (row_exp / row_total).astype(jnp.bfloat16)
        mixed = jnp.einsum(
            "hqk,khd->qhd", row_probs, value_rows, preferred_element_type=jnp.float32
        )
        row_lse = (row_max + jnp.log(row_total))[..., 0]
        return (mixed.astype(jnp.bfloat16).reshape(seq_len, local_width), row_lse)

    context_rows, lse_rows = lax.map(
        row_forward, (heads_split[0], heads_split[1], heads_split[2], segment_ids)
    )
    context = context_rows.reshape(rows_here * seq_len, local_width)
    attn_part = jnp.einsum("tn,dn->td", context, out_copy, preferred_element_type=jnp.float32)
    attn_share = lax.psum_scatter(
        attn_part.astype(jnp.bfloat16), "mp", scatter_dimension=0, tiled=True
    ).astype(jnp.float32)
    share_rows = attn_share.shape[0]
    share_start = lax.axis_index("mp") * share_rows
    token_share = lax.dynamic_slice_in_dim(tokens_in, share_start, share_rows, 0).astype(
        jnp.float32
    )
    hidden_one, norm_one_back = jax.vjp(
        layer_norm, token_share + attn_share, norm_full[0], norm_full[1]
    )
    hidden_low = lax.all_gather(hidden_one.astype(jnp.bfloat16), "mp", axis=0, tiled=True)
    pre_act = jnp.dot(hidden_low, up_copy, preferred_element_type=jnp.float32)
    act_full, gelu_back = jax.vjp(exact_gelu, pre_act)
    act_low = act_full.astype(jnp.bfloat16)
    ffn_part = jnp.einsum("tf,df->td", act_low, down_copy, preferred_element_type=jnp.float32)
    ffn_share = lax.psum_scatter(
        ffn_part.astype(jnp.bfloat16), "mp", scatter_dimension=0, tiled=True
    ).astype(jnp.float32)
    result, norm_two_back = jax.vjp(layer_norm, hidden_one + ffn_share, norm_full[2], norm_full[3])
    layer_out = result.astype(jnp.bfloat16)
    regathered = (
        lax.all_gather(project_weight.astype(jnp.bfloat16), "dp", axis=1, tiled=True),
        lax.all_gather(output_weight.astype(jnp.bfloat16), "dp", axis=0, tiled=True),
        lax.all_gather(up_weight.astype(jnp.bfloat16), "dp", axis=0, tiled=True),
        lax.all_gather(down_weight.astype(jnp.bfloat16), "dp", axis=0, tiled=True),
    )
    proj_copy, out_copy, up_copy, down_copy = regathered
    d_resid_two, d_gain_two, d_shift_two = norm_two_back(cotangent.astype(jnp.float32))
    d_ffn = lax.all_gather(d_resid_two.astype(jnp.bfloat16), "mp", axis=0, tiled=True)
    down_grad = jnp.einsum("td,tf->df", d_ffn, act_low, preferred_element_type=jnp.float32)
    d_act = jnp.dot(d_ffn, down_copy, preferred_element_type=jnp.float32)
    d_pre = gelu_back(d_act)[0].astype(jnp.bfloat16)
    up_grad = jnp.einsum("tc,tf->cf", hidden_low, d_pre, preferred_element_type=jnp.float32)
    d_hidden_part = jnp.einsum("tf,cf->tc", d_pre, up_copy, preferred_element_type=jnp.float32)
    d_hidden = d_resid_two + lax.psum_scatter(
        d_hidden_part.astype(jnp.bfloat16), "mp", scatter_dimension=0, tiled=True
    ).astype(jnp.float32)
    d_resid_one, d_gain_one, d_shift_one = norm_one_back(d_hidden)
    d_attn = lax.all_gather(d_resid_one.astype(jnp.bfloat16), "mp", axis=0, tiled=True)
    output_grad = jnp.einsum("td,tn->dn", d_attn, context, preferred_element_type=jnp.float32)
    d_context = jnp.dot(d_attn, out_copy, preferred_element_type=jnp.float32).astype(jnp.bfloat16)

    def row_backward(packed):
        query_rows, key_rows, value_rows, row_segments, row_lse, row_grad = packed
        scores = masked_scores(query_rows, key_rows, row_segments)
        row_probs = jnp.exp(scores - row_lse[..., None])
        grad_heads = row_grad.reshape(seq_len, heads_here, HEAD_DIM)
        d_probs = jnp.einsum(
            "qhd,khd->hqk", grad_heads, value_rows, preferred_element_type=jnp.float32
        )
        row_inner = jnp.sum(d_probs * row_probs, axis=-1, keepdims=True)
        d_scores = (row_probs * (d_probs - row_inner)).astype(jnp.bfloat16)
        d_value = jnp.einsum(
            "hqk,qhd->khd",
            row_probs.astype(jnp.bfloat16),
            grad_heads,
            preferred_element_type=jnp.float32,
        )
        d_query = (
            jnp.einsum("hqk,khd->qhd", d_scores, key_rows, preferred_element_type=jnp.float32)
            * score_scale
        )
        d_key = (
            jnp.einsum("hqk,qhd->khd", d_scores, query_rows, preferred_element_type=jnp.float32)
            * score_scale
        )
        return (
            d_query.astype(jnp.bfloat16).reshape(seq_len, local_width),
            d_key.astype(jnp.bfloat16).reshape(seq_len, local_width),
            d_value.astype(jnp.bfloat16).reshape(seq_len, local_width),
        )

    grad_context_rows = d_context.reshape(rows_here, seq_len, local_width)
    d_rows = lax.map(
        row_backward,
        (heads_split[0], heads_split[1], heads_split[2], segment_ids, lse_rows, grad_context_rows),
    )
    d_proj = jnp.stack(d_rows).reshape(3, rows_here * seq_len, local_width)
    project_grad = jnp.einsum("tc,stn->scn", tokens_in, d_proj, preferred_element_type=jnp.float32)
    d_input_part = jnp.einsum("stn,scn->tc", d_proj, proj_copy, preferred_element_type=jnp.float32)
    input_grad = d_resid_one + lax.psum_scatter(
        d_input_part.astype(jnp.bfloat16), "mp", scatter_dimension=0, tiled=True
    ).astype(jnp.float32)
    norm_local = jnp.stack([d_gain_one, d_shift_one, d_gain_two, d_shift_two])
    norm_red = lax.psum_scatter(norm_local, ("dp", "mp"), scatter_dimension=1, tiled=True)
    proj_red, out_red, up_red, down_red = (
        lax.psum_scatter(
            project_grad.astype(jnp.bfloat16), "dp", scatter_dimension=1, tiled=True
        ).astype(jnp.float32),
        lax.psum_scatter(
            output_grad.astype(jnp.bfloat16), "dp", scatter_dimension=0, tiled=True
        ).astype(jnp.float32),
        lax.psum_scatter(
            up_grad.astype(jnp.bfloat16), "dp", scatter_dimension=0, tiled=True
        ).astype(jnp.float32),
        lax.psum_scatter(
            down_grad.astype(jnp.bfloat16), "dp", scatter_dimension=0, tiled=True
        ).astype(jnp.float32),
    )
    proj_new = adam_step(proj_red, project_weight, project_momentum, project_squares, D ** (-0.5))
    out_new = adam_step(out_red, output_weight, output_momentum, output_squares, 4.0 * D ** (-0.5))
    up_new = adam_step(up_red, up_weight, up_momentum, up_squares, D ** (-0.5))
    down_new = adam_step(down_red, down_weight, down_momentum, down_squares, FF ** (-0.5))
    norm_new = adam_step(norm_red, norm_params, norm_momentum, norm_squares, 0.3)
    return (
        layer_out,
        input_grad,
        proj_new[0],
        proj_new[1],
        proj_new[2],
        proj_new[3],
        out_new[0],
        out_new[1],
        out_new[2],
        out_new[3],
        up_new[0],
        up_new[1],
        up_new[2],
        up_new[3],
        down_new[0],
        down_new[1],
        down_new[2],
        down_new[3],
        norm_new[0],
        norm_new[1],
        norm_new[2],
        norm_new[3],
    )


MESH = pl.DeviceIdType.MESH
BF16 = jnp.bfloat16
F32 = jnp.float32
ANY = pl.BlockSpec(memory_space=pl.ANY)
VMEM = pl.BlockSpec(memory_space=pltpu.VMEM)
DMA = pltpu.SemaphoreType.DMA

HOP_X, HOP_Y, HOP_C, OWN = (0, 1, 0, 0), (0, 0, 0, 1), (0, 0, 1, 0), (0, 0, 0, 0)


def hop_z(mask):
    return (mask, 0, 0, 0)


def position():
    dp = lax.axis_index("dp")
    return (dp // 4, (dp // 2) % 2, dp % 2, lax.axis_index("mp"))


def moved(me, hop):
    return tuple(m ^ h if h else m for m, h in zip(me, hop))


def device_at(me, hop):
    z, x, c, y = moved(me, hop)
    return (z * 4 + x * 2 + c, y)


def entry_barrier(me, nz):
    barrier = pltpu.get_barrier_semaphore()
    hops = [HOP_X, HOP_Y, HOP_C] + [hop_z(a) for a in range(1, nz)]
    for hop in hops:
        pl.semaphore_signal(barrier, inc=1, device_id=device_at(me, hop), device_id_type=MESH)
    pl.semaphore_wait(barrier, len(hops))


def view_rows(ref, pos):
    z, x, c, y = pos
    half = ref.shape[4] // 2
    return ref.at[z, x, c, :, pl.ds(pl.multiple_of(y * half, half), half)]


def view_stack(ref, pos):
    z, x, c, y = pos
    half = ref.shape[5] // 2
    return ref.at[:, z, x, c, :, pl.ds(pl.multiple_of(y * half, half), half)]


class Gather:
    def __init__(self, me, nz, own, out, view, send_sem, recv_sem, base):
        self.me, self.nz, self.own, self.out, self.view = me, nz, own, out, view
        self.send_sem, self.recv_sem, self.base = send_sem, recv_sem, base
        self.sent = []

    def slot(self, rel):
        a, b, d, e = rel
        return self.base + ((a * 2 + b) * 2 + d) * 2 + e

    def piece(self, rel):
        return self.view(self.out, moved(self.me, rel))

    def copy(self, rel, hop):
        arrives = tuple(r ^ h for r, h in zip(rel, hop))
        return pltpu.make_async_remote_copy(
            src_ref=self.own if rel == OWN else self.piece(rel),
            dst_ref=self.piece(rel),
            send_sem=self.send_sem.at[self.slot(arrives)],
            recv_sem=self.recv_sem.at[self.slot(arrives)],
            device_id=device_at(self.me, hop),
            device_id_type=MESH,
        )

    def send(self, rel, hop):
        self.copy(rel, hop).start()
        self.sent.append((rel, hop))

    def wait(self, rel):
        pltpu.make_async_remote_copy(
            src_ref=self.own,
            dst_ref=self.piece(rel),
            send_sem=self.send_sem.at[self.slot(rel)],
            recv_sem=self.recv_sem.at[self.slot(rel)],
            device_id=device_at(self.me, HOP_C),
            device_id_type=MESH,
        ).wait_recv()

    def run(self, steps):
        for kind, rel, hop in steps:
            if kind == "send":
                self.send(rel, hop)
            else:
                self.wait(rel)

    def steps_first(self):
        out = [("send", OWN, HOP_X), ("send", OWN, HOP_Y)]
        out += [("send", OWN, hop_z(a)) for a in range(1, self.nz)]
        return out + [("send", OWN, HOP_C)]

    def steps_square(self, a):
        out = [("wait", (a, 1, 0, 0), None), ("wait", (a, 0, 0, 1), None)]
        if a < self.nz // 2:
            out.append(("send", (a, 1, 0, 0), HOP_Y))
        else:
            out.append(("send", (a, 0, 0, 1), HOP_X))
        return out + [("send", (a, 1, 0, 0), HOP_C), ("send", (a, 0, 0, 1), HOP_C)]

    def steps_level(self, a):
        piece = hop_z(a)
        return [("wait", piece, None)] + [("send", piece, hop) for hop in (HOP_X, HOP_Y, HOP_C)]

    def steps_middle(self):
        out = []
        for a in range(1, self.nz):
            out += self.steps_level(a) + self.steps_square(a - 1)
        return out + self.steps_square(self.nz - 1)

    def steps_diagonal(self):
        out = []
        for a in range(self.nz):
            out += [("wait", (a, 1, 0, 1), None), ("send", (a, 1, 0, 1), HOP_C)]
        return out

    def steps_last(self):
        return [("wait", (a, b, 1, e), None) for a in range(self.nz) for b in range(2) for e in range(2)]

    def drain(self):
        for rel, hop in self.sent:
            self.copy(rel, hop).wait_send()


def sum_hops(nz):
    hops, mask = [HOP_C, HOP_X, HOP_Y], 1
    while mask < nz:
        hops.append(hop_z(mask))
        mask *= 2
    return hops


class SmallSum:
    def __init__(self, me, nz, parts, came, send_sem, recv_sem):
        self.me, self.hops, self.parts, self.came = me, sum_hops(nz), parts, came
        self.send_sem, self.recv_sem = send_sem, recv_sem

    def copy(self, i):
        return pltpu.make_async_remote_copy(
            src_ref=self.parts.at[i],
            dst_ref=self.came.at[i],
            send_sem=self.send_sem.at[i],
            recv_sem=self.recv_sem.at[i],
            device_id=device_at(self.me, self.hops[i]),
            device_id_type=MESH,
        )

    def start(self, i):
        self.copy(i).start()

    def finish(self, i):
        self.copy(i).wait()
        self.parts[i + 1] = self.parts[i] + self.came[i]


def add_blocks(dst, terms, rows=16):
    lead = range(dst.shape[0]) if len(dst.shape) == 3 else (None,)

    def body(i, carry):
        start = pl.multiple_of(i * rows, rows)
        for s in lead:
            idx = (pl.ds(start, rows), slice(None)) if s is None else (s, pl.ds(start, rows), slice(None))
            total = terms[0][idx].astype(F32)
            for term in terms[1:]:
                total = total + term[idx].astype(F32)
            dst[idx] = total.astype(dst.dtype)
        return carry

    lax.fori_loop(0, dst.shape[-2] // rows, body, 0)


class Scatter:
    def __init__(self, me, nz, grad, result, view, held, from_c, from_d, from_x, from_y, from_z,
                 load_sem, send_sem, recv_sem, base):
        self.me, self.nz, self.grad, self.result, self.view = me, nz, grad, result, view
        self.held, self.from_c, self.from_d = held, from_c, from_d
        self.from_x, self.from_y, self.from_z = from_x, from_y, from_z
        self.load_sem, self.send_sem, self.recv_sem, self.base = load_sem, send_sem, recv_sem, base
        self.sent = []

    def index(self, a, b, e):
        return (a * 2 + b) * 2 + e

    def remote(self, src, dst, slot, hop):
        sem = self.base * 8 * self.nz + slot
        return pltpu.make_async_remote_copy(
            src_ref=src, dst_ref=dst, send_sem=self.send_sem.at[sem], recv_sem=self.recv_sem.at[sem],
            device_id=device_at(self.me, hop), device_id_type=MESH,
        )

    def send(self, src, dst, slot, hop):
        copy = self.remote(src, dst, slot, hop)
        copy.start()
        self.sent.append(copy)

    def wait(self, dst, slot):
        self.remote(dst, dst, slot, HOP_C).wait_recv()

    def load(self, a, b, e):
        i = self.index(a, b, e)
        return pltpu.make_async_copy(
            self.view(self.grad, moved(self.me, (a, b, 0, e))), self.held.at[i],
            self.load_sem.at[self.base * 4 * self.nz + i],
        )

    def stage_core(self, a):
        for b, e in ((1, 1), (1, 0), (0, 1), (0, 0)):
            i = self.index(a, b, e)
            self.send(self.view(self.grad, moved(self.me, (a, b, 1, e))), self.from_c.at[i], i, HOP_C)
            self.load(a, b, e).start()

    def slot_of(self, kind, a):
        return 4 * self.nz + self.nz * "dxyz".index(kind) + a

    def stage_diagonal(self, a):
        for b, e in ((1, 1), (1, 0), (0, 1), (0, 0)):
            i = self.index(a, b, e)
            self.load(a, b, e).wait()
            self.wait(self.from_c.at[i], i)
            add_blocks(self.held.at[i], [self.held.at[i], self.from_c.at[i]])
            if (b, e) == (1, 1):
                hop = HOP_Y if a < self.nz // 2 else HOP_X
                self.send(self.held.at[i], self.from_d.at[a], self.slot_of("d", a), hop)
            elif (b, e) == (1, 0) and a >= self.nz // 2:
                self.send(self.held.at[i], self.from_x.at[a], self.slot_of("x", a), HOP_X)
            elif (b, e) == (0, 1) and a < self.nz // 2:
                self.send(self.held.at[i], self.from_y.at[a], self.slot_of("y", a), HOP_Y)

    def stage_square(self, a):
        self.wait(self.from_d.at[a], self.slot_of("d", a))
        if a < self.nz // 2:
            i = self.index(a, 1, 0)
            add_blocks(self.held.at[i], [self.held.at[i], self.from_d.at[a]])
            self.send(self.held.at[i], self.from_x.at[a], self.slot_of("x", a), HOP_X)
        else:
            i = self.index(a, 0, 1)
            add_blocks(self.held.at[i], [self.held.at[i], self.from_d.at[a]])
            self.send(self.held.at[i], self.from_y.at[a], self.slot_of("y", a), HOP_Y)

    def stage_column(self, a):
        self.wait(self.from_x.at[a], self.slot_of("x", a))
        self.wait(self.from_y.at[a], self.slot_of("y", a))
        i = self.index(a, 0, 0)
        terms = [self.held.at[i], self.from_x.at[a], self.from_y.at[a]]
        if a:
            add_blocks(self.held.at[i], terms)
            self.send(self.held.at[i], self.from_z.at[a], self.slot_of("z", a), hop_z(a))
        else:
            for other in range(1, self.nz):
                self.wait(self.from_z.at[other], self.slot_of("z", other))
                terms.append(self.from_z.at[other])
            add_blocks(self.result, terms)

    def order(self):
        half = self.nz // 2
        out = []
        for k in range(half):
            out += [self.nz - 1 - k, half - 1 - k]
        return out

    def stages(self):
        order = self.order()
        calls = [(self.stage_core, a) for a in order]
        kinds = (self.stage_diagonal, self.stage_square, self.stage_column)
        for t in range(len(order) + 2):
            for lag, kind in enumerate(kinds):
                if 0 <= t - lag < len(order):
                    calls.append((kind, order[t - lag]))
        return calls

    def drain(self):
        for copy in self.sent:
            copy.wait_send()


def scatter_kernel(nz, *refs):
    grads, norm = refs[:4], refs[4]
    results, norm_all = refs[5:9], refs[9]
    buffers, rest = refs[10:34], refs[34:]
    load_sem, send_sem, recv_sem, parts, came, sum_send, sum_recv = rest
    me = position()
    entry_barrier(me, nz)
    views = (view_rows, view_rows, view_rows, view_stack)
    scatters = [
        Scatter(me, nz, grads[i], results[i], views[i], *buffers[6 * i : 6 * i + 6],
                load_sem, send_sem, recv_sem, i)
        for i in range(4)
    ]
    small = SmallSum(me, nz, parts, came, sum_send, sum_recv)
    parts[0] = norm[...]
    for i in range(len(small.hops)):
        small.start(i)
        small.finish(i)
    norm_all[...] = parts[len(small.hops)]
    for s in scatters:
        for call, a in s.stages():
            call(a)
    for s in scatters:
        s.drain()


def scatter_grads(nz, down, up, out, proj, norm):
    grads = [g.reshape(nz, 2, 2, D // (4 * nz), g.shape[1]) for g in (down, up, out)]
    grads.append(proj.reshape(3, nz, 2, 2, D // (4 * nz), proj.shape[2]))
    shapes, buffers = [], []
    for g in grads:
        piece = (g.shape[-2], g.shape[-1] // 2)
        if g.ndim == 6:
            piece = (3,) + piece
        shapes.append(jax.ShapeDtypeStruct(piece, F32))
        for count in (4 * nz, 4 * nz, nz, nz, nz, nz):
            buffers.append(pltpu.VMEM((count,) + piece, BF16))
    n_sum = len(sum_hops(nz))
    return pl.pallas_call(
        functools.partial(scatter_kernel, nz),
        out_shape=shapes + [jax.ShapeDtypeStruct(norm.shape, F32)],
        in_specs=[ANY] * 4 + [VMEM],
        out_specs=[VMEM] * 5,
        scratch_shapes=buffers
        + [
            DMA((16 * nz,)),
            DMA((32 * nz,)),
            DMA((32 * nz,)),
            pltpu.VMEM((n_sum + 1,) + norm.shape, F32),
            pltpu.VMEM((n_sum,) + norm.shape, F32),
            DMA((n_sum,)),
            DMA((n_sum,)),
        ],
        compiler_params=pltpu.CompilerParams(
            collective_id=1, has_side_effects=True, vmem_limit_bytes=56 << 20
        ),
        name="scatter_grads",
    )(*grads, norm)


ERFC_SLOPE = 0.33 * 0.5**0.5
ERFC_POLY = (
    0.1863683316091749,
    0.1828075671230129,
    0.2020873146971517,
    0.044528074107268695,
    0.41336767744180025,
    -0.35626105794547547,
    0.4631297570306923,
    -0.13602774732192066,
)
PDF_SCALE = 0.3989422804014327


def gelu_pair(u):
    size = jnp.abs(u)
    t = 1.0 / (1.0 + ERFC_SLOPE * size)
    poly = 0.5 * ERFC_POLY[-1]
    for coefficient in ERFC_POLY[-2::-1]:
        poly = poly * t + 0.5 * coefficient
    bell = jnp.exp(u * u * -0.5)
    tail = poly * t * bell
    phi = jnp.where(u >= 0.0, 1.0 - tail, tail)
    return u * phi, phi + u * bell * PDF_SCALE


def dot_nn(a, b):
    return jnp.dot(a, b, preferred_element_type=F32)


def dot_nt(a, b):
    return lax.dot_general(a, b, (((1,), (1,)), ((), ())), preferred_element_type=F32)


def normed(rows):
    center = rows - jnp.mean(rows, axis=-1, keepdims=True)
    scale = lax.rsqrt(jnp.mean(center * center, axis=-1, keepdims=True) + EPS_NORM)
    return center * scale, scale


def norm_backward(grad, n, scale):
    inner = jnp.mean(grad * n, axis=-1, keepdims=True)
    return scale * (grad - jnp.mean(grad, axis=-1, keepdims=True) - n * inner)


def at_slots(i, plan):
    for k in sorted(plan):
        @pl.when(i == k)
        def _(k=k):
            for call in plan[k]:
                call()


def phase(count, body, plan):
    def step(i, carry):
        at_slots(i, plan)
        body(i)
        return carry

    lax.fori_loop(0, count, step, 0)


def spread(calls, spans):
    plans, calls = [{} for _ in spans], list(calls)
    for plan, (count, start, each) in zip(plans, spans):
        for i in range(count):
            while calls and calls[0][0] <= start + i * each:
                plan.setdefault(i, []).append(calls.pop(0)[1])
    return plans, [call for _, call in calls]


def gather_calls(gathers, costs, start):
    calls, marks, clock = [], [], start
    nz = gathers[0].nz

    def add(when, g, steps):
        calls.append((when, functools.partial(g.run, steps)))

    for i, (g, cost) in enumerate(zip(gathers, costs)):
        first = g.steps_first()
        if i == 0:
            add(clock, g, first)
        unit = cost / (3 * nz - 1)
        tick = 0
        for a in range(1, nz):
            tick += 1
            add(clock + tick * unit, g, g.steps_level(a))
            if a == nz - 1 and i + 1 < len(gathers):
                add(clock + tick * unit, gathers[i + 1], gathers[i + 1].steps_first()[2:-1])
            tick += 1
            add(clock + tick * unit, g, g.steps_square(a - 1))
        tick += 1
        add(clock + tick * unit, g, g.steps_square(nz - 1))
        if i + 1 < len(gathers):
            nxt = gathers[i + 1].steps_first()
            add(clock + tick * unit, gathers[i + 1], nxt[:2] + nxt[-1:])
        steps = g.steps_diagonal()
        for a in range(nz):
            tick += 1
            add(clock + tick * unit, g, steps[2 * a : 2 * a + 2])
        add(clock + cost, g, g.steps_last())
        marks.append(len(calls))
        clock += cost
    return calls, marks


def forward_kernel(nz, tokens, cotangent, seg_col, seg_row, proj, out, up, down, norm,
                   proj_all, out_all, up_all, down_all, norm_all, qkv_out, ctx_out, lse,
                   resid_out, hidden_out, act_out, slope_out, layer_out, dres_out, dffn_out, dnorm,
                   tok, cot, w_small, w_up, qkv, ctx, bias, res, hidden, act, pre, slope,
                   send_sem, recv_sem, local_sem, parts, came, sum_send, sum_recv, io_sem):
    me = position()
    t_here, seq = tok.shape[0], seg_row.shape[2]
    rows_here, pairs = t_here // seq, D // 128
    copies = {}

    def begin(key, src, dst, sem):
        copies[key] = pltpu.make_async_copy(src, dst, io_sem.at[sem])
        copies[key].start()

    mine = pl.ds(pl.multiple_of(me[3] * t_here, t_here), t_here)
    begin("tok", tokens.at[mine, :], tok, 0)
    begin("cot", cotangent, cot, 1)
    parts[0] = norm[...]
    entry_barrier(me, nz)
    owns, fulls = (proj, out, up, down), (proj_all, out_all, up_all, down_all)
    views = (view_stack, view_rows, view_rows, view_rows)
    n = 8 * nz
    gathers = [
        Gather(me, nz, owns[i], fulls[i], views[i], send_sem, recv_sem, n * i) for i in range(4)
    ]
    keep = [pltpu.make_async_copy(g.own, g.piece(OWN), local_sem.at[i]) for i, g in enumerate(gathers)]
    costs = FORWARD_COSTS
    calls, marks = gather_calls(gathers, costs, 0.0)
    calls[0][1]()
    for copy in keep:
        copy.start()
    small = SmallSum(me, nz, parts, came, sum_send, sum_recv)
    for i in range(len(small.hops)):
        small.start(i)
        small.finish(i)
    norm_all[...] = parts[len(small.hops)]

    def bias_step(r):
        rows = pl.ds(pl.multiple_of(r * seq, seq), seq)
        same = seg_col[rows, 0:1] == seg_row[r]
        bias[r] = jnp.where(same, 0.0, NEG_FILL)

    phase(rows_here, bias_step, {})
    for _, call in calls[1 : marks[0]]:
        call()
    for copy in keep:
        copy.wait()
    copies["tok"].wait()
    begin("proj", proj_all, w_small.at[pl.ds(0, 3)], 2)

    step_q, step_a, step_o, step_u = FORWARD_STEPS
    n_q, n_a, n_o, n_u = 3 * D // 256, rows_here * pairs, t_here // 256, FF // 256
    start_q = costs[0] + 2.0
    start_a = start_q + n_q * step_q
    plans, _ = spread(
        calls[marks[0] : marks[2]], [(n_q, start_q, step_q), (n_a, start_a, step_a)]
    )
    done = sum(len(c) for plan in plans for c in plan.values())
    rest_out = calls[marks[0] + done : marks[1]]
    later = marks[0] + done + len(rest_out)
    copies["proj"].wait()

    def qkv_step(j):
        s, col = j // (D // 256), pl.ds(pl.multiple_of((j % (D // 256)) * 256, 256), 256)
        weight = w_small[s, :, :, :, :, col].reshape(D, 256)
        qkv[s, :, col] = dot_nn(tok[...], weight).astype(BF16)

    phase(n_q, qkv_step, plans[0])
    begin("qkv", qkv, qkv_out, 3)
    head_of = lax.broadcasted_iota(jnp.int32, (128, 128), 1) // HEAD_DIM

    def attend_step(u):
        r, p = u // pairs, u % pairs
        col = pl.ds(pl.multiple_of(p * 128, 128), 128)
        for qb in range(seq // 128):
            low, high = max(0, qb - 2) * 128, min(seq // 128, qb + 3) * 128
            q_rows = pl.ds(pl.multiple_of(r * seq + qb * 128, 128), 128)
            k_rows = pl.ds(pl.multiple_of(r * seq + low, 128), high - low)
            q = qkv[0, q_rows, col] * jnp.asarray(HEAD_DIM**-0.5, BF16)
            both = jnp.concatenate([jnp.where(head_of == h, q, jnp.zeros_like(q)) for h in range(2)])
            block = bias[r, qb * 128 : qb * 128 + 128, low:high]
            scores = dot_nt(both, qkv[1, k_rows, col]) + jnp.concatenate([block, block])
            top = jnp.max(scores, axis=-1, keepdims=True)
            weights = jnp.exp(scores - top)
            total = jnp.sum(weights, axis=-1, keepdims=True)
            probs = (weights * (1.0 / total)).astype(BF16)
            mixed = dot_nn(probs, qkv[2, k_rows, col])
            ctx[q_rows, col] = jnp.where(head_of == 0, mixed[:128], mixed[128:]).astype(BF16)
            level = top + jnp.log(total)
            for h in range(2):
                wide = jnp.broadcast_to(level[h * 128 : h * 128 + 128], (128, 128))
                lse[u, h : h + 1, qb * 128 : qb * 128 + 128] = wide.T[0:1]

    phase(n_a, attend_step, plans[1])
    for _, call in rest_out:
        call()
    begin("out", out_all, w_small.at[3], 4)
    begin("ctx", ctx, ctx_out, 5)
    start_o = max(start_a + n_a * step_a, costs[0] + costs[1])
    plans, rest_up = spread(calls[later : marks[2]], [(n_o, start_o, step_o)])
    copies["out"].wait()

    def out_step(m):
        rows = pl.ds(pl.multiple_of(m * 256, 256), 256)
        attended = dot_nt(ctx[rows, :], w_small[3].reshape(D, D))
        total = tok[rows, :].astype(F32) + attended
        res[rows, :] = total
        unit, _ = normed(total)
        hidden[rows, :] = (unit * norm_all[0:1, :] + norm_all[1:2, :]).astype(BF16)

    phase(n_o, out_step, plans[0])
    begin("res", res, resid_out, 6)
    begin("hidden", hidden, hidden_out, 7)
    for call in rest_up:
        call()
    begin("up", up_all, w_up, 8)
    start_u = costs[0] + costs[1] + costs[2] + 2.0
    plans, rest_down = spread(calls[marks[2] :], [(n_u, start_u, step_u)])
    copies["up"].wait()

    def up_step(j):
        col = pl.ds(pl.multiple_of(j * 256, 256), 256)
        slot = j % 2
        pre[...] = dot_nn(hidden[...], w_up[:, :, :, :, col].reshape(D, 256))

        @pl.when(j >= 2)
        def _():
            slope_copy(j - 2, slot).wait()

        def chunk(i, carry):
            rows = pl.ds(pl.multiple_of(i * 32, 32), 32)
            value, tangent = gelu_pair(pre[rows, :])
            act[rows, col] = value.astype(BF16)
            slope[slot, rows, :] = tangent.astype(BF16)
            return carry

        lax.fori_loop(0, t_here // 32, chunk, 0)
        slope_copy(j, slot).start()

    def slope_copy(j, slot):
        col = pl.ds(pl.multiple_of(j * 256, 256), 256)
        return pltpu.make_async_copy(slope.at[slot], slope_out.at[:, col], io_sem.at[9 + slot])

    phase(n_u, up_step, plans[0])
    begin("act", act, act_out, 11)
    for call in rest_down:
        call()
    for k in range(4):
        begin(("down", k), down_all.at[:, :, :, :, pl.ds(k * D, D)], w_small.at[k], 12 + k)
    for j in (n_u - 2, n_u - 1):
        slope_copy(j, j % 2).wait()
    for key in ("cot", "res", "hidden") + tuple(("down", k) for k in range(4)):
        copies[key].wait()
    dnorm[...] = jnp.zeros_like(dnorm)

    def down_step(m):
        rows = pl.ds(pl.multiple_of(m * 256, 256), 256)
        unit, _ = normed(res[rows, :])
        total = unit * norm_all[0:1, :] + norm_all[1:2, :]
        for k in range(4):
            total = total + dot_nt(act[rows, k * D : (k + 1) * D], w_small[k].reshape(D, D))
        unit, scale = normed(total)
        tok[rows, :] = (unit * norm_all[2:3, :] + norm_all[3:4, :]).astype(BF16)
        grad = cot[rows, :].astype(F32)
        dnorm[0:1, :] = dnorm[0:1, :] + jnp.sum(grad * unit, axis=0, keepdims=True)
        dnorm[1:2, :] = dnorm[1:2, :] + jnp.sum(grad, axis=0, keepdims=True)
        dres = norm_backward(grad * norm_all[2:3, :], unit, scale)
        res[rows, :] = dres
        hidden[rows, :] = dres.astype(BF16)

    phase(t_here // 256, down_step, {})
    begin("layer", tok, layer_out, 16)
    begin("dres", res, dres_out, 17)
    begin("dffn", hidden, dffn_out, 18)
    for key in ("qkv", "ctx", "act", "layer", "dres", "dffn"):
        copies[key].wait()
    for g in gathers:
        g.drain()


FORWARD_COSTS = (31.0, 10.0, 42.0, 42.0)
FORWARD_STEPS = (0.8, 1.4, 1.2, 1.7)


def run_forward(nz, tokens_in, cotangent, segments, proj, out, up, down, norm):
    t_here = cotangent.shape[0]
    rows_here, seq = segments.shape
    n_sum = len(sum_hops(nz))
    rows = D // (4 * nz)
    full = lambda cols: jax.ShapeDtypeStruct((nz, 2, 2, rows, cols), BF16)
    flat = lambda cols, kind: jax.ShapeDtypeStruct((t_here, cols), kind)
    seg_col = jnp.broadcast_to(segments.reshape(t_here, 1), (t_here, 128))
    seg_row = segments.reshape(rows_here, 1, seq)
    return pl.pallas_call(
        functools.partial(forward_kernel, nz),
        out_shape=[
            jax.ShapeDtypeStruct((3, nz, 2, 2, rows, D), BF16),
            full(D),
            full(FF),
            full(FF),
            jax.ShapeDtypeStruct(norm.shape, F32),
            jax.ShapeDtypeStruct((3, t_here, D), BF16),
            flat(D, BF16),
            jax.ShapeDtypeStruct((rows_here * (D // 128), 8, seq), F32),
            flat(D, F32),
            flat(D, BF16),
            flat(FF, BF16),
            flat(FF, BF16),
            flat(D, BF16),
            flat(D, F32),
            flat(D, BF16),
            jax.ShapeDtypeStruct((8, D), F32),
        ],
        in_specs=[ANY, ANY, VMEM, VMEM, ANY, ANY, ANY, ANY, VMEM],
        out_specs=[ANY] * 4 + [VMEM, ANY, ANY, VMEM] + [ANY] * 7 + [VMEM],
        scratch_shapes=[
            pltpu.VMEM((t_here, D), BF16),
            pltpu.VMEM((t_here, D), BF16),
            pltpu.VMEM((4, nz, 2, 2, rows, D), BF16),
            pltpu.VMEM((nz, 2, 2, rows, FF), BF16),
            pltpu.VMEM((3, t_here, D), BF16),
            pltpu.VMEM((t_here, D), BF16),
            pltpu.VMEM((rows_here, seq, seq), F32),
            pltpu.VMEM((t_here, D), F32),
            pltpu.VMEM((t_here, D), BF16),
            pltpu.VMEM((t_here, FF), BF16),
            pltpu.VMEM((t_here, 256), F32),
            pltpu.VMEM((2, t_here, 256), BF16),
            DMA((32 * nz,)),
            DMA((32 * nz,)),
            DMA((4,)),
            pltpu.VMEM((n_sum + 1,) + norm.shape, F32),
            pltpu.VMEM((n_sum,) + norm.shape, F32),
            DMA((n_sum,)),
            DMA((n_sum,)),
            DMA((19,)),
        ],
        compiler_params=pltpu.CompilerParams(
            collective_id=0, has_side_effects=True, vmem_limit_bytes=60 << 20
        ),
        name="forward",
    )(tokens_in, cotangent, seg_col, seg_row, proj, out, up, down, norm)


def dot_f32(spec, a, b):
    return jnp.einsum(spec, a, b, preferred_element_type=F32)


def local_rows(
    tokens_in,
    cotangent,
    segment_ids,
    project_weight,
    project_momentum,
    project_squares,
    output_weight,
    output_momentum,
    output_squares,
    up_weight,
    up_momentum,
    up_squares,
    down_weight,
    down_momentum,
    down_squares,
    norm_params,
    norm_momentum,
    norm_squares,
):
    nz = lax.axis_size("dp") // 4
    dp, mp = lax.axis_index("dp"), lax.axis_index("mp")
    norm_cols = norm_params.shape[1]
    norm_start = (dp * 2 + mp) * norm_cols
    norm_wide = lax.dynamic_update_slice(
        jnp.zeros((8, D), F32), norm_params.astype(BF16).astype(F32), (0, norm_start)
    )
    rows_here = segment_ids.shape[0] // 2
    seq_len = segment_ids.shape[1]
    tokens_here = rows_here * seq_len
    heads = D // HEAD_DIM
    score_scale = HEAD_DIM ** (-0.5)
    segments = lax.dynamic_slice_in_dim(segment_ids, mp * rows_here, rows_here, 0)
    (proj_w, out_w, up_w, down_w, norm_full, qkv, context, lse, resid_one, hidden_low, act_low, slope,
     layer_out, d_resid_two, d_ffn, d_norm_two) = run_forward(
        nz,
        tokens_in,
        cotangent,
        segments,
        project_weight.astype(BF16),
        output_weight.astype(BF16),
        up_weight.astype(BF16),
        down_weight.astype(BF16),
        norm_wide,
    )
    proj_w, out_w = proj_w.reshape(3, D, D), out_w.reshape(D, D)
    up_w, down_w = up_w.reshape(D, FF), down_w.reshape(D, FF)
    tokens = lax.dynamic_slice_in_dim(tokens_in, mp * tokens_here, tokens_here, 0)
    heads_split = qkv.reshape(3, rows_here, seq_len, heads, HEAD_DIM)
    lse_rows = lse[:, :2].reshape(rows_here, heads, seq_len)

    def masked_scores(query_rows, key_rows, row_segments):
        scores = dot_f32("qhd,khd->hqk", query_rows, key_rows) * score_scale
        same_doc = row_segments[:, None] == row_segments[None, :]
        return jnp.where(same_doc[None], scores, NEG_FILL)

    d_gain_two, d_shift_two = d_norm_two[0], d_norm_two[1]
    down_grad = dot_f32("td,tf->df", d_ffn, act_low).astype(BF16)
    d_act = jnp.dot(d_ffn, down_w, preferred_element_type=F32)
    d_pre = (d_act * slope.astype(F32)).astype(BF16)
    up_grad = dot_f32("tc,tf->cf", hidden_low, d_pre).astype(BF16)
    d_hidden = d_resid_two + dot_f32("tf,cf->tc", d_pre, up_w)
    unit, unit_scale = normed(resid_one)
    d_gain_one, d_shift_one = jnp.sum(d_hidden * unit, axis=0), jnp.sum(d_hidden, axis=0)
    d_resid_one = norm_backward(d_hidden * norm_full[0], unit, unit_scale)
    d_attn = d_resid_one.astype(BF16)
    output_grad = dot_f32("td,tn->dn", d_attn, context).astype(BF16)
    d_context = jnp.dot(d_attn, out_w, preferred_element_type=F32).astype(BF16)

    def row_backward(packed):
        query_rows, key_rows, value_rows, row_segments, row_lse, row_grad = packed
        scores = masked_scores(query_rows, key_rows, row_segments)
        row_probs = jnp.exp(scores - row_lse[..., None])
        grad_heads = row_grad.reshape(seq_len, heads, HEAD_DIM)
        d_probs = dot_f32("qhd,khd->hqk", grad_heads, value_rows)
        row_inner = jnp.sum(d_probs * row_probs, axis=-1, keepdims=True)
        d_scores = (row_probs * (d_probs - row_inner)).astype(BF16)
        d_value = dot_f32("hqk,qhd->khd", row_probs.astype(BF16), grad_heads)
        d_query = dot_f32("hqk,khd->qhd", d_scores, key_rows) * score_scale
        d_key = dot_f32("hqk,qhd->khd", d_scores, query_rows) * score_scale
        return tuple(g.astype(BF16).reshape(seq_len, D) for g in (d_query, d_key, d_value))

    d_rows = lax.map(
        row_backward,
        (
            heads_split[0],
            heads_split[1],
            heads_split[2],
            segments,
            lse_rows,
            d_context.reshape(rows_here, seq_len, D),
        ),
    )
    d_proj = jnp.stack(d_rows).reshape(3, tokens_here, D)
    project_grad = dot_f32("tc,stn->scn", tokens, d_proj).astype(BF16)
    input_grad = d_resid_one + dot_f32("stn,scn->tc", d_proj, proj_w)
    norm_local = jnp.stack([d_gain_one, d_shift_one, d_gain_two, d_shift_two])
    norm_local = jnp.concatenate([norm_local, jnp.zeros_like(norm_local)])
    down_red, up_red, out_red, proj_red, norm_sum = scatter_grads(
        nz, down_grad, up_grad, output_grad, project_grad, norm_local
    )
    norm_red = lax.dynamic_slice(norm_sum, (0, norm_start), (4, norm_cols))
    return (
        layer_out,
        input_grad,
        *adam_step(proj_red, project_weight, project_momentum, project_squares, D ** (-0.5)),
        *adam_step(out_red, output_weight, output_momentum, output_squares, 4.0 * D ** (-0.5)),
        *adam_step(up_red, up_weight, up_momentum, up_squares, D ** (-0.5)),
        *adam_step(down_red, down_weight, down_momentum, down_squares, FF ** (-0.5)),
        *adam_step(norm_red, norm_params, norm_momentum, norm_squares, 0.3),
    )


def by_rows(mesh):
    dp, mp = mesh.shape["dp"], mesh.shape["mp"]
    return mp == 2 and dp >= 8 and dp & (dp - 1) == 0 and D % (64 * dp) == 0


def solution(mesh):
    body = local_rows if by_rows(mesh) else local_plain
    return jax.shard_map(
        body,
        mesh=mesh,
        in_specs=(
            P("dp", None),
            P(("dp", "mp"), None),
            P("dp", None),
            P(None, "dp", "mp"),
            P(None, "dp", "mp"),
            P(None, "dp", "mp"),
            P("dp", "mp"),
            P("dp", "mp"),
            P("dp", "mp"),
            P("dp", "mp"),
            P("dp", "mp"),
            P("dp", "mp"),
            P("dp", "mp"),
            P("dp", "mp"),
            P("dp", "mp"),
            P(None, ("dp", "mp")),
            P(None, ("dp", "mp")),
            P(None, ("dp", "mp")),
        ),
        out_specs=(
            P(("dp", "mp"), None),
            P(("dp", "mp"), None),
            P(None, "dp", "mp"),
            P(None, "dp", "mp"),
            P(None, "dp", "mp"),
            P(None, "dp", "mp"),
            P("dp", "mp"),
            P("dp", "mp"),
            P("dp", "mp"),
            P("dp", "mp"),
            P("dp", "mp"),
            P("dp", "mp"),
            P("dp", "mp"),
            P("dp", "mp"),
            P("dp", "mp"),
            P("dp", "mp"),
            P("dp", "mp"),
            P("dp", "mp"),
            P(None, ("dp", "mp")),
            P(None, ("dp", "mp")),
            P(None, ("dp", "mp")),
            P(None, ("dp", "mp")),
        ),
        check_vma=False,
    )
```

```python
import functools

import jax
import jax.numpy as jnp
from jax import lax
from jax.experimental import pallas as pl
from jax.experimental.pallas import tpu as pltpu
from jax.sharding import PartitionSpec as P

D = 1024
HEAD_DIM = 64
FF = 4096
STEP = 3


EPS_NORM = 1e-12
NEG_FILL = -1e30
BETA_ONE = 0.5
BETA_TWO = 0.5
ADAM_EPS = 1e-08
DECAY_RATE = 0.01


def layer_norm(values, norm_gain, norm_shift):
    center = values - jnp.mean(values, axis=-1, keepdims=True)
    spread = jnp.mean(center * center, axis=-1, keepdims=True)
    return center * lax.rsqrt(spread + EPS_NORM) * norm_gain + norm_shift


def exact_gelu(values):
    return jax.nn.gelu(values, approximate=False)


def adam_step(gradient, weight, first_old, second, step_rate):
    correct_one = 1.0 - BETA_ONE**STEP
    correct_two = 1.0 - BETA_TWO**STEP
    moment = BETA_ONE * first_old + (1.0 - BETA_ONE) * gradient
    square = BETA_TWO * second + (1.0 - BETA_TWO) * gradient * gradient
    normed = moment / correct_one / (jnp.sqrt(square / correct_two) + ADAM_EPS)
    updated = weight - step_rate * (normed + DECAY_RATE * weight)
    return (gradient, moment, square, updated)


def local_plain(
    tokens_in,
    cotangent,
    segment_ids,
    project_weight,
    project_momentum,
    project_squares,
    output_weight,
    output_momentum,
    output_squares,
    up_weight,
    up_momentum,
    up_squares,
    down_weight,
    down_momentum,
    down_squares,
    norm_params,
    norm_momentum,
    norm_squares,
):
    gathered = (
        lax.all_gather(project_weight.astype(jnp.bfloat16), "dp", axis=1, tiled=True),
        lax.all_gather(output_weight.astype(jnp.bfloat16), "dp", axis=0, tiled=True),
        lax.all_gather(up_weight.astype(jnp.bfloat16), "dp", axis=0, tiled=True),
        lax.all_gather(down_weight.astype(jnp.bfloat16), "dp", axis=0, tiled=True),
    )
    proj_copy, out_copy, up_copy, down_copy = gathered
    norm_full = lax.all_gather(
        norm_params.astype(jnp.bfloat16), ("dp", "mp"), axis=1, tiled=True
    ).astype(jnp.float32)
    rows_here = segment_ids.shape[0]
    seq_len = segment_ids.shape[1]
    local_width = proj_copy.shape[2]
    heads_here = local_width // HEAD_DIM
    score_scale = HEAD_DIM ** (-0.5)
    projected = jnp.einsum(
        "tc,scn->stn", tokens_in, proj_copy, preferred_element_type=jnp.float32
    ).astype(jnp.bfloat16)
    heads_split = projected.reshape(3, rows_here, seq_len, heads_here, HEAD_DIM)

    def masked_scores(query_rows, key_rows, row_segments):
        scores = (
            jnp.einsum("qhd,khd->hqk", query_rows, key_rows, preferred_element_type=jnp.float32)
            * score_scale
        )
        same_doc = row_segments[:, None] == row_segments[None, :]
        return jnp.where(same_doc[None], scores, NEG_FILL)

    def row_forward(packed):
        query_rows, key_rows, value_rows, row_segments = packed
        scores = masked_scores(query_rows, key_rows, row_segments)
        row_max = jnp.max(scores, axis=-1, keepdims=True)
        row_exp = jnp.exp(scores - row_max)
        row_total = jnp.sum(row_exp, axis=-1, keepdims=True)
        row_probs = (row_exp / row_total).astype(jnp.bfloat16)
        mixed = jnp.einsum(
            "hqk,khd->qhd", row_probs, value_rows, preferred_element_type=jnp.float32
        )
        row_lse = (row_max + jnp.log(row_total))[..., 0]
        return (mixed.astype(jnp.bfloat16).reshape(seq_len, local_width), row_lse)

    context_rows, lse_rows = lax.map(
        row_forward, (heads_split[0], heads_split[1], heads_split[2], segment_ids)
    )
    context = context_rows.reshape(rows_here * seq_len, local_width)
    attn_part = jnp.einsum("tn,dn->td", context, out_copy, preferred_element_type=jnp.float32)
    attn_share = lax.psum_scatter(
        attn_part.astype(jnp.bfloat16), "mp", scatter_dimension=0, tiled=True
    ).astype(jnp.float32)
    share_rows = attn_share.shape[0]
    share_start = lax.axis_index("mp") * share_rows
    token_share = lax.dynamic_slice_in_dim(tokens_in, share_start, share_rows, 0).astype(
        jnp.float32
    )
    hidden_one, norm_one_back = jax.vjp(
        layer_norm, token_share + attn_share, norm_full[0], norm_full[1]
    )
    hidden_low = lax.all_gather(hidden_one.astype(jnp.bfloat16), "mp", axis=0, tiled=True)
    pre_act = jnp.dot(hidden_low, up_copy, preferred_element_type=jnp.float32)
    act_full, gelu_back = jax.vjp(exact_gelu, pre_act)
    act_low = act_full.astype(jnp.bfloat16)
    ffn_part = jnp.einsum("tf,df->td", act_low, down_copy, preferred_element_type=jnp.float32)
    ffn_share = lax.psum_scatter(
        ffn_part.astype(jnp.bfloat16), "mp", scatter_dimension=0, tiled=True
    ).astype(jnp.float32)
    result, norm_two_back = jax.vjp(layer_norm, hidden_one + ffn_share, norm_full[2], norm_full[3])
    layer_out = result.astype(jnp.bfloat16)
    regathered = (
        lax.all_gather(project_weight.astype(jnp.bfloat16), "dp", axis=1, tiled=True),
        lax.all_gather(output_weight.astype(jnp.bfloat16), "dp", axis=0, tiled=True),
        lax.all_gather(up_weight.astype(jnp.bfloat16), "dp", axis=0, tiled=True),
        lax.all_gather(down_weight.astype(jnp.bfloat16), "dp", axis=0, tiled=True),
    )
    proj_copy, out_copy, up_copy, down_copy = regathered
    d_resid_two, d_gain_two, d_shift_two = norm_two_back(cotangent.astype(jnp.float32))
    d_ffn = lax.all_gather(d_resid_two.astype(jnp.bfloat16), "mp", axis=0, tiled=True)
    down_grad = jnp.einsum("td,tf->df", d_ffn, act_low, preferred_element_type=jnp.float32)
    d_act = jnp.dot(d_ffn, down_copy, preferred_element_type=jnp.float32)
    d_pre = gelu_back(d_act)[0].astype(jnp.bfloat16)
    up_grad = jnp.einsum("tc,tf->cf", hidden_low, d_pre, preferred_element_type=jnp.float32)
    d_hidden_part = jnp.einsum("tf,cf->tc", d_pre, up_copy, preferred_element_type=jnp.float32)
    d_hidden = d_resid_two + lax.psum_scatter(
        d_hidden_part.astype(jnp.bfloat16), "mp", scatter_dimension=0, tiled=True
    ).astype(jnp.float32)
    d_resid_one, d_gain_one, d_shift_one = norm_one_back(d_hidden)
    d_attn = lax.all_gather(d_resid_one.astype(jnp.bfloat16), "mp", axis=0, tiled=True)
    output_grad = jnp.einsum("td,tn->dn", d_attn, context, preferred_element_type=jnp.float32)
    d_context = jnp.dot(d_attn, out_copy, preferred_element_type=jnp.float32).astype(jnp.bfloat16)

    def row_backward(packed):
        query_rows, key_rows, value_rows, row_segments, row_lse, row_grad = packed
        scores = masked_scores(query_rows, key_rows, row_segments)
        row_probs = jnp.exp(scores - row_lse[..., None])
        grad_heads = row_grad.reshape(seq_len, heads_here, HEAD_DIM)
        d_probs = jnp.einsum(
            "qhd,khd->hqk", grad_heads, value_rows, preferred_element_type=jnp.float32
        )
        row_inner = jnp.sum(d_probs * row_probs, axis=-1, keepdims=True)
        d_scores = (row_probs * (d_probs - row_inner)).astype(jnp.bfloat16)
        d_value = jnp.einsum(
            "hqk,qhd->khd",
            row_probs.astype(jnp.bfloat16),
            grad_heads,
            preferred_element_type=jnp.float32,
        )
        d_query = (
            jnp.einsum("hqk,khd->qhd", d_scores, key_rows, preferred_element_type=jnp.float32)
            * score_scale
        )
        d_key = (
            jnp.einsum("hqk,qhd->khd", d_scores, query_rows, preferred_element_type=jnp.float32)
            * score_scale
        )
        return (
            d_query.astype(jnp.bfloat16).reshape(seq_len, local_width),
            d_key.astype(jnp.bfloat16).reshape(seq_len, local_width),
            d_value.astype(jnp.bfloat16).reshape(seq_len, local_width),
        )

    grad_context_rows = d_context.reshape(rows_here, seq_len, local_width)
    d_rows = lax.map(
        row_backward,
        (heads_split[0], heads_split[1], heads_split[2], segment_ids, lse_rows, grad_context_rows),
    )
    d_proj = jnp.stack(d_rows).reshape(3, rows_here * seq_len, local_width)
    project_grad = jnp.einsum("tc,stn->scn", tokens_in, d_proj, preferred_element_type=jnp.float32)
    d_input_part = jnp.einsum("stn,scn->tc", d_proj, proj_copy, preferred_element_type=jnp.float32)
    input_grad = d_resid_one + lax.psum_scatter(
        d_input_part.astype(jnp.bfloat16), "mp", scatter_dimension=0, tiled=True
    ).astype(jnp.float32)
    norm_local = jnp.stack([d_gain_one, d_shift_one, d_gain_two, d_shift_two])
    norm_red = lax.psum_scatter(norm_local, ("dp", "mp"), scatter_dimension=1, tiled=True)
    proj_red, out_red, up_red, down_red = (
        lax.psum_scatter(
            project_grad.astype(jnp.bfloat16), "dp", scatter_dimension=1, tiled=True
        ).astype(jnp.float32),
        lax.psum_scatter(
            output_grad.astype(jnp.bfloat16), "dp", scatter_dimension=0, tiled=True
        ).astype(jnp.float32),
        lax.psum_scatter(
            up_grad.astype(jnp.bfloat16), "dp", scatter_dimension=0, tiled=True
        ).astype(jnp.float32),
        lax.psum_scatter(
            down_grad.astype(jnp.bfloat16), "dp", scatter_dimension=0, tiled=True
        ).astype(jnp.float32),
    )
    proj_new = adam_step(proj_red, project_weight, project_momentum, project_squares, D ** (-0.5))
    out_new = adam_step(out_red, output_weight, output_momentum, output_squares, 4.0 * D ** (-0.5))
    up_new = adam_step(up_red, up_weight, up_momentum, up_squares, D ** (-0.5))
    down_new = adam_step(down_red, down_weight, down_momentum, down_squares, FF ** (-0.5))
    norm_new = adam_step(norm_red, norm_params, norm_momentum, norm_squares, 0.3)
    return (
        layer_out,
        input_grad,
        proj_new[0],
        proj_new[1],
        proj_new[2],
        proj_new[3],
        out_new[0],
        out_new[1],
        out_new[2],
        out_new[3],
        up_new[0],
        up_new[1],
        up_new[2],
        up_new[3],
        down_new[0],
        down_new[1],
        down_new[2],
        down_new[3],
        norm_new[0],
        norm_new[1],
        norm_new[2],
        norm_new[3],
    )


MESH = pl.DeviceIdType.MESH
BF16 = jnp.bfloat16
F32 = jnp.float32
ANY = pl.BlockSpec(memory_space=pl.ANY)
VMEM = pl.BlockSpec(memory_space=pltpu.VMEM)
DMA = pltpu.SemaphoreType.DMA

HOP_X, HOP_Y, HOP_C, OWN = (0, 1, 0, 0), (0, 0, 0, 1), (0, 0, 1, 0), (0, 0, 0, 0)


def hop_z(mask):
    return (mask, 0, 0, 0)


def position():
    dp = lax.axis_index("dp")
    return (dp // 4, (dp // 2) % 2, dp % 2, lax.axis_index("mp"))


def moved(me, hop):
    return tuple(m ^ h if h else m for m, h in zip(me, hop))


def device_at(me, hop):
    z, x, c, y = moved(me, hop)
    return (z * 4 + x * 2 + c, y)


def entry_barrier(me, nz):
    barrier = pltpu.get_barrier_semaphore()
    hops = [HOP_X, HOP_Y, HOP_C] + [hop_z(a) for a in range(1, nz)]
    for hop in hops:
        pl.semaphore_signal(barrier, inc=1, device_id=device_at(me, hop), device_id_type=MESH)
    pl.semaphore_wait(barrier, len(hops))


def view_rows(ref, pos):
    z, x, c, y = pos
    half = ref.shape[4] // 2
    return ref.at[z, x, c, :, pl.ds(pl.multiple_of(y * half, half), half)]


def view_stack(ref, pos):
    z, x, c, y = pos
    half = ref.shape[5] // 2
    return ref.at[:, z, x, c, :, pl.ds(pl.multiple_of(y * half, half), half)]


class Gather:
    def __init__(self, me, nz, own, out, view, send_sem, recv_sem, base):
        self.me, self.nz, self.own, self.out, self.view = me, nz, own, out, view
        self.send_sem, self.recv_sem, self.base = send_sem, recv_sem, base
        self.sent = []

    def slot(self, rel):
        a, b, d, e = rel
        return self.base + ((a * 2 + b) * 2 + d) * 2 + e

    def piece(self, rel):
        return self.view(self.out, moved(self.me, rel))

    def copy(self, rel, hop):
        arrives = tuple(r ^ h for r, h in zip(rel, hop))
        return pltpu.make_async_remote_copy(
            src_ref=self.own if rel == OWN else self.piece(rel),
            dst_ref=self.piece(rel),
            send_sem=self.send_sem.at[self.slot(arrives)],
            recv_sem=self.recv_sem.at[self.slot(arrives)],
            device_id=device_at(self.me, hop),
            device_id_type=MESH,
        )

    def send(self, rel, hop):
        self.copy(rel, hop).start()
        self.sent.append((rel, hop))

    def wait(self, rel):
        pltpu.make_async_remote_copy(
            src_ref=self.own,
            dst_ref=self.piece(rel),
            send_sem=self.send_sem.at[self.slot(rel)],
            recv_sem=self.recv_sem.at[self.slot(rel)],
            device_id=device_at(self.me, HOP_C),
            device_id_type=MESH,
        ).wait_recv()

    def run(self, steps):
        for kind, rel, hop in steps:
            if kind == "send":
                self.send(rel, hop)
            else:
                self.wait(rel)

    def steps_first(self):
        out = [("send", OWN, HOP_X), ("send", OWN, HOP_Y)]
        out += [("send", OWN, hop_z(a)) for a in range(1, self.nz)]
        return out + [("send", OWN, HOP_C)]

    def steps_square(self, a):
        out = [("wait", (a, 1, 0, 0), None), ("wait", (a, 0, 0, 1), None)]
        if a < self.nz // 2:
            out.append(("send", (a, 1, 0, 0), HOP_Y))
        else:
            out.append(("send", (a, 0, 0, 1), HOP_X))
        return out + [("send", (a, 1, 0, 0), HOP_C), ("send", (a, 0, 0, 1), HOP_C)]

    def steps_level(self, a):
        piece = hop_z(a)
        return [("wait", piece, None)] + [("send", piece, hop) for hop in (HOP_X, HOP_Y, HOP_C)]

    def steps_middle(self):
        out = []
        for a in range(1, self.nz):
            out += self.steps_level(a) + self.steps_square(a - 1)
        return out + self.steps_square(self.nz - 1)

    def steps_diagonal(self):
        out = []
        for a in range(self.nz):
            out += [("wait", (a, 1, 0, 1), None), ("send", (a, 1, 0, 1), HOP_C)]
        return out

    def steps_last(self):
        return [("wait", (a, b, 1, e), None) for a in range(self.nz) for b in range(2) for e in range(2)]

    def drain(self):
        for rel, hop in self.sent:
            self.copy(rel, hop).wait_send()


def sum_hops(nz):
    hops, mask = [HOP_C, HOP_X, HOP_Y], 1
    while mask < nz:
        hops.append(hop_z(mask))
        mask *= 2
    return hops


class SmallSum:
    def __init__(self, me, nz, parts, came, send_sem, recv_sem):
        self.me, self.hops, self.parts, self.came = me, sum_hops(nz), parts, came
        self.send_sem, self.recv_sem = send_sem, recv_sem

    def copy(self, i):
        return pltpu.make_async_remote_copy(
            src_ref=self.parts.at[i],
            dst_ref=self.came.at[i],
            send_sem=self.send_sem.at[i],
            recv_sem=self.recv_sem.at[i],
            device_id=device_at(self.me, self.hops[i]),
            device_id_type=MESH,
        )

    def start(self, i):
        self.copy(i).start()

    def finish(self, i):
        self.copy(i).wait()
        self.parts[i + 1] = self.parts[i] + self.came[i]


ERFC_SLOPE = 0.33 * 0.5**0.5
ERFC_POLY = (
    0.1863683316091749,
    0.1828075671230129,
    0.2020873146971517,
    0.044528074107268695,
    0.41336767744180025,
    -0.35626105794547547,
    0.4631297570306923,
    -0.13602774732192066,
)
PDF_SCALE = 0.3989422804014327


def gelu_pair(u):
    size = jnp.abs(u)
    t = 1.0 / (1.0 + ERFC_SLOPE * size)
    poly = 0.5 * ERFC_POLY[-1]
    for coefficient in ERFC_POLY[-2::-1]:
        poly = poly * t + 0.5 * coefficient
    bell = jnp.exp(u * u * -0.5)
    tail = poly * t * bell
    phi = jnp.where(u >= 0.0, 1.0 - tail, tail)
    return u * phi, phi + u * bell * PDF_SCALE


def dot_nn(a, b):
    return jnp.dot(a, b, preferred_element_type=F32)


def dot_nt(a, b):
    return lax.dot_general(a, b, (((1,), (1,)), ((), ())), preferred_element_type=F32)


def normed(rows):
    center = rows - jnp.mean(rows, axis=-1, keepdims=True)
    scale = lax.rsqrt(jnp.mean(center * center, axis=-1, keepdims=True) + EPS_NORM)
    return center * scale, scale


def norm_backward(grad, n, scale):
    inner = jnp.mean(grad * n, axis=-1, keepdims=True)
    return scale * (grad - jnp.mean(grad, axis=-1, keepdims=True) - n * inner)


def at_slots(i, plan):
    for k in sorted(plan):
        @pl.when(i == k)
        def _(k=k):
            for call in plan[k]:
                call()


def phase(count, parts, plan):
    def step(i, carry):
        for k, part in enumerate(parts):
            at_slots(i, {slot // len(parts): plan[slot] for slot in plan if slot % len(parts) == k})
            part(i)
        return carry

    lax.fori_loop(0, count, step, 0)


def spread(calls, spans):
    plans, calls = [{} for _ in spans], list(calls)
    for plan, (count, start, each) in zip(plans, spans):
        for i in range(count):
            while calls and calls[0][0] <= start + i * each:
                plan.setdefault(i, []).append(calls.pop(0)[1])
    return plans, calls


def gather_calls(gathers, costs, start):
    calls, marks, clock = [], [], start
    nz = gathers[0].nz

    def add(when, g, steps):
        calls.append((when, functools.partial(g.run, steps)))

    for i, (g, cost) in enumerate(zip(gathers, costs)):
        first = g.steps_first()
        if i == 0:
            add(clock, g, first)
        unit = cost / (3 * nz - 1)
        tick = 0
        for a in range(1, nz):
            tick += 1
            add(clock + tick * unit, g, g.steps_level(a))
            if a == nz - 1 and i + 1 < len(gathers):
                add(clock + tick * unit, gathers[i + 1], gathers[i + 1].steps_first()[2:-1])
            tick += 1
            add(clock + tick * unit, g, g.steps_square(a - 1))
        tick += 1
        add(clock + tick * unit, g, g.steps_square(nz - 1))
        if i + 1 < len(gathers):
            nxt = gathers[i + 1].steps_first()
            add(clock + tick * unit, gathers[i + 1], nxt[:2] + nxt[-1:])
        steps = g.steps_diagonal()
        for a in range(nz):
            tick += 1
            add(clock + tick * unit, g, steps[2 * a : 2 * a + 2])
        add(clock + cost, g, g.steps_last())
        marks.append(len(calls))
        clock += cost
    return calls, marks


def forward_kernel(nz, tokens, cotangent, seg_col, seg_row, proj, out, up, down, norm,
                   proj_all, out_all, up_all, down_all, norm_all, qkv_out, ctx_out, lse,
                   resid_out, hidden_out, act_out, slope_out, layer_out, dres_out, dffn_out, dnorm,
                   tok, cot, w_small, w_up, qkv, ctx, bias, res, hidden, act, pre, slope,
                   send_sem, recv_sem, local_sem, parts, came, sum_send, sum_recv, io_sem):
    me = position()
    t_here, seq = tok.shape[0], seg_row.shape[2]
    rows_here, pairs = t_here // seq, D // 128
    copies = {}

    def begin(key, src, dst, sem):
        copies[key] = pltpu.make_async_copy(src, dst, io_sem.at[sem])
        copies[key].start()

    mine = pl.ds(pl.multiple_of(me[3] * t_here, t_here), t_here)
    begin("tok", tokens.at[mine, :], tok, 0)
    begin("cot", cotangent, cot, 1)
    parts[0] = norm[...]
    entry_barrier(me, nz)
    owns, fulls = (proj, out, up, down), (proj_all, out_all, up_all, down_all)
    views = (view_stack, view_rows, view_rows, view_rows)
    n = 8 * nz
    gathers = [
        Gather(me, nz, owns[i], fulls[i], views[i], send_sem, recv_sem, n * i) for i in range(4)
    ]
    keep = [pltpu.make_async_copy(g.own, g.piece(OWN), local_sem.at[i]) for i, g in enumerate(gathers)]
    costs = FORWARD_COSTS
    calls, marks = gather_calls(gathers, costs, 0.0)
    calls[0][1]()
    for copy in keep:
        copy.start()
    small = SmallSum(me, nz, parts, came, sum_send, sum_recv)
    for i in range(len(small.hops)):
        small.start(i)
        small.finish(i)
    norm_all[...] = parts[len(small.hops)]

    def bias_step(r):
        rows = pl.ds(pl.multiple_of(r * seq, seq), seq)
        same = seg_col[rows, 0:1] == seg_row[r]
        bias[r] = jnp.where(same, 0.0, NEG_FILL)

    phase(rows_here, [bias_step], {})
    for _, call in calls[1 : marks[0]]:
        call()
    for copy in keep:
        copy.wait()
    copies["tok"].wait()
    begin("proj", proj_all, w_small.at[pl.ds(0, 3)], 2)

    step_q, step_a, step_o, step_u = FORWARD_STEPS
    n_q, n_a, n_o, n_u = 3 * D // 256, rows_here * pairs, t_here // 256, FF // 256
    start_q = costs[0] + 2.0
    start_a = start_q + n_q * step_q
    plans, _ = spread(
        calls[marks[0] : marks[2]], [(n_q, start_q, step_q), (n_a, start_a, step_a)]
    )
    done = sum(len(c) for plan in plans for c in plan.values())
    rest_out = calls[marks[0] + done : marks[1]]
    later = marks[0] + done + len(rest_out)
    copies["proj"].wait()

    def qkv_step(j):
        s, col = j // (D // 256), pl.ds(pl.multiple_of((j % (D // 256)) * 256, 256), 256)
        weight = w_small[s, :, :, :, :, col].reshape(D, 256)
        qkv[s, :, col] = dot_nn(tok[...], weight).astype(BF16)

    phase(n_q, [qkv_step], plans[0])
    begin("qkv", qkv, qkv_out, 3)
    head_of = lax.broadcasted_iota(jnp.int32, (128, 128), 1) // HEAD_DIM

    def attend_step(u):
        r, p = u // pairs, u % pairs
        col = pl.ds(pl.multiple_of(p * 128, 128), 128)
        for qb in range(seq // 128):
            low, high = max(0, qb - 2) * 128, min(seq // 128, qb + 3) * 128
            q_rows = pl.ds(pl.multiple_of(r * seq + qb * 128, 128), 128)
            k_rows = pl.ds(pl.multiple_of(r * seq + low, 128), high - low)
            q = qkv[0, q_rows, col] * jnp.asarray(HEAD_DIM**-0.5, BF16)
            both = jnp.concatenate([jnp.where(head_of == h, q, jnp.zeros_like(q)) for h in range(2)])
            block = bias[r, qb * 128 : qb * 128 + 128, low:high]
            scores = dot_nt(both, qkv[1, k_rows, col]) + jnp.concatenate([block, block])
            top = jnp.max(scores, axis=-1, keepdims=True)
            weights = jnp.exp(scores - top)
            total = jnp.sum(weights, axis=-1, keepdims=True)
            probs = (weights * (1.0 / total)).astype(BF16)
            mixed = dot_nn(probs, qkv[2, k_rows, col])
            ctx[q_rows, col] = jnp.where(head_of == 0, mixed[:128], mixed[128:]).astype(BF16)
            level = top + jnp.log(total)
            for h in range(2):
                wide = jnp.broadcast_to(level[h * 128 : h * 128 + 128], (128, 128))
                lse[u, h : h + 1, qb * 128 : qb * 128 + 128] = wide.T[0:1]

    phase(n_a, [attend_step], plans[1])
    for _, call in rest_out:
        call()
    begin("out", out_all, w_small.at[3], 4)
    begin("ctx", ctx, ctx_out, 5)
    start_o = max(start_a + n_a * step_a, costs[0] + costs[1])
    plans, rest_up = spread(calls[later : marks[2]], [(n_o, start_o, step_o)])
    copies["out"].wait()

    def out_step(m):
        rows = pl.ds(pl.multiple_of(m * 256, 256), 256)
        attended = dot_nt(ctx[rows, :], w_small[3].reshape(D, D))
        total = tok[rows, :].astype(F32) + attended
        res[rows, :] = total
        unit, _ = normed(total)
        hidden[rows, :] = (unit * norm_all[0:1, :] + norm_all[1:2, :]).astype(BF16)

    phase(n_o, [out_step], plans[0])
    begin("res", res, resid_out, 6)
    begin("hidden", hidden, hidden_out, 7)
    for _, call in rest_up:
        call()
    begin("up", up_all, w_up, 8)
    start_u = costs[0] + costs[1] + costs[2] + 2.0
    plans, rest_down = spread(calls[marks[2] :], [(n_u, start_u, step_u)])
    copies["up"].wait()

    def up_step(j):
        col = pl.ds(pl.multiple_of(j * 256, 256), 256)
        slot = j % 2
        pre[...] = dot_nn(hidden[...], w_up[:, :, :, :, col].reshape(D, 256))

        @pl.when(j >= 2)
        def _():
            slope_copy(j - 2, slot).wait()

        def chunk(i, carry):
            rows = pl.ds(pl.multiple_of(i * 32, 32), 32)
            value, tangent = gelu_pair(pre[rows, :])
            act[rows, col] = value.astype(BF16)
            slope[slot, rows, :] = tangent.astype(BF16)
            return carry

        lax.fori_loop(0, t_here // 32, chunk, 0)
        slope_copy(j, slot).start()

    def slope_copy(j, slot):
        col = pl.ds(pl.multiple_of(j * 256, 256), 256)
        return pltpu.make_async_copy(slope.at[slot], slope_out.at[:, col], io_sem.at[9 + slot])

    phase(n_u, [up_step], plans[0])
    begin("act", act, act_out, 11)
    for _, call in rest_down:
        call()
    for k in range(4):
        begin(("down", k), down_all.at[:, :, :, :, pl.ds(k * D, D)], w_small.at[k], 12 + k)
    for j in (n_u - 2, n_u - 1):
        slope_copy(j, j % 2).wait()
    for key in ("cot", "res", "hidden") + tuple(("down", k) for k in range(4)):
        copies[key].wait()
    dnorm[...] = jnp.zeros_like(dnorm)

    def down_step(m):
        rows = pl.ds(pl.multiple_of(m * 256, 256), 256)
        unit, _ = normed(res[rows, :])
        total = unit * norm_all[0:1, :] + norm_all[1:2, :]
        for k in range(4):
            total = total + dot_nt(act[rows, k * D : (k + 1) * D], w_small[k].reshape(D, D))
        unit, scale = normed(total)
        tok[rows, :] = (unit * norm_all[2:3, :] + norm_all[3:4, :]).astype(BF16)
        grad = cot[rows, :].astype(F32)
        dnorm[0:1, :] = dnorm[0:1, :] + jnp.sum(grad * unit, axis=0, keepdims=True)
        dnorm[1:2, :] = dnorm[1:2, :] + jnp.sum(grad, axis=0, keepdims=True)
        dres = norm_backward(grad * norm_all[2:3, :], unit, scale)
        res[rows, :] = dres
        hidden[rows, :] = dres.astype(BF16)

    phase(t_here // 256, [down_step], {})
    begin("layer", tok, layer_out, 16)
    begin("dres", res, dres_out, 17)
    begin("dffn", hidden, dffn_out, 18)
    for key in ("qkv", "ctx", "act", "layer", "dres", "dffn"):
        copies[key].wait()
    for g in gathers:
        g.drain()


FORWARD_COSTS = (31.0, 10.0, 42.0, 42.0)
FORWARD_STEPS = (0.8, 1.4, 1.2, 1.7)


def run_forward(nz, tokens_in, cotangent, segments, proj, out, up, down, norm):
    t_here = cotangent.shape[0]
    rows_here, seq = segments.shape
    n_sum = len(sum_hops(nz))
    rows = D // (4 * nz)
    full = lambda cols: jax.ShapeDtypeStruct((nz, 2, 2, rows, cols), BF16)
    flat = lambda cols, kind: jax.ShapeDtypeStruct((t_here, cols), kind)
    seg_col = jnp.broadcast_to(segments.reshape(t_here, 1), (t_here, 128))
    seg_row = segments.reshape(rows_here, 1, seq)
    return pl.pallas_call(
        functools.partial(forward_kernel, nz),
        out_shape=[
            jax.ShapeDtypeStruct((3, nz, 2, 2, rows, D), BF16),
            full(D),
            full(FF),
            full(FF),
            jax.ShapeDtypeStruct(norm.shape, F32),
            jax.ShapeDtypeStruct((3, t_here, D), BF16),
            flat(D, BF16),
            jax.ShapeDtypeStruct((rows_here * (D // 128), 8, seq), F32),
            flat(D, F32),
            flat(D, BF16),
            flat(FF, BF16),
            flat(FF, BF16),
            flat(D, BF16),
            flat(D, F32),
            flat(D, BF16),
            jax.ShapeDtypeStruct((8, D), F32),
        ],
        in_specs=[ANY, ANY, VMEM, VMEM, ANY, ANY, ANY, ANY, VMEM],
        out_specs=[ANY] * 4 + [VMEM, ANY, ANY, VMEM] + [ANY] * 7 + [VMEM],
        scratch_shapes=[
            pltpu.VMEM((t_here, D), BF16),
            pltpu.VMEM((t_here, D), BF16),
            pltpu.VMEM((4, nz, 2, 2, rows, D), BF16),
            pltpu.VMEM((nz, 2, 2, rows, FF), BF16),
            pltpu.VMEM((3, t_here, D), BF16),
            pltpu.VMEM((t_here, D), BF16),
            pltpu.VMEM((rows_here, seq, seq), F32),
            pltpu.VMEM((t_here, D), F32),
            pltpu.VMEM((t_here, D), BF16),
            pltpu.VMEM((t_here, FF), BF16),
            pltpu.VMEM((t_here, 256), F32),
            pltpu.VMEM((2, t_here, 256), BF16),
            DMA((32 * nz,)),
            DMA((32 * nz,)),
            DMA((4,)),
            pltpu.VMEM((n_sum + 1,) + norm.shape, F32),
            pltpu.VMEM((n_sum,) + norm.shape, F32),
            DMA((n_sum,)),
            DMA((n_sum,)),
            DMA((19,)),
        ],
        compiler_params=pltpu.CompilerParams(
            collective_id=0, has_side_effects=True, vmem_limit_bytes=60 << 20
        ),
        name="forward",
    )(tokens_in, cotangent, seg_col, seg_row, proj, out, up, down, norm)


def view_flat(ref, pos):
    z, x, c, y = pos
    rows, half = 64, ref.shape[1] // 2
    row = (z * 4 + x * 2 + c) * rows
    return ref.at[pl.ds(pl.multiple_of(row, rows), rows), pl.ds(pl.multiple_of(y * half, half), half)]


def add_rows(dst, terms, rows=16):
    def body(i, carry):
        block = pl.ds(pl.multiple_of(i * rows, rows), rows)
        total = terms[0][block, :].astype(F32)
        for term in terms[1:]:
            total = total + term[block, :].astype(F32)
        dst[block, :] = total.astype(dst.dtype)
        return carry

    lax.fori_loop(0, dst.shape[0] // rows, body, 0)


class Scatter:
    def __init__(self, me, nz, index, grad, from_c, held, swap, came, result, sems, before):
        self.me, self.nz, self.index, self.grad, self.from_c = me, nz, index, grad, from_c
        self.held, self.swap, self.came, self.result = held, swap, came, result
        self.load_sem, self.send_sem, self.recv_sem = sems
        self.before = before
        half = nz // 2
        self.order = [a for k in range(half) for a in (nz - 1 - k, half - 1 - k)]

    def where(self, a, b, e):
        return (a * 2 + b) * 2 + e

    def remote(self, src, dst, slot, hop):
        sem = self.index * 8 * self.nz + slot
        return pltpu.make_async_remote_copy(
            src_ref=src, dst_ref=dst, send_sem=self.send_sem.at[sem], recv_sem=self.recv_sem.at[sem],
            device_id=device_at(self.me, hop), device_id_type=MESH,
        )

    def core_copy(self, a, b, e):
        i = self.where(a, b, e)
        return self.remote(view_flat(self.grad, moved(self.me, (a, b, 1, e))), self.from_c.at[i], i, HOP_C)

    def hop_copy(self, kind, a):
        low = a < self.nz // 2
        b, e = {"d": (1, 1), "x": (1, 0), "y": (0, 1), "z": (0, 0)}[kind]
        hop = {"d": HOP_Y if low else HOP_X, "x": HOP_X, "y": HOP_Y, "z": hop_z(a)}[kind]
        k = "dxyz".index(kind)
        return self.remote(
            self.held.at[self.where(a, b, e)], self.came.at[k * self.nz + a], (4 + k) * self.nz + a, hop
        )

    def took(self, kind, a):
        self.hop_copy(kind, a).wait_recv()
        return self.came.at["dxyz".index(kind) * self.nz + a]

    def loads(self, a):
        side = self.order.index(a) % 2
        out = []
        for b in range(2):
            for e in range(2):
                i, k = self.where(a, b, e), b * 2 + e
                out.append(pltpu.make_async_copy(
                    view_flat(self.grad, moved(self.me, (a, b, 0, e))), self.held.at[i], self.load_sem.at[side * 8 + k]
                ))
                out.append(pltpu.make_async_copy(
                    self.from_c.at[i], self.swap.at[side * 4 + k], self.load_sem.at[side * 8 + 4 + k]
                ))
        return out

    def exchange(self, a):
        for b, e in ((1, 1), (1, 0), (0, 1), (0, 0)):
            self.core_copy(a, b, e).start()

    def fetch(self, a):
        if self.before is not None:
            self.before.release(a)
        for b, e in ((1, 1), (1, 0), (0, 1), (0, 0)):
            self.core_copy(a, b, e).wait_recv()
        for load in self.loads(a):
            load.start()

    def diagonal(self, a):
        for load in self.loads(a):
            load.wait()
        side, low = self.order.index(a) % 2, a < self.nz // 2
        for b, e in ((1, 1), (1, 0), (0, 1), (0, 0)):
            mine = self.held.at[self.where(a, b, e)]
            add_rows(mine, [mine, self.swap.at[side * 4 + b * 2 + e]])
            if (b, e) == (1, 1):
                self.hop_copy("d", a).start()
            elif (b, e) == ((0, 1) if low else (1, 0)):
                self.hop_copy("y" if low else "x", a).start()

    def square(self, a):
        low = a < self.nz // 2
        b, e = (1, 0) if low else (0, 1)
        mine = self.held.at[self.where(a, b, e)]
        add_rows(mine, [mine, self.took("d", a)])
        self.hop_copy("x" if low else "y", a).start()

    def column(self, a):
        mine = self.held.at[self.where(a, 0, 0)]
        terms = [mine, self.took("x", a), self.took("y", a)]
        if a:
            add_rows(mine, terms)
            self.hop_copy("z", a).start()
        else:
            add_rows(self.result, terms + [self.took("z", k) for k in range(1, self.nz)])

    def release(self, a):
        for b in range(2):
            for e in range(2):
                self.core_copy(a, b, e).wait_send()
        for kind in "dxyz" if a else "dxy":
            self.hop_copy(kind, a).wait_send()

    def calls(self, start, cost):
        n = len(self.order)
        out = [(start, functools.partial(self.exchange, a)) for a in self.order]
        kinds = (self.fetch, self.diagonal, self.square, self.column)
        lags = (0, 2, 3, 4)
        steps = [
            functools.partial(kind, self.order[t - lag])
            for t in range(n + lags[-1])
            for kind, lag in reversed(list(zip(kinds, lags)))
            if 0 <= t - lag < n
        ]
        unit = cost / len(steps)
        return out + [(start + unit * (i + 1), step) for i, step in enumerate(steps)]


def transpose_into(dst, src):
    def body(i, carry):
        block = pl.ds(pl.multiple_of(i * 128, 128), 128)
        dst[:, block] = src[block, :].T
        return carry

    lax.fori_loop(0, src.shape[0] // 128, body, 0)


def backward_kernel(nz, tokens, seg_col, seg_row, proj, out, up, down, norm, qkv_in, ctx_in, lse,
                    resid, hidden, act, slope, dres, dffn, dnorm_two,
                    input_grad, down_red, up_red, mix_red, norm_sum,
                    down_grad, up_grad, mix_grad, down_c, up_c, mix_c,
                    tiles, buf_a, buf_b, buf_c, total, dpre, stage, ctx, w_out, bias, dqkv, resid_tile, dq,
                    held, swap, came_down, came_up, came_mix,
                    load_sem, send_sem, recv_sem, io_sem, parts, came, sum_send, sum_recv):
    me = position()
    t_here, seq = total.shape[0], seg_row.shape[2]
    rows_here, pairs = t_here // seq, D // 128
    n_ff = FF // 512
    copies = {}

    def begin(key, src, dst, sem):
        copies[key] = pltpu.make_async_copy(src, dst, io_sem.at[sem])
        copies[key].start()

    def col512(j):
        return pl.ds(pl.multiple_of(j * 512, 512), 512)

    def tile_copy(src, j, base, sem):
        return pltpu.make_async_copy(src.at[:, col512(j)], tiles.at[base + j % 2], io_sem.at[sem + j % 2])

    def stage_copy(dst, col, slot):
        return pltpu.make_async_copy(stage.at[slot], dst.at[:, col], io_sem.at[8 + slot])

    def put_stage(i, value, dst, col):
        slot = i % 2

        @pl.when(i >= 2)
        def _():
            stage_copy(dst, col, slot).wait()

        stage[slot] = value.astype(BF16)
        stage_copy(dst, col, slot).start()

    def flush_stage(dst):
        for slot in range(2):
            stage_copy(dst, pl.ds(0, 512), slot).wait()

    begin("dffn", dffn, buf_a, 10)
    begin("hidden", hidden, ctx, 11)
    begin("dres", dres, total, 12)
    tile_copy(act, 0, 0, 0).start()
    entry_barrier(me, nz)
    sems = (load_sem, send_sem, recv_sem)
    first = Scatter(me, nz, 0, down_grad, down_c, held, swap, came_down, down_red, sems, None)
    second = Scatter(me, nz, 1, up_grad, up_c, held, swap, came_up, up_red, sems, first)
    third = Scatter(me, nz, 2, mix_grad, mix_c, held, swap, came_mix, mix_red, sems, second)
    small = SmallSum(me, nz, parts, came, sum_send, sum_recv)

    step_down, step_ffn, step_ln, step_out, step_attn, step_proj, step_in = BACKWARD_STEPS
    cost = BACKWARD_COST
    n_attn, n_m = rows_here * pairs, t_here // 256
    t_down = n_ff * step_down
    t_ffn = t_down + 3 * n_ff * step_ffn
    t_ln = t_ffn + n_m * step_ln
    t_mix = t_ln + 4 * step_out
    t_attn = t_mix + n_attn * step_attn
    t_proj = t_attn + 6 * step_proj
    calls = first.calls(t_down, cost)
    plans, left = spread(calls, [(3 * n_ff, t_down, step_ffn)])
    plan_ffn = plans[0]
    calls = left + second.calls(max(t_ffn, t_down + cost), cost)
    n_small = len(small.hops)
    sums = [(t_ln, functools.partial(small.start, 0))]
    for i in range(n_small):
        sums.append((t_mix + 4.0 * (i + 1), functools.partial(small.finish, i)))
        if i + 1 < n_small:
            sums.append((t_mix + 4.0 * (i + 1), functools.partial(small.start, i + 1)))
    calls = sorted(calls + sums, key=lambda c: c[0])
    plans, left = spread(
        calls,
        [(n_m, t_ffn, step_ln), (2, t_ln, step_out), (2, t_ln + 2 * step_out, step_out),
         (n_attn, t_mix, step_attn), (6, t_attn, step_proj)],
    )
    plan_ln, plan_out, plan_ctx, plan_attn, plan_proj = plans

    copies["dffn"].wait()
    transpose_into(buf_b, buf_a)

    def down_step(j):
        @pl.when(j + 1 < n_ff)
        def _():
            tile_copy(act, j + 1, 0, 0).start()

        tile_copy(act, j, 0, 0).wait()
        put_stage(j, dot_nn(buf_b[...], tiles[j % 2]), down_grad, col512(j))

    phase(n_ff, [down_step], {})
    for src, base in ((down, 2), (slope, 4), (up, 6)):
        tile_copy(src, 0, base, base).start()
    copies["hidden"].wait()
    transpose_into(buf_c, ctx)
    begin("ctx", ctx_in, ctx, 11)
    begin("w_out", out, w_out, 13)
    flush_stage(down_grad)
    copies["dres"].wait()

    def pre_step(j):
        @pl.when(j + 1 < n_ff)
        def _():
            for src, base in ((down, 2), (slope, 4), (up, 6)):
                tile_copy(src, j + 1, base, base).start()

        for src, base in ((down, 2), (slope, 4), (up, 6)):
            tile_copy(src, j, base, base).wait()
        dpre[...] = (dot_nn(buf_a[...], tiles[2 + j % 2]) * tiles[4 + j % 2].astype(F32)).astype(BF16)

    def up_grad_step(j):
        put_stage(j, dot_nn(buf_c[...], dpre[...]), up_grad, col512(j))

    def hidden_step(j):
        total[...] += dot_nt(dpre[...], tiles[6 + j % 2])

    phase(n_ff, [pre_step, up_grad_step, hidden_step], plan_ffn)
    flush_stage(up_grad)
    for i in range(6):
        begin(("qkv", i), qkv_in.at[i // 2, :, pl.ds((i % 2) * 512, 512)], tiles.at[i], i)
    norm_sum[...] = jnp.zeros_like(norm_sum)

    def resid_copy(m):
        rows = pl.ds(pl.multiple_of(m * 256, 256), 256)
        return pltpu.make_async_copy(resid.at[rows, :], resid_tile.at[m % 2], io_sem.at[14 + m % 2])

    resid_copy(0).start()

    def norm_step(m):
        @pl.when(m + 1 < n_m)
        def _():
            resid_copy(m + 1).start()

        resid_copy(m).wait()
        rows = pl.ds(pl.multiple_of(m * 256, 256), 256)
        unit, scale = normed(resid_tile[m % 2])
        grad = total[rows, :]
        norm_sum[0:1, :] = norm_sum[0:1, :] + jnp.sum(grad * unit, axis=0, keepdims=True)
        norm_sum[1:2, :] = norm_sum[1:2, :] + jnp.sum(grad, axis=0, keepdims=True)
        moved_grad = norm_backward(grad * norm[0:1, :], unit, scale)
        total[rows, :] = moved_grad
        buf_b[rows, :] = moved_grad.astype(BF16)

    phase(n_m, [norm_step], plan_ln)
    norm_sum[2:4, :] = dnorm_two[0:2, :]
    parts[0] = norm_sum[...]
    transpose_into(buf_a, buf_b)
    copies["ctx"].wait()
    copies["w_out"].wait()

    def out_grad_step(j):
        put_stage(j, dot_nn(buf_a[...], ctx[:, col512(j)]), mix_grad, col512(4 * j + 3))

    phase(2, [out_grad_step], plan_out)

    def ctx_step(j):
        buf_a[:, col512(j)] = dot_nn(buf_b[...], w_out[:, col512(j)]).astype(BF16)

    phase(2, [ctx_step], plan_ctx)
    flush_stage(mix_grad)
    mine = pl.ds(pl.multiple_of(me[3] * t_here, t_here), t_here)
    begin("tok", tokens.at[mine, :], buf_b, 10)

    def bias_step(r):
        rows = pl.ds(pl.multiple_of(r * seq, seq), seq)
        bias[r] = jnp.where(seg_col[rows, 0:1] == seg_row[r], 0.0, NEG_FILL)

    phase(rows_here, [bias_step], {})
    for i in range(6):
        copies[("qkv", i)].wait()
    head_of = lax.broadcasted_iota(jnp.int32, (128, 128), 1) // HEAD_DIM
    head_pick = (
        lax.broadcasted_iota(jnp.int32, (8, 128), 1) // HEAD_DIM == lax.broadcasted_iota(jnp.int32, (8, 128), 0)
    ).astype(BF16)
    shrink = jnp.asarray(HEAD_DIM**-0.5, BF16)

    def per_head(block):
        return jnp.concatenate([jnp.where(head_of == h, block, jnp.zeros_like(block)) for h in range(2)])

    def attend_step(u):
        r, p = u // pairs, u % pairs
        side = p // 4
        col = pl.ds(pl.multiple_of(p * 128, 128), 128)
        near = pl.ds(pl.multiple_of((p % 4) * 128, 128), 128)
        whole = pl.ds(pl.multiple_of(r * seq, seq), seq)
        product = buf_a[whole, col].astype(F32) * ctx[whole, col].astype(F32)
        coarse = product.astype(BF16)
        fine = (product - coarse.astype(F32)).astype(BF16)
        delta = dot_nt(head_pick, coarse) + dot_nt(head_pick, fine)
        dq[...] = jnp.zeros_like(dq)
        for kb in range(seq // 128):
            low, high = max(0, kb - 2) * 128, min(seq // 128, kb + 3) * 128
            k_rows = pl.ds(pl.multiple_of(r * seq + kb * 128, 128), 128)
            q_rows = pl.ds(pl.multiple_of(r * seq + low, 128), high - low)
            q = tiles[side, q_rows, near] * shrink
            keys = per_head(tiles[2 + side, k_rows, near])
            grad = buf_a[q_rows, col]
            block = bias[r, kb * 128 : kb * 128 + 128, low:high]
            scores = dot_nt(keys, q)
            d_probs = dot_nt(per_head(tiles[4 + side, k_rows, near]), grad)
            probs, d_scores = [], []
            for h in range(2):
                part = slice(h * 128, h * 128 + 128)
                prob = jnp.exp(scores[part] + block - lse[u, h : h + 1, low:high])
                probs.append(prob.astype(BF16))
                d_scores.append((prob * (d_probs[part] - delta[h : h + 1, low:high])).astype(BF16))
            probs, d_scores = jnp.concatenate(probs), jnp.concatenate(d_scores)
            d_value = dot_nn(probs, grad)
            d_key = dot_nn(d_scores, q)
            dqkv[4 + side, k_rows, near] = jnp.where(head_of == 0, d_value[:128], d_value[128:]).astype(BF16)
            dqkv[2 + side, k_rows, near] = jnp.where(head_of == 0, d_key[:128], d_key[128:]).astype(BF16)
            dq[:, low:high] += dot_nn(keys.T, d_scores)
        dqkv[side, whole, near] = (dq[...].T * HEAD_DIM**-0.5).astype(BF16)

    phase(n_attn, [attend_step], plan_attn)
    for i in range(6):
        begin(("proj", i), proj.at[i // 2, :, pl.ds((i % 2) * 512, 512)], tiles.at[i], i)
    copies["tok"].wait()
    transpose_into(buf_c, buf_b)

    def proj_step(i):
        put_stage(i, dot_nn(buf_c[...], dqkv[i]), mix_grad, col512((i % 2) * 4 + i // 2))

    phase(6, [proj_step], plan_proj)
    flush_stage(mix_grad)
    for i in range(6):
        copies[("proj", i)].wait()
    calls = left + third.calls(t_proj, cost)
    plans, left = spread(calls, [(n_m, t_proj, step_in)])

    def in_copy(m):
        rows = pl.ds(pl.multiple_of(m * 256, 256), 256)
        return pltpu.make_async_copy(total.at[rows, :], input_grad.at[rows, :], io_sem.at[16 + m])

    def input_step(m):
        rows = pl.ds(pl.multiple_of(m * 256, 256), 256)
        value = total[rows, :]
        for i in range(6):
            value = value + dot_nt(dqkv[i, rows, :], tiles[i])
        total[rows, :] = value

    phase(n_m, [input_step], plans[0])
    for m in range(n_m):
        in_copy(m).start()
    for _, call in left:
        call()
    for a in third.order:
        third.release(a)
    for m in range(n_m):
        in_copy(m).wait()
    norm_sum[...] = parts[n_small]


BACKWARD_STEPS = (1.5, 1.5, 1.2, 1.5, 2.6, 1.6, 2.6)
BACKWARD_COST = 42.0


def run_backward(nz, tokens_in, segments, proj, out, up, down, norm, qkv, ctx, lse,
                 resid, hidden, act, slope, dres, dffn, dnorm_two):
    t_here = dffn.shape[0]
    rows_here, seq = segments.shape
    n_sum = len(sum_hops(nz))
    piece = (64, FF // 2)
    seg_col = jnp.broadcast_to(segments.reshape(t_here, 1), (t_here, 128))
    seg_row = segments.reshape(rows_here, 1, seq)
    grad = jax.ShapeDtypeStruct((D, FF), BF16)
    swapped = jax.ShapeDtypeStruct((4 * nz,) + piece, BF16)
    red = jax.ShapeDtypeStruct(piece, F32)
    results = pl.pallas_call(
        functools.partial(backward_kernel, nz),
        out_shape=[jax.ShapeDtypeStruct((t_here, D), F32), red, red, red, jax.ShapeDtypeStruct(norm.shape, F32)]
        + [grad] * 3 + [swapped] * 3,
        in_specs=[ANY, VMEM, VMEM] + [ANY] * 4 + [VMEM, ANY, ANY, VMEM] + [ANY] * 6 + [VMEM],
        out_specs=[ANY] + [VMEM] * 4 + [ANY] * 6,
        scratch_shapes=[
            pltpu.VMEM((8, t_here, 512), BF16),
            pltpu.VMEM((t_here, D), BF16),
            pltpu.VMEM((t_here, D), BF16),
            pltpu.VMEM((t_here, D), BF16),
            pltpu.VMEM((t_here, D), F32),
            pltpu.VMEM((t_here, 512), BF16),
            pltpu.VMEM((2, t_here, 512), BF16),
            pltpu.VMEM((t_here, D), BF16),
            pltpu.VMEM((D, D), BF16),
            pltpu.VMEM((rows_here, seq, seq), F32),
            pltpu.VMEM((6, t_here, 512), BF16),
            pltpu.VMEM((2, 256, D), F32),
            pltpu.VMEM((128, seq), F32),
            pltpu.VMEM((4 * nz,) + piece, BF16),
            pltpu.VMEM((8,) + piece, BF16),
            pltpu.VMEM((4 * nz,) + piece, BF16),
            pltpu.VMEM((4 * nz,) + piece, BF16),
            pltpu.VMEM((4 * nz,) + piece, BF16),
            DMA((16,)),
            DMA((24 * nz,)),
            DMA((24 * nz,)),
            DMA((20,)),
            pltpu.VMEM((n_sum + 1,) + norm.shape, F32),
            pltpu.VMEM((n_sum,) + norm.shape, F32),
            DMA((n_sum,)),
            DMA((n_sum,)),
        ],
        compiler_params=pltpu.CompilerParams(
            collective_id=1, has_side_effects=True, vmem_limit_bytes=62 << 20
        ),
        name="backward",
    )(tokens_in, seg_col, seg_row, proj, out, up, down, norm, qkv, ctx, lse,
      resid, hidden, act, slope, dres, dffn, dnorm_two)
    return results[:5]


def local_rows(
    tokens_in,
    cotangent,
    segment_ids,
    project_weight,
    project_momentum,
    project_squares,
    output_weight,
    output_momentum,
    output_squares,
    up_weight,
    up_momentum,
    up_squares,
    down_weight,
    down_momentum,
    down_squares,
    norm_params,
    norm_momentum,
    norm_squares,
):
    nz = lax.axis_size("dp") // 4
    dp, mp = lax.axis_index("dp"), lax.axis_index("mp")
    norm_cols = norm_params.shape[1]
    norm_start = (dp * 2 + mp) * norm_cols
    norm_wide = lax.dynamic_update_slice(
        jnp.zeros((8, D), F32), norm_params.astype(BF16).astype(F32), (0, norm_start)
    )
    rows_here = segment_ids.shape[0] // 2
    segments = lax.dynamic_slice_in_dim(segment_ids, mp * rows_here, rows_here, 0)
    (proj_w, out_w, up_w, down_w, norm_full, qkv, context, lse, resid_one, hidden_low, act_low, slope,
     layer_out, d_resid_two, d_ffn, d_norm_two) = run_forward(
        nz,
        tokens_in,
        cotangent,
        segments,
        project_weight.astype(BF16),
        output_weight.astype(BF16),
        up_weight.astype(BF16),
        down_weight.astype(BF16),
        norm_wide,
    )
    input_grad, down_red, up_red, mix_red, norm_sum = run_backward(
        nz,
        tokens_in,
        segments,
        proj_w.reshape(3, D, D),
        out_w.reshape(D, D),
        up_w.reshape(D, FF),
        down_w.reshape(D, FF),
        norm_full,
        qkv,
        context,
        lse,
        resid_one,
        hidden_low,
        act_low,
        slope,
        d_resid_two,
        d_ffn,
        d_norm_two,
    )
    mix_red = mix_red.reshape(mix_red.shape[0], 4, -1).transpose(1, 0, 2)
    proj_red, out_red = mix_red[:3], mix_red[3]
    norm_red = lax.dynamic_slice(norm_sum, (0, norm_start), (4, norm_cols))
    return (
        layer_out,
        input_grad,
        *adam_step(proj_red, project_weight, project_momentum, project_squares, D ** (-0.5)),
        *adam_step(out_red, output_weight, output_momentum, output_squares, 4.0 * D ** (-0.5)),
        *adam_step(up_red, up_weight, up_momentum, up_squares, D ** (-0.5)),
        *adam_step(down_red, down_weight, down_momentum, down_squares, FF ** (-0.5)),
        *adam_step(norm_red, norm_params, norm_momentum, norm_squares, 0.3),
    )


def by_rows(mesh):
    dp, mp = mesh.shape["dp"], mesh.shape["mp"]
    return mp == 2 and dp >= 8 and dp & (dp - 1) == 0 and D % (64 * dp) == 0


def solution(mesh):
    body = local_rows if by_rows(mesh) else local_plain
    return jax.shard_map(
        body,
        mesh=mesh,
        in_specs=(
            P("dp", None),
            P(("dp", "mp"), None),
            P("dp", None),
            P(None, "dp", "mp"),
            P(None, "dp", "mp"),
            P(None, "dp", "mp"),
            P("dp", "mp"),
            P("dp", "mp"),
            P("dp", "mp"),
            P("dp", "mp"),
            P("dp", "mp"),
            P("dp", "mp"),
            P("dp", "mp"),
            P("dp", "mp"),
            P("dp", "mp"),
            P(None, ("dp", "mp")),
            P(None, ("dp", "mp")),
            P(None, ("dp", "mp")),
        ),
        out_specs=(
            P(("dp", "mp"), None),
            P(("dp", "mp"), None),
            P(None, "dp", "mp"),
            P(None, "dp", "mp"),
            P(None, "dp", "mp"),
            P(None, "dp", "mp"),
            P("dp", "mp"),
            P("dp", "mp"),
            P("dp", "mp"),
            P("dp", "mp"),
            P("dp", "mp"),
            P("dp", "mp"),
            P("dp", "mp"),
            P("dp", "mp"),
            P("dp", "mp"),
            P("dp", "mp"),
            P("dp", "mp"),
            P("dp", "mp"),
            P(None, ("dp", "mp")),
            P(None, ("dp", "mp")),
            P(None, ("dp", "mp")),
            P(None, ("dp", "mp")),
        ),
        check_vma=False,
    )
```

```python
import functools

import jax
import jax.numpy as jnp
from jax import lax
from jax.experimental import pallas as pl
from jax.experimental.pallas import tpu as pltpu
from jax.sharding import PartitionSpec as P

D = 1024
HEAD_DIM = 64
FF = 4096
STEP = 3


EPS_NORM = 1e-12
NEG_FILL = -1e30
BETA_ONE = 0.5
BETA_TWO = 0.5
ADAM_EPS = 1e-08
DECAY_RATE = 0.01


def layer_norm(values, norm_gain, norm_shift):
    center = values - jnp.mean(values, axis=-1, keepdims=True)
    spread = jnp.mean(center * center, axis=-1, keepdims=True)
    return center * lax.rsqrt(spread + EPS_NORM) * norm_gain + norm_shift


def exact_gelu(values):
    return jax.nn.gelu(values, approximate=False)


def adam_step(gradient, weight, first_old, second, step_rate):
    correct_one = 1.0 - BETA_ONE**STEP
    correct_two = 1.0 - BETA_TWO**STEP
    moment = BETA_ONE * first_old + (1.0 - BETA_ONE) * gradient
    square = BETA_TWO * second + (1.0 - BETA_TWO) * gradient * gradient
    normed = moment / correct_one / (jnp.sqrt(square / correct_two) + ADAM_EPS)
    updated = weight - step_rate * (normed + DECAY_RATE * weight)
    return (gradient, moment, square, updated)


def local_plain(
    tokens_in,
    cotangent,
    segment_ids,
    project_weight,
    project_momentum,
    project_squares,
    output_weight,
    output_momentum,
    output_squares,
    up_weight,
    up_momentum,
    up_squares,
    down_weight,
    down_momentum,
    down_squares,
    norm_params,
    norm_momentum,
    norm_squares,
):
    gathered = (
        lax.all_gather(project_weight.astype(jnp.bfloat16), "dp", axis=1, tiled=True),
        lax.all_gather(output_weight.astype(jnp.bfloat16), "dp", axis=0, tiled=True),
        lax.all_gather(up_weight.astype(jnp.bfloat16), "dp", axis=0, tiled=True),
        lax.all_gather(down_weight.astype(jnp.bfloat16), "dp", axis=0, tiled=True),
    )
    proj_copy, out_copy, up_copy, down_copy = gathered
    norm_full = lax.all_gather(
        norm_params.astype(jnp.bfloat16), ("dp", "mp"), axis=1, tiled=True
    ).astype(jnp.float32)
    rows_here = segment_ids.shape[0]
    seq_len = segment_ids.shape[1]
    local_width = proj_copy.shape[2]
    heads_here = local_width // HEAD_DIM
    score_scale = HEAD_DIM ** (-0.5)
    projected = jnp.einsum(
        "tc,scn->stn", tokens_in, proj_copy, preferred_element_type=jnp.float32
    ).astype(jnp.bfloat16)
    heads_split = projected.reshape(3, rows_here, seq_len, heads_here, HEAD_DIM)

    def masked_scores(query_rows, key_rows, row_segments):
        scores = (
            jnp.einsum("qhd,khd->hqk", query_rows, key_rows, preferred_element_type=jnp.float32)
            * score_scale
        )
        same_doc = row_segments[:, None] == row_segments[None, :]
        return jnp.where(same_doc[None], scores, NEG_FILL)

    def row_forward(packed):
        query_rows, key_rows, value_rows, row_segments = packed
        scores = masked_scores(query_rows, key_rows, row_segments)
        row_max = jnp.max(scores, axis=-1, keepdims=True)
        row_exp = jnp.exp(scores - row_max)
        row_total = jnp.sum(row_exp, axis=-1, keepdims=True)
        row_probs = (row_exp / row_total).astype(jnp.bfloat16)
        mixed = jnp.einsum(
            "hqk,khd->qhd", row_probs, value_rows, preferred_element_type=jnp.float32
        )
        row_lse = (row_max + jnp.log(row_total))[..., 0]
        return (mixed.astype(jnp.bfloat16).reshape(seq_len, local_width), row_lse)

    context_rows, lse_rows = lax.map(
        row_forward, (heads_split[0], heads_split[1], heads_split[2], segment_ids)
    )
    context = context_rows.reshape(rows_here * seq_len, local_width)
    attn_part = jnp.einsum("tn,dn->td", context, out_copy, preferred_element_type=jnp.float32)
    attn_share = lax.psum_scatter(
        attn_part.astype(jnp.bfloat16), "mp", scatter_dimension=0, tiled=True
    ).astype(jnp.float32)
    share_rows = attn_share.shape[0]
    share_start = lax.axis_index("mp") * share_rows
    token_share = lax.dynamic_slice_in_dim(tokens_in, share_start, share_rows, 0).astype(
        jnp.float32
    )
    hidden_one, norm_one_back = jax.vjp(
        layer_norm, token_share + attn_share, norm_full[0], norm_full[1]
    )
    hidden_low = lax.all_gather(hidden_one.astype(jnp.bfloat16), "mp", axis=0, tiled=True)
    pre_act = jnp.dot(hidden_low, up_copy, preferred_element_type=jnp.float32)
    act_full, gelu_back = jax.vjp(exact_gelu, pre_act)
    act_low = act_full.astype(jnp.bfloat16)
    ffn_part = jnp.einsum("tf,df->td", act_low, down_copy, preferred_element_type=jnp.float32)
    ffn_share = lax.psum_scatter(
        ffn_part.astype(jnp.bfloat16), "mp", scatter_dimension=0, tiled=True
    ).astype(jnp.float32)
    result, norm_two_back = jax.vjp(layer_norm, hidden_one + ffn_share, norm_full[2], norm_full[3])
    layer_out = result.astype(jnp.bfloat16)
    regathered = (
        lax.all_gather(project_weight.astype(jnp.bfloat16), "dp", axis=1, tiled=True),
        lax.all_gather(output_weight.astype(jnp.bfloat16), "dp", axis=0, tiled=True),
        lax.all_gather(up_weight.astype(jnp.bfloat16), "dp", axis=0, tiled=True),
        lax.all_gather(down_weight.astype(jnp.bfloat16), "dp", axis=0, tiled=True),
    )
    proj_copy, out_copy, up_copy, down_copy = regathered
    d_resid_two, d_gain_two, d_shift_two = norm_two_back(cotangent.astype(jnp.float32))
    d_ffn = lax.all_gather(d_resid_two.astype(jnp.bfloat16), "mp", axis=0, tiled=True)
    down_grad = jnp.einsum("td,tf->df", d_ffn, act_low, preferred_element_type=jnp.float32)
    d_act = jnp.dot(d_ffn, down_copy, preferred_element_type=jnp.float32)
    d_pre = gelu_back(d_act)[0].astype(jnp.bfloat16)
    up_grad = jnp.einsum("tc,tf->cf", hidden_low, d_pre, preferred_element_type=jnp.float32)
    d_hidden_part = jnp.einsum("tf,cf->tc", d_pre, up_copy, preferred_element_type=jnp.float32)
    d_hidden = d_resid_two + lax.psum_scatter(
        d_hidden_part.astype(jnp.bfloat16), "mp", scatter_dimension=0, tiled=True
    ).astype(jnp.float32)
    d_resid_one, d_gain_one, d_shift_one = norm_one_back(d_hidden)
    d_attn = lax.all_gather(d_resid_one.astype(jnp.bfloat16), "mp", axis=0, tiled=True)
    output_grad = jnp.einsum("td,tn->dn", d_attn, context, preferred_element_type=jnp.float32)
    d_context = jnp.dot(d_attn, out_copy, preferred_element_type=jnp.float32).astype(jnp.bfloat16)

    def row_backward(packed):
        query_rows, key_rows, value_rows, row_segments, row_lse, row_grad = packed
        scores = masked_scores(query_rows, key_rows, row_segments)
        row_probs = jnp.exp(scores - row_lse[..., None])
        grad_heads = row_grad.reshape(seq_len, heads_here, HEAD_DIM)
        d_probs = jnp.einsum(
            "qhd,khd->hqk", grad_heads, value_rows, preferred_element_type=jnp.float32
        )
        row_inner = jnp.sum(d_probs * row_probs, axis=-1, keepdims=True)
        d_scores = (row_probs * (d_probs - row_inner)).astype(jnp.bfloat16)
        d_value = jnp.einsum(
            "hqk,qhd->khd",
            row_probs.astype(jnp.bfloat16),
            grad_heads,
            preferred_element_type=jnp.float32,
        )
        d_query = (
            jnp.einsum("hqk,khd->qhd", d_scores, key_rows, preferred_element_type=jnp.float32)
            * score_scale
        )
        d_key = (
            jnp.einsum("hqk,qhd->khd", d_scores, query_rows, preferred_element_type=jnp.float32)
            * score_scale
        )
        return (
            d_query.astype(jnp.bfloat16).reshape(seq_len, local_width),
            d_key.astype(jnp.bfloat16).reshape(seq_len, local_width),
            d_value.astype(jnp.bfloat16).reshape(seq_len, local_width),
        )

    grad_context_rows = d_context.reshape(rows_here, seq_len, local_width)
    d_rows = lax.map(
        row_backward,
        (heads_split[0], heads_split[1], heads_split[2], segment_ids, lse_rows, grad_context_rows),
    )
    d_proj = jnp.stack(d_rows).reshape(3, rows_here * seq_len, local_width)
    project_grad = jnp.einsum("tc,stn->scn", tokens_in, d_proj, preferred_element_type=jnp.float32)
    d_input_part = jnp.einsum("stn,scn->tc", d_proj, proj_copy, preferred_element_type=jnp.float32)
    input_grad = d_resid_one + lax.psum_scatter(
        d_input_part.astype(jnp.bfloat16), "mp", scatter_dimension=0, tiled=True
    ).astype(jnp.float32)
    norm_local = jnp.stack([d_gain_one, d_shift_one, d_gain_two, d_shift_two])
    norm_red = lax.psum_scatter(norm_local, ("dp", "mp"), scatter_dimension=1, tiled=True)
    proj_red, out_red, up_red, down_red = (
        lax.psum_scatter(
            project_grad.astype(jnp.bfloat16), "dp", scatter_dimension=1, tiled=True
        ).astype(jnp.float32),
        lax.psum_scatter(
            output_grad.astype(jnp.bfloat16), "dp", scatter_dimension=0, tiled=True
        ).astype(jnp.float32),
        lax.psum_scatter(
            up_grad.astype(jnp.bfloat16), "dp", scatter_dimension=0, tiled=True
        ).astype(jnp.float32),
        lax.psum_scatter(
            down_grad.astype(jnp.bfloat16), "dp", scatter_dimension=0, tiled=True
        ).astype(jnp.float32),
    )
    proj_new = adam_step(proj_red, project_weight, project_momentum, project_squares, D ** (-0.5))
    out_new = adam_step(out_red, output_weight, output_momentum, output_squares, 4.0 * D ** (-0.5))
    up_new = adam_step(up_red, up_weight, up_momentum, up_squares, D ** (-0.5))
    down_new = adam_step(down_red, down_weight, down_momentum, down_squares, FF ** (-0.5))
    norm_new = adam_step(norm_red, norm_params, norm_momentum, norm_squares, 0.3)
    return (
        layer_out,
        input_grad,
        proj_new[0],
        proj_new[1],
        proj_new[2],
        proj_new[3],
        out_new[0],
        out_new[1],
        out_new[2],
        out_new[3],
        up_new[0],
        up_new[1],
        up_new[2],
        up_new[3],
        down_new[0],
        down_new[1],
        down_new[2],
        down_new[3],
        norm_new[0],
        norm_new[1],
        norm_new[2],
        norm_new[3],
    )


MESH = pl.DeviceIdType.MESH
BF16 = jnp.bfloat16
F32 = jnp.float32
ANY = pl.BlockSpec(memory_space=pl.ANY)
VMEM = pl.BlockSpec(memory_space=pltpu.VMEM)
DMA = pltpu.SemaphoreType.DMA

HOP_X, HOP_Y, HOP_C, OWN = (0, 1, 0, 0), (0, 0, 0, 1), (0, 0, 1, 0), (0, 0, 0, 0)


def hop_z(mask):
    return (mask, 0, 0, 0)


def position():
    dp = lax.axis_index("dp")
    return (dp // 4, (dp // 2) % 2, dp % 2, lax.axis_index("mp"))


def moved(me, hop):
    return tuple(m ^ h if h else m for m, h in zip(me, hop))


def device_at(me, hop):
    z, x, c, y = moved(me, hop)
    return (z * 4 + x * 2 + c, y)


def entry_barrier(me, nz):
    barrier = pltpu.get_barrier_semaphore()
    hops = [HOP_X, HOP_Y, HOP_C] + [hop_z(a) for a in range(1, nz)]
    for hop in hops:
        pl.semaphore_signal(barrier, inc=1, device_id=device_at(me, hop), device_id_type=MESH)
    pl.semaphore_wait(barrier, len(hops))


def view_rows(ref, pos):
    z, x, c, y = pos
    half = ref.shape[4] // 2
    return ref.at[z, x, c, :, pl.ds(pl.multiple_of(y * half, half), half)]


class Gather:
    def __init__(self, me, nz, out, view, send_sem, recv_sem, base):
        self.me, self.nz, self.out, self.view = me, nz, out, view
        self.send_sem, self.recv_sem, self.base = send_sem, recv_sem, base
        self.sent = []

    def slot(self, rel):
        a, b, d, e = rel
        return self.base + ((a * 2 + b) * 2 + d) * 2 + e

    def piece(self, rel):
        return self.view(self.out, moved(self.me, rel))

    def copy(self, rel, hop):
        arrives = self.slot(tuple(r ^ h for r, h in zip(rel, hop)))
        return pltpu.make_async_remote_copy(
            src_ref=self.piece(rel),
            dst_ref=self.piece(rel),
            send_sem=self.send_sem.at[arrives],
            recv_sem=self.recv_sem.at[arrives],
            device_id=device_at(self.me, hop),
            device_id_type=MESH,
        )

    def send(self, rel, *hops):
        for hop in hops:
            self.copy(rel, hop).start()
            self.sent.append((rel, hop))

    def wait(self, rel):
        self.copy(tuple(r ^ h for r, h in zip(rel, HOP_C)), HOP_C).wait_recv()

    def first_square(self):
        self.send(OWN, HOP_X, HOP_Y, HOP_C)

    def first_column(self, *levels):
        self.send(OWN, *[hop_z(a) for a in levels])

    def level(self, a):
        self.wait(hop_z(a))
        self.send(hop_z(a), HOP_X, HOP_Y, HOP_C)

    def square(self, a):
        self.wait((a, 1, 0, 0))
        if a % 4 == 0:
            self.send((a, 1, 0, 0), HOP_Y)
        self.wait((a, 0, 0, 1))
        if a % 4 == 2:
            self.send((a, 0, 0, 1), HOP_X)
        self.send((a, 1, 0, 0), HOP_C)
        self.send((a, 0, 0, 1), HOP_C)

    def diagonal(self, a):
        self.wait((a, 1, 0, 1))
        if a % 2 == 0:
            self.send((a, 1, 0, 1), hop_z(1))
        self.send((a, 1, 0, 1), HOP_C)

    def whole(self, a):
        for b in range(2):
            for e in range(2):
                self.wait((a, b, 1, e))

    def drain(self):
        for rel, hop in self.sent:
            self.copy(rel, hop).wait_send()


def sum_hops(nz):
    hops, mask = [HOP_C, HOP_X, HOP_Y], 1
    while mask < nz:
        hops.append(hop_z(mask))
        mask *= 2
    return hops


class SmallSum:
    def __init__(self, me, nz, parts, came, send_sem, recv_sem):
        self.me, self.hops, self.parts, self.came = me, sum_hops(nz), parts, came
        self.send_sem, self.recv_sem = send_sem, recv_sem

    def copy(self, i):
        return pltpu.make_async_remote_copy(
            src_ref=self.parts.at[i],
            dst_ref=self.came.at[i],
            send_sem=self.send_sem.at[i],
            recv_sem=self.recv_sem.at[i],
            device_id=device_at(self.me, self.hops[i]),
            device_id_type=MESH,
        )

    def start(self, i):
        self.copy(i).start()

    def finish(self, i):
        self.copy(i).wait()
        self.parts[i + 1] = self.parts[i] + self.came[i]


LOG2_E = 1.4426950408889634
PDF_SCALE = 0.3989422804014327


def gelu_pair(u):
    phi = 0.5 + 0.5 * lax.erf(u * 0.5**0.5)
    bell = jnp.exp2(u * u * (-0.5 * LOG2_E))
    return u * phi, phi + u * PDF_SCALE * bell


def dot_nn(a, b):
    return jnp.dot(a, b, preferred_element_type=F32)


def dot_nt(a, b):
    return lax.dot_general(a, b, (((1,), (1,)), ((), ())), preferred_element_type=F32)


def normed(rows):
    center = rows - jnp.mean(rows, axis=-1, keepdims=True)
    scale = lax.rsqrt(jnp.mean(center * center, axis=-1, keepdims=True) + EPS_NORM)
    return center * scale, scale


def norm_backward(grad, n, scale):
    inner = jnp.mean(grad * n, axis=-1, keepdims=True)
    return scale * (grad - jnp.mean(grad, axis=-1, keepdims=True) - n * inner)


def at_slots(i, plan):
    for k in sorted(plan):
        @pl.when(i == k)
        def _(k=k):
            for call in plan[k]:
                call()


def phase(count, parts, plan):
    def step(i, carry):
        for k, part in enumerate(parts):
            at_slots(i, {slot // len(parts): plan[slot] for slot in plan if slot % len(parts) == k})
            part(i)
        return carry

    lax.fori_loop(0, count, step, 0)


ACTORS = "qkvoud"
METHODS = (
    "first_square", "first_column", "level", "square", "diagonal", "whole",
    "exchange", "fetch", "join", "bend", "column",
)


def script_plans(script, actors):
    plans = {}
    for place, slots in script:
        for slot, numbers in slots:
            calls = plans.setdefault(place, {}).setdefault(slot, [])
            for number in numbers:
                actor = actors[ACTORS[number // 1000]]
                method, level = METHODS[number // 10 % 100], number % 10
                if method == "fetch":
                    actor.take_side(level)
                calls.append(functools.partial(getattr(actor, method), *(() if method == "first_square" else (level,))))
    return plans


def run_calls(plans, name):
    for call in plans.get(name, {}).get(-1, []):
        call()


def forward_kernel(nz, tokens, cotangent, seg_col, seg_row, proj, out, up, down, norm,
                   proj_all, out_all, up_all, down_all, norm_all, qkv_out, ctx_out, lse,
                   resid_out, hidden_out, act_out, slope_out, layer_out, dres_out, dffn_out, dnorm,
                   tok, cot, w_small, w_up, w_down, qkv, ctx, bias, res, hidden, act, pre, slope,
                   send_sem, recv_sem, parts, came, sum_send, sum_recv, io_sem):
    me = position()
    t_here, seq = tok.shape[0], seg_row.shape[2]
    rows_here, pairs = t_here // seq, D // 128
    copies = {}

    def begin(key, src, dst, sem):
        copies[key] = pltpu.make_async_copy(src, dst, io_sem.at[sem])
        copies[key].start()

    mine = pl.ds(pl.multiple_of(me[3] * t_here, t_here), t_here)
    begin("tok", tokens.at[mine, :], tok, 0)
    begin("cot", cotangent, cot, 1)
    parts[0] = norm[...]
    fulls = [w_small.at[i] for i in range(4)] + [w_up, w_down]
    owns = [proj.at[i] for i in range(3)] + [out, up, down]
    gathers = {
        name: Gather(me, nz, fulls[i], view_rows, send_sem, recv_sem, 8 * nz * i) for i, name in enumerate("qkvoud")
    }
    for g, own in zip(gathers.values(), owns):
        g.piece(OWN)[...] = own[...].astype(BF16)
    entry_barrier(me, nz)
    small = SmallSum(me, nz, parts, came, sum_send, sum_recv)
    plans = script_plans(FORWARD_SCRIPT, gathers)
    run_calls(plans, "start")
    small.start(0)
    for i in range(len(small.hops)):
        calls = plans.setdefault("attn", {}).setdefault(2 * i, [])
        calls.append(functools.partial(small.finish, i))
        if i + 1 < len(small.hops):
            calls.append(functools.partial(small.start, i + 1))

    def bias_step(r):
        rows = pl.ds(pl.multiple_of(r * seq, seq), seq)
        same = seg_col[rows, 0:1] == seg_row[r]
        bias[r] = jnp.where(same, 0.0, NEG_FILL)

    phase(rows_here, [bias_step], {})
    copies["tok"].wait()
    n_q, n_a, n_o, n_u = D // 256, rows_here * pairs, t_here // 256, FF // 256
    for s, name in enumerate("qkv"):
        run_calls(plans, name)

        def project_step(j, s=s):
            col = pl.ds(pl.multiple_of(j * 256, 256), 256)
            qkv[s, :, col] = dot_nn(tok[...], w_small[s, :, :, :, :, col].reshape(D, 256)).astype(BF16)

        phase(n_q, [project_step], plans.get(name + "m", {}))
    begin("proj", w_small.at[pl.ds(0, 3)], proj_all, 2)
    begin("qkv", qkv, qkv_out, 3)
    head_of = lax.broadcasted_iota(jnp.int32, (seq, 128), 1) // HEAD_DIM
    ones = jnp.ones((16, seq), BF16)

    def attend_step(u):
        r, p = u // pairs, u % pairs
        col = pl.ds(pl.multiple_of(p * 128, 128), 128)
        whole = pl.ds(pl.multiple_of(r * seq, seq), seq)
        keys, values = qkv[1, whole, col], qkv[2, whole, col].T
        keys = [jnp.where(head_of == h, keys, jnp.zeros_like(keys)) for h in range(2)]
        values = [jnp.concatenate([values[h * HEAD_DIM : (h + 1) * HEAD_DIM], ones]) for h in range(2)]
        blocks = [(low, h) for low in range(0, seq, 256) for h in range(2)]

        def score(low, h):
            q = qkv[0, pl.ds(pl.multiple_of(r * seq + low, 256), 256), col] * jnp.asarray(HEAD_DIM**-0.5, BF16)
            return dot_nt(keys[h], q) + bias[r, :, low : low + 256]

        waiting, mixed = [score(*blocks[0])], []
        for n, (low, h) in enumerate(blocks):
            if n + 1 < len(blocks):
                waiting.append(score(*blocks[n + 1]))
            scores = waiting.pop(0)
            top = jnp.max(scores, axis=0, keepdims=True)
            weights = jnp.exp(scores - top).astype(BF16)
            sums = dot_nn(values[h], weights)
            total = sums[HEAD_DIM : HEAD_DIM + 1]
            mixed.append(sums[:HEAD_DIM] * (1.0 / total))
            lse[u, h : h + 1, low : low + 256] = top + jnp.log(total)
        for n, low in enumerate(range(0, seq, 256)):
            rows = pl.ds(pl.multiple_of(r * seq + low, 256), 256)
            ctx[rows, col] = jnp.concatenate(mixed[2 * n : 2 * n + 2]).T.astype(BF16)

    phase(n_a, [attend_step], plans["attn"])
    run_calls(plans, "o")
    norm_all[...] = parts[len(small.hops)]
    begin("out", w_small.at[3], out_all, 4)
    begin("ctx", ctx, ctx_out, 5)

    def out_step(m):
        rows = pl.ds(pl.multiple_of(m * 256, 256), 256)
        attended = dot_nt(ctx[rows, :], w_small[3].reshape(D, D))
        total = tok[rows, :].astype(F32) + attended
        res[rows, :] = total
        unit, _ = normed(total)
        hidden[rows, :] = (unit * norm_all[0:1, :] + norm_all[1:2, :]).astype(BF16)

    phase(n_o, [out_step], plans.get("out", {}))
    begin("res", res, resid_out, 6)
    begin("hidden", hidden, hidden_out, 7)
    run_calls(plans, "u")
    begin("up", w_up, up_all, 8)

    n_half = 2 * FF // 256
    rows_half = t_here // 2

    def half_of(i):
        col = pl.ds(pl.multiple_of((i // 2) * 256, 256), 256)
        rows = pl.ds(pl.multiple_of((i % 2) * rows_half, rows_half), rows_half)
        return rows, col

    def up_dot(i, dst):
        rows, col = half_of(i)
        dst[...] = dot_nn(hidden[rows, :], w_up[:, :, :, :, col].reshape(D, 256))

    def up_act(i, src):
        rows, col = half_of(i)
        for k in range(0, rows_half, 64):
            part = pl.ds(pl.multiple_of((i % 2) * rows_half + k, 64), 64)
            value, tangent = gelu_pair(src[k : k + 64, :])
            act[part, col] = value.astype(BF16)
            slope[(i // 2) % 2, part, :] = tangent.astype(BF16)

    def slope_copy(j):
        col = pl.ds(pl.multiple_of(j * 256, 256), 256)
        return pltpu.make_async_copy(slope.at[j % 2], slope_out.at[:, col], io_sem.at[9 + j % 2])

    up_dot(0, pre.at[0])

    def up_step(j):
        @pl.when(j >= 2)
        def _():
            slope_copy(j - 2).wait()

        up_dot(2 * j + 1, pre.at[1])
        up_act(2 * j, pre.at[0])

    def up_next(j):
        up_dot((2 * j + 2) % n_half, pre.at[0])
        up_act(2 * j + 1, pre.at[1])
        slope_copy(j).start()

    phase(n_u, [up_step, up_next], plans.get("up", {}))
    begin("act", act, act_out, 11)
    for j in (n_u - 2, n_u - 1):
        slope_copy(j).wait()
    for key in ("cot", "res", "hidden"):
        copies[key].wait()
    dnorm[...] = jnp.zeros_like(dnorm)

    def hidden_step(m):
        rows = pl.ds(pl.multiple_of(m * 128, 128), 128)
        unit, _ = normed(res[rows, :])
        res[rows, :] = unit * norm_all[0:1, :] + norm_all[1:2, :]

    phase(t_here // 128, [hidden_step], {})
    for a in DOWN_LEVELS:
        run_calls(plans, "d%d" % a)
        level = me[0] ^ a
        width = D // nz
        col = pl.ds(pl.multiple_of(level * width, width), width)

        def down_step(m):
            rows = pl.ds(pl.multiple_of(m * 512, 512), 512)
            res[rows, col] += dot_nt(act[rows, :], w_down[level].reshape(width, FF))

        phase(t_here // 512, [down_step], {})
    begin("down", w_down, down_all, 12)

    def norm_step(m):
        rows = pl.ds(pl.multiple_of(m * 128, 128), 128)
        unit, scale = normed(res[rows, :])
        tok[rows, :] = (unit * norm_all[2:3, :] + norm_all[3:4, :]).astype(BF16)
        grad = cot[rows, :].astype(F32)
        dnorm[0:1, :] = dnorm[0:1, :] + jnp.sum(grad * unit, axis=0, keepdims=True)
        dnorm[1:2, :] = dnorm[1:2, :] + jnp.sum(grad, axis=0, keepdims=True)
        dres = norm_backward(grad * norm_all[2:3, :], unit, scale)
        res[rows, :] = dres
        hidden[rows, :] = dres.astype(BF16)

    phase(t_here // 128, [norm_step], {})
    begin("layer", tok, layer_out, 13)
    begin("dres", res, dres_out, 14)
    begin("dffn", hidden, dffn_out, 15)
    for g in gathers.values():
        g.drain()
    for key in ("proj", "out", "up", "down", "qkv", "ctx", "act", "layer", "dres", "dffn"):
        copies[key].wait()


FORWARD_SCRIPT = (
    ("start", (
        (-1, (12, 11, 1000, 0, 1013, 1012, 13, 3011, 3000, 2000, 3012,)),
    )),
    ("q", (
        (-1, (30, 2012, 22, 21, 2011, 4011, 1023, 2030, 1022, 3021, 1011, 4012, 32, 3022, 2022, 1030, 2021,
            2040, 3032, 4000, 1032, 40, 42, 23, 1040, 3013, 3030, 2013, 2032, 3042, 52, 41, 1021, 1042, 4030,
            31, 1033, 3040, 3052, 3023, 1041, 2023, 33, 3043, 43, 1031, 1043, 2042, 4022, 2050, 4013, 5011,
            1052, 5000, 4021, 53, 2041, 1051, 3041, 3031, 1053, 2031, 50, 3050, 2052, 51,)),
    )),
    ("qm", (
        (0, (1050,)),
        (3, (2043,)),
    )),
    ("k", (
        (-1, ()),
    )),
    ("km", (
        (1, (3051, 3033, 2051,)),
        (2, (2033, 5012,)),
    )),
    ("v", (
        (-1, (3053, 5013, 4040, 2053,)),
    )),
    ("attn", (
        (1, (4032,)),
        (5, (5030,)),
        (10, (4041, 4042, 4023,)),
        (13, (5022, 5021, 5040,)),
    )),
    ("o", (
        (-1, ()),
    )),
    ("out", (
        (0, (5050, 4031, 4052,)),
        (1, (4033, 4043,)),
    )),
    ("u", (
        (-1, (5041, 4050, 4053, 4051,)),
    )),
    ("up", (
        (1, (5032, 5023,)),
        (17, (5042, 5031,)),
        (26, (5033,)),
        (29, (5043, 5052, 5051,)),
    )),
    ("d0", (
        (-1, ()),
    )),
    ("d1", (
        (-1, ()),
    )),
    ("d2", (
        (-1, ()),
    )),
    ("d3", (
        (-1, (5053,)),
    )),
)
DOWN_LEVELS = (0, 1, 2, 3)


def run_forward(nz, tokens_in, cotangent, segments, proj, out, up, down, norm):
    t_here = cotangent.shape[0]
    rows_here, seq = segments.shape
    n_sum = len(sum_hops(nz))
    rows = D // (4 * nz)
    full = lambda cols: jax.ShapeDtypeStruct((nz, 2, 2, rows, cols), BF16)
    flat = lambda cols, kind: jax.ShapeDtypeStruct((t_here, cols), kind)
    seg_col = jnp.broadcast_to(segments.reshape(t_here, 1), (t_here, 128))
    seg_row = segments.reshape(rows_here, 1, seq)
    return pl.pallas_call(
        functools.partial(forward_kernel, nz),
        out_shape=[
            jax.ShapeDtypeStruct((3, nz, 2, 2, rows, D), BF16),
            full(D),
            full(FF),
            full(FF),
            jax.ShapeDtypeStruct(norm.shape, F32),
            jax.ShapeDtypeStruct((3, t_here, D), BF16),
            flat(D, BF16),
            jax.ShapeDtypeStruct((rows_here * (D // 128), 8, seq), F32),
            flat(D, F32),
            flat(D, BF16),
            flat(FF, BF16),
            flat(FF, BF16),
            flat(D, BF16),
            flat(D, F32),
            flat(D, BF16),
            jax.ShapeDtypeStruct((8, D), F32),
        ],
        in_specs=[ANY, ANY] + [VMEM] * 7,
        out_specs=[ANY] * 4 + [VMEM, ANY, ANY, VMEM] + [ANY] * 7 + [VMEM],
        scratch_shapes=[
            pltpu.VMEM((t_here, D), BF16),
            pltpu.VMEM((t_here, D), BF16),
            pltpu.VMEM((4, nz, 2, 2, rows, D), BF16),
            pltpu.VMEM((nz, 2, 2, rows, FF), BF16),
            pltpu.VMEM((nz, 2, 2, rows, FF), BF16),
            pltpu.VMEM((3, t_here, D), BF16),
            pltpu.VMEM((t_here, D), BF16),
            pltpu.VMEM((rows_here, seq, seq), F32),
            pltpu.VMEM((t_here, D), F32),
            pltpu.VMEM((t_here, D), BF16),
            pltpu.VMEM((t_here, FF), BF16),
            pltpu.VMEM((2, t_here // 2, 256), F32),
            pltpu.VMEM((2, t_here, 256), BF16),
            DMA((48 * nz,)),
            DMA((48 * nz,)),
            pltpu.VMEM((n_sum + 1,) + norm.shape, F32),
            pltpu.VMEM((n_sum,) + norm.shape, F32),
            DMA((n_sum,)),
            DMA((n_sum,)),
            DMA((16,)),
        ],
        compiler_params=pltpu.CompilerParams(
            collective_id=0, has_side_effects=True, vmem_limit_bytes=62 << 20
        ),
        name="forward",
    )(tokens_in, cotangent, seg_col, seg_row, proj, out, up, down, norm)


def view_flat(ref, pos):
    z, x, c, y = pos
    rows, half = 64, ref.shape[1] // 2
    row = (z * 4 + x * 2 + c) * rows
    return ref.at[pl.ds(pl.multiple_of(row, rows), rows), pl.ds(pl.multiple_of(y * half, half), half)]


def add_rows(dst, terms, rows=16):
    def body(i, carry):
        block = pl.ds(pl.multiple_of(i * rows, rows), rows)
        total = terms[0][block, :].astype(F32)
        for term in terms[1:]:
            total = total + term[block, :].astype(F32)
        dst[block, :] = total.astype(dst.dtype)
        return carry

    lax.fori_loop(0, dst.shape[0] // rows, body, 0)


def add_pair(dst, other, rows=16):
    def body(i, carry):
        block = pl.ds(pl.multiple_of(i * rows, rows), rows)
        dst[block, :] = dst[block, :] + other[block, :]
        return carry

    lax.fori_loop(0, dst.shape[0] // rows, body, 0)


class Scatter:
    def __init__(self, me, nz, index, grad, from_c, cut, held, swap, came, result, sems, counter, before=()):
        self.me, self.nz, self.index, self.grad, self.from_c = me, nz, index, grad, from_c
        self.cut, self.held, self.swap, self.came, self.result = cut, held, swap, came, result
        self.load_sem, self.send_sem, self.recv_sem = sems
        self.counter, self.side, self.before = counter, {}, before

    def where(self, a, b, e):
        return (a * 2 + b) * 2 + e

    def part(self, ref, i):
        return ref.at[i, :, pl.ds(*self.cut)]

    def remote(self, src, dst, slot, hop):
        sem = self.index * 8 * self.nz + slot
        return pltpu.make_async_remote_copy(
            src_ref=src, dst_ref=dst, send_sem=self.send_sem.at[sem], recv_sem=self.recv_sem.at[sem],
            device_id=device_at(self.me, hop), device_id_type=MESH,
        )

    def core_copy(self, a, b, e):
        i = self.where(a, b, e)
        return self.remote(view_flat(self.grad, moved(self.me, (a, b, 1, e))), self.from_c.at[i], i, HOP_C)

    def hop_copy(self, kind, a):
        b, e = {"w": (1, 1), "d": (1, 1), "x": (1, 0), "y": (0, 1), "z": (0, 0)}[kind]
        hop = {"w": hop_z(1), "d": HOP_Y if a % 4 == 0 else HOP_X, "x": HOP_X, "y": HOP_Y, "z": hop_z(a)}[kind]
        slot = {"w": a // 2, "d": self.nz // 2 + a // 2, "x": self.nz + a, "y": 2 * self.nz + a, "z": 3 * self.nz + a}[kind]
        return self.remote(
            self.part(self.held, self.where(a, b, e)), self.part(self.came, slot), 4 * self.nz + slot, hop
        )

    def took(self, kind, a):
        copy = self.hop_copy(kind, a)
        copy.wait_recv()
        return copy.dst_ref

    def mine(self, a, b, e):
        return self.part(self.held, self.where(a, b, e))

    def pairs(self, a):
        return [(self.where(a, b, e), b * 2 + e, (a, b, 0, e)) for b in range(2) for e in range(2)]

    def loads(self, a):
        out, side = [], self.side[a]
        for i, k, rel in self.pairs(a):
            out.append(pltpu.make_async_copy(
                view_flat(self.grad, moved(self.me, rel)), self.part(self.held, i), self.load_sem.at[side * 8 + k]
            ))
            out.append(pltpu.make_async_copy(
                self.from_c.at[i], self.part(self.swap, side * 4 + k), self.load_sem.at[side * 8 + 4 + k]
            ))
        return out

    def exchange(self, a):
        for b, e in ((1, 1), (1, 0), (0, 1), (0, 0)):
            self.core_copy(a, b, e).start()

    def take_side(self, a):
        self.side[a] = len(self.counter) % 2
        self.counter.append(a)

    def fetch(self, a):
        for other in self.before:
            other.release(a)
        for b, e in ((1, 1), (1, 0), (0, 1), (0, 0)):
            self.core_copy(a, b, e).wait_recv()
        for load in self.loads(a):
            load.start()

    def join(self, a):
        for load in self.loads(a):
            load.wait()
        for i, k, _ in self.pairs(a):
            add_pair(self.part(self.held, i), self.part(self.swap, self.side[a] * 4 + k))
        if a % 2:
            self.hop_copy("w", a).start()
        if a % 4 != 0:
            self.hop_copy("x", a).start()
        if a % 4 != 2:
            self.hop_copy("y", a).start()

    def bend(self, a):
        add_pair(self.mine(a, 1, 1), self.took("w", a))
        self.hop_copy("d", a).start()

    def square(self, a):
        kind, b, e = ("x", 1, 0) if a % 4 == 0 else ("y", 0, 1)
        add_pair(self.mine(a, b, e), self.took("d", a))
        self.hop_copy(kind, a).start()

    def column(self, a):
        terms = [self.mine(a, 0, 0), self.took("x", a), self.took("y", a)]
        if a:
            add_rows(terms[0], terms)
            self.hop_copy("z", a).start()
        else:
            add_rows(self.result, terms + [self.took("z", k) for k in range(1, self.nz)])

    def release(self, a):
        for b in range(2):
            for e in range(2):
                self.core_copy(a, b, e).wait_send()
        for kind in ("w", "x", "y", "z") if a % 2 else ("d", "x", "y", "z") if a else ("d", "x", "y"):
            self.hop_copy(kind, a).wait_send()


def transpose_into(dst, src):
    def body(i, carry):
        block = pl.ds(pl.multiple_of(i * 128, 128), 128)
        dst[:, block] = src[block, :].T
        return carry

    lax.fori_loop(0, src.shape[0] // 128, body, 0)


def backward_kernel(nz, tokens, seg_col, seg_row, proj, out, up, down, norm, qkv_in, ctx_in, lse,
                    resid, hidden, act, slope, dres, dffn, dnorm_two,
                    input_grad, *refs):
    red, norm_sum, grads, swaps, refs = refs[:6], refs[6], refs[7:13], refs[13:19], refs[19:]
    down_grad, up_grad, out_grad = grads[:3]
    (tiles, buf_a, buf_b, buf_c, total, dpre, stage, ctx, w_out, bias, dqkv, resid_tile, dq,
     held, swap, came_down, came_up, came_mix,
     load_sem, send_sem, recv_sem, io_sem, parts, came, sum_send, sum_recv) = refs
    me = position()
    t_here, seq = total.shape[0], seg_row.shape[2]
    rows_here, pairs = t_here // seq, D // 128
    n_ff = FF // 512
    copies = {}

    def begin(key, src, dst, sem):
        copies[key] = pltpu.make_async_copy(src, dst, io_sem.at[sem])
        copies[key].start()

    def col512(j):
        return pl.ds(pl.multiple_of(j * 512, 512), 512)

    def tile_copy(src, j, base, sem):
        return pltpu.make_async_copy(src.at[:, col512(j)], tiles.at[base + j % 2], io_sem.at[sem + j % 2])

    def stage_copy(dst, col, slot):
        return pltpu.make_async_copy(stage.at[slot], dst.at[:, col], io_sem.at[8 + slot])

    def put_stage(i, value, dst, col):
        slot = i % 2

        @pl.when(i >= 2)
        def _():
            stage_copy(dst, col, slot).wait()

        stage[slot] = value.astype(BF16)
        stage_copy(dst, col, slot).start()

    def flush_stage(dst):
        for slot in range(2):
            stage_copy(dst, pl.ds(0, 512), slot).wait()

    begin("dffn", dffn, buf_a, 10)
    begin("hidden", hidden, ctx, 11)
    begin("dres", dres, total, 12)
    tile_copy(act, 0, 0, 0).start()
    entry_barrier(me, nz)
    sems = (load_sem, send_sem, recv_sem)
    counter = []
    half = D // 2
    cuts = [(0, FF // 2)] * 2 + [(i * half, half) for i in (3, 0, 1, 2)]
    arrivals = (came_down, came_up) + (came_mix,) * 4
    scatters = {}
    for i, name in enumerate("duoqkv"):
        before = {"u": "d", "o": "u"}.get(name)
        scatters[name] = Scatter(
            me, nz, i, grads[i], swaps[i], cuts[i], held, swap, arrivals[i], red[i], sems, counter,
            [scatters[before]] if before else [],
        )
    small = SmallSum(me, nz, parts, came, sum_send, sum_recv)
    n_small = len(small.hops)
    n_attn, n_m = rows_here * pairs, t_here // 256
    plans = script_plans(BACKWARD_SCRIPT, scatters)
    for i in range(n_small):
        calls = plans.setdefault("attn", {}).setdefault(2 * i + 1, [])
        calls.append(functools.partial(small.finish, i))
        if i + 1 < n_small:
            calls.append(functools.partial(small.start, i + 1))

    copies["dffn"].wait()
    transpose_into(buf_b, buf_a)

    def down_step(j):
        @pl.when(j + 1 < n_ff)
        def _():
            tile_copy(act, j + 1, 0, 0).start()

        tile_copy(act, j, 0, 0).wait()
        put_stage(j, dot_nn(buf_b[...], tiles[j % 2]), down_grad, col512(j))

    phase(n_ff, [down_step], {})
    for src, base in ((down, 2), (slope, 4), (up, 6)):
        tile_copy(src, 0, base, base).start()
    copies["hidden"].wait()
    transpose_into(buf_c, ctx)
    begin("ctx", ctx_in, ctx, 11)
    begin("w_out", out, w_out, 13)
    flush_stage(down_grad)
    copies["dres"].wait()

    def pre_step(j):
        @pl.when(j + 1 < n_ff)
        def _():
            for src, base in ((down, 2), (slope, 4), (up, 6)):
                tile_copy(src, j + 1, base, base).start()

        for src, base in ((down, 2), (slope, 4), (up, 6)):
            tile_copy(src, j, base, base).wait()
        dpre[...] = (dot_nn(buf_a[...], tiles[2 + j % 2]) * tiles[4 + j % 2].astype(F32)).astype(BF16)

    def up_grad_step(j):
        put_stage(j, dot_nn(buf_c[...], dpre[...]), up_grad, col512(j))

    def hidden_step(j):
        total[...] += dot_nt(dpre[...], tiles[6 + j % 2])

    phase(n_ff, [pre_step, up_grad_step, hidden_step], plans.get("ffn", {}))
    flush_stage(up_grad)
    for i in range(6):
        begin(("qkv", i), qkv_in.at[i // 2, :, pl.ds((i % 2) * 512, 512)], tiles.at[i], i)
    norm_sum[...] = jnp.zeros_like(norm_sum)

    def resid_copy(m):
        rows = pl.ds(pl.multiple_of(m * 256, 256), 256)
        return pltpu.make_async_copy(resid.at[rows, :], resid_tile.at[m % 2], io_sem.at[14 + m % 2])

    resid_copy(0).start()

    def norm_step(m):
        @pl.when(m + 1 < n_m)
        def _():
            resid_copy(m + 1).start()

        resid_copy(m).wait()
        rows = pl.ds(pl.multiple_of(m * 256, 256), 256)
        unit, scale = normed(resid_tile[m % 2])
        grad = total[rows, :]
        norm_sum[0:1, :] = norm_sum[0:1, :] + jnp.sum(grad * unit, axis=0, keepdims=True)
        norm_sum[1:2, :] = norm_sum[1:2, :] + jnp.sum(grad, axis=0, keepdims=True)
        moved_grad = norm_backward(grad * norm[0:1, :], unit, scale)
        total[rows, :] = moved_grad
        buf_b[rows, :] = moved_grad.astype(BF16)

    phase(n_m, [norm_step], plans.get("ln", {}))
    norm_sum[2:4, :] = dnorm_two[0:2, :]
    parts[0] = norm_sum[...]
    small.start(0)
    transpose_into(buf_a, buf_b)
    copies["ctx"].wait()
    copies["w_out"].wait()

    def out_grad_step(j):
        put_stage(j, dot_nn(buf_a[...], ctx[:, col512(j)]), out_grad, col512(j))

    phase(2, [out_grad_step], plans.get("out", {}))
    flush_stage(out_grad)

    def ctx_step(j):
        buf_a[:, col512(j)] = dot_nn(buf_b[...], w_out[:, col512(j)]).astype(BF16)

    phase(2, [ctx_step], plans.get("ctx", {}))
    mine = pl.ds(pl.multiple_of(me[3] * t_here, t_here), t_here)
    begin("tok", tokens.at[mine, :], buf_b, 10)

    def bias_step(r):
        rows = pl.ds(pl.multiple_of(r * seq, seq), seq)
        bias[r] = jnp.where(seg_col[rows, 0:1] == seg_row[r], 0.0, NEG_FILL)

    phase(rows_here, [bias_step], {})
    for i in range(6):
        copies[("qkv", i)].wait()
    head_of = lax.broadcasted_iota(jnp.int32, (128, 128), 1) // HEAD_DIM
    head_pick = (
        lax.broadcasted_iota(jnp.int32, (8, 128), 1) // HEAD_DIM == lax.broadcasted_iota(jnp.int32, (8, 128), 0)
    ).astype(BF16)
    shrink = jnp.asarray(HEAD_DIM**-0.5, BF16)

    def per_head(block):
        return jnp.concatenate([jnp.where(head_of == h, block, jnp.zeros_like(block)) for h in range(2)])

    def attend_step(u):
        r, p = u // pairs, u % pairs
        side = p // 4
        col = pl.ds(pl.multiple_of(p * 128, 128), 128)
        near = pl.ds(pl.multiple_of((p % 4) * 128, 128), 128)
        whole = pl.ds(pl.multiple_of(r * seq, seq), seq)
        product = buf_a[whole, col].astype(F32) * ctx[whole, col].astype(F32)
        coarse = product.astype(BF16)
        fine = (product - coarse.astype(F32)).astype(BF16)
        delta = dot_nt(head_pick, coarse) + dot_nt(head_pick, fine)
        dq[...] = jnp.zeros_like(dq)
        n_blocks = seq // 128

        def block_of(kb):
            low, high = max(0, kb - 2) * 128, min(n_blocks, kb + 3) * 128
            k_rows = pl.ds(pl.multiple_of(r * seq + kb * 128, 128), 128)
            q_rows = pl.ds(pl.multiple_of(r * seq + low, 128), high - low)
            return low, high, k_rows, q_rows

        def products(kb):
            low, high, k_rows, q_rows = block_of(kb)
            q = tiles[side, q_rows, near] * shrink
            keys = per_head(tiles[2 + side, k_rows, near])
            return keys, q, dot_nt(keys, q), dot_nt(per_head(tiles[4 + side, k_rows, near]), buf_a[q_rows, col])

        waiting = [products(0)]
        for kb in range(n_blocks):
            if kb + 1 < n_blocks:
                waiting.append(products(kb + 1))
            keys, q, scores, d_probs = waiting.pop(0)
            low, high, k_rows, q_rows = block_of(kb)
            block = bias[r, kb * 128 : kb * 128 + 128, low:high]
            probs, d_scores = [], []
            for h in range(2):
                part = slice(h * 128, h * 128 + 128)
                prob = jnp.exp(scores[part] + block - lse[u, h : h + 1, low:high])
                probs.append(prob.astype(BF16))
                d_scores.append((prob * (d_probs[part] - delta[h : h + 1, low:high])).astype(BF16))
            probs, d_scores = jnp.concatenate(probs), jnp.concatenate(d_scores)
            d_value = dot_nn(probs, buf_a[q_rows, col])
            d_key = dot_nn(d_scores, q)
            dqkv[4 + side, k_rows, near] = jnp.where(head_of == 0, d_value[:128], d_value[128:]).astype(BF16)
            dqkv[2 + side, k_rows, near] = jnp.where(head_of == 0, d_key[:128], d_key[128:]).astype(BF16)
            dq[:, low:high] += dot_nn(keys.T, d_scores)
        dqkv[side, whole, near] = (dq[...].T * HEAD_DIM**-0.5).astype(BF16)

    phase(n_attn, [attend_step], plans["attn"])
    for i in range(6):
        begin(("proj", i), proj.at[i // 2, :, pl.ds((i % 2) * 512, 512)], tiles.at[i], i)
    copies["tok"].wait()
    transpose_into(buf_c, buf_b)

    for s, name in enumerate("qkv"):

        def project_step(i, s=s):
            put_stage(i, dot_nn(buf_c[...], dqkv[2 * s + i]), grads[3 + s], col512(i))

        phase(2, [project_step], plans.get("p" + name, {}))
        flush_stage(grads[3 + s])
    for i in range(6):
        copies[("proj", i)].wait()
    def in_copy(m):
        rows = pl.ds(pl.multiple_of(m * 256, 256), 256)
        return pltpu.make_async_copy(total.at[rows, :], input_grad.at[rows, :], io_sem.at[16 + m])

    def input_step(m):
        rows = pl.ds(pl.multiple_of(m * 256, 256), 256)
        value = total[rows, :]
        for i in range(6):
            value = value + dot_nt(dqkv[i, rows, :], tiles[i])
        total[rows, :] = value

    phase(n_m, [input_step], plans.get("in", {}))
    for m in range(n_m):
        in_copy(m).start()
    run_calls(plans, "end")
    for name in "oqkv":
        for a in range(nz):
            scatters[name].release(a)
    for m in range(n_m):
        in_copy(m).wait()
    norm_sum[...] = parts[n_small]


BACKWARD_SCRIPT = (
    ("ffn", (
        (0, (5062, 5061, 5060,)),
        (4, (5072, 5063,)),
        (6, (5082, 5071,)),
        (7, (5070,)),
        (8, (5081,)),
        (9, (5080, 5073,)),
        (11, (5083,)),
        (13, (5090,)),
        (14, (5101,)),
        (17, (5092,)),
        (21, (5103,)),
        (23, (5032,)),
    )),
    ("ln", (
        (1, (5030, 4063, 4061,)),
    )),
    ("out", (
        (1, (4073, 4062, 4060, 5102,)),
    )),
    ("ctx", (
        (1, (3063, 3060, 3061, 4071, 4083, 3062,)),
    )),
    ("attn", (
        (0, (4072, 4081,)),
        (4, (5100, 4082, 4103, 3073, 4070, 4092,)),
        (5, (3083,)),
        (6, (4080, 4101, 3071,)),
        (7, (3081,)),
        (8, (4090,)),
        (12, (4032,)),
    )),
    ("pq", (
        (0, (4030, 3103,)),
    )),
    ("pk", (
        (0, (4102, 3101, 3072, 63, 61, 62, 60,)),
        (1, (3082, 3092,)),
    )),
    ("pv", (
        (0, (73, 72, 1061, 1063, 1060, 1062, 83, 82, 71,)),
        (1, (3032, 81, 1073, 1071,)),
    )),
    ("in", (
        (0, (103, 4100, 92, 1083, 3102, 3070, 1081, 70, 2063, 101, 3080, 3090, 1072, 80, 90, 1070, 2061, 32,
            1082, 2073, 1080, 2062, 1103, 1092, 2060, 2083,)),
        (1, (3030, 2072, 2071,)),
        (2, (30, 1032, 1090, 2082, 1101, 2092, 3100, 102, 2081, 2070,)),
        (3, (2080, 2103,)),
    )),
    ("end", (
        (-1, (100, 1030, 2032, 2101, 1102, 2090, 2102, 2030, 1100, 2100,)),
    )),
)


def run_backward(nz, tokens_in, segments, proj, out, up, down, norm, qkv, ctx, lse,
                 resid, hidden, act, slope, dres, dffn, dnorm_two):
    t_here = dffn.shape[0]
    rows_here, seq = segments.shape
    n_sum = len(sum_hops(nz))
    piece = (64, FF // 2)
    seg_col = jnp.broadcast_to(segments.reshape(t_here, 1), (t_here, 128))
    seg_row = segments.reshape(rows_here, 1, seq)
    widths = (FF // 2,) * 2 + (D // 2,) * 4
    reduced = [jax.ShapeDtypeStruct((64, w), F32) for w in widths]
    grads = [jax.ShapeDtypeStruct((D, 2 * w), BF16) for w in widths]
    swapped = [jax.ShapeDtypeStruct((4 * nz, 64, w), BF16) for w in widths]
    results = pl.pallas_call(
        functools.partial(backward_kernel, nz),
        out_shape=[jax.ShapeDtypeStruct((t_here, D), F32)] + reduced + [jax.ShapeDtypeStruct(norm.shape, F32)]
        + grads + swapped,
        in_specs=[ANY, VMEM, VMEM] + [ANY] * 4 + [VMEM, ANY, ANY, VMEM] + [ANY] * 6 + [VMEM],
        out_specs=[ANY] + [VMEM] * 7 + [ANY] * 12,
        scratch_shapes=[
            pltpu.VMEM((8, t_here, 512), BF16),
            pltpu.VMEM((t_here, D), BF16),
            pltpu.VMEM((t_here, D), BF16),
            pltpu.VMEM((t_here, D), BF16),
            pltpu.VMEM((t_here, D), F32),
            pltpu.VMEM((t_here, 512), BF16),
            pltpu.VMEM((2, t_here, 512), BF16),
            pltpu.VMEM((t_here, D), BF16),
            pltpu.VMEM((D, D), BF16),
            pltpu.VMEM((rows_here, seq, seq), F32),
            pltpu.VMEM((6, t_here, 512), BF16),
            pltpu.VMEM((2, 256, D), F32),
            pltpu.VMEM((128, seq), F32),
            pltpu.VMEM((4 * nz,) + piece, BF16),
            pltpu.VMEM((8,) + piece, BF16),
            pltpu.VMEM((4 * nz,) + piece, BF16),
            pltpu.VMEM((4 * nz,) + piece, BF16),
            pltpu.VMEM((4 * nz,) + piece, BF16),
            DMA((16,)),
            DMA((48 * nz,)),
            DMA((48 * nz,)),
            DMA((20,)),
            pltpu.VMEM((n_sum + 1,) + norm.shape, F32),
            pltpu.VMEM((n_sum,) + norm.shape, F32),
            DMA((n_sum,)),
            DMA((n_sum,)),
        ],
        compiler_params=pltpu.CompilerParams(
            collective_id=1, has_side_effects=True, vmem_limit_bytes=62 << 20
        ),
        name="backward",
    )(tokens_in, seg_col, seg_row, proj, out, up, down, norm, qkv, ctx, lse,
      resid, hidden, act, slope, dres, dffn, dnorm_two)
    return results[:8]


def local_rows(
    tokens_in,
    cotangent,
    segment_ids,
    project_weight,
    project_momentum,
    project_squares,
    output_weight,
    output_momentum,
    output_squares,
    up_weight,
    up_momentum,
    up_squares,
    down_weight,
    down_momentum,
    down_squares,
    norm_params,
    norm_momentum,
    norm_squares,
):
    nz = lax.axis_size("dp") // 4
    dp, mp = lax.axis_index("dp"), lax.axis_index("mp")
    norm_cols = norm_params.shape[1]
    norm_start = (dp * 2 + mp) * norm_cols
    norm_wide = lax.dynamic_update_slice(
        jnp.zeros((8, D), F32), norm_params.astype(BF16).astype(F32), (0, norm_start)
    )
    rows_here = segment_ids.shape[0] // 2
    segments = lax.dynamic_slice_in_dim(segment_ids, mp * rows_here, rows_here, 0)
    (proj_w, out_w, up_w, down_w, norm_full, qkv, context, lse, resid_one, hidden_low, act_low, slope,
     layer_out, d_resid_two, d_ffn, d_norm_two) = run_forward(
        nz,
        tokens_in,
        cotangent,
        segments,
        project_weight,
        output_weight,
        up_weight,
        down_weight,
        norm_wide,
    )
    input_grad, down_red, up_red, out_red, *proj_red, norm_sum = run_backward(
        nz,
        tokens_in,
        segments,
        proj_w.reshape(3, D, D),
        out_w.reshape(D, D),
        up_w.reshape(D, FF),
        down_w.reshape(D, FF),
        norm_full,
        qkv,
        context,
        lse,
        resid_one,
        hidden_low,
        act_low,
        slope,
        d_resid_two,
        d_ffn,
        d_norm_two,
    )
    proj_red = jnp.stack(proj_red)
    norm_red = lax.dynamic_slice(norm_sum, (0, norm_start), (4, norm_cols))
    return (
        layer_out,
        input_grad,
        *adam_step(proj_red, project_weight, project_momentum, project_squares, D ** (-0.5)),
        *adam_step(out_red, output_weight, output_momentum, output_squares, 4.0 * D ** (-0.5)),
        *adam_step(up_red, up_weight, up_momentum, up_squares, D ** (-0.5)),
        *adam_step(down_red, down_weight, down_momentum, down_squares, FF ** (-0.5)),
        *adam_step(norm_red, norm_params, norm_momentum, norm_squares, 0.3),
    )


def by_rows(mesh):
    dp, mp = mesh.shape["dp"], mesh.shape["mp"]
    return mp == 2 and dp >= 8 and dp & (dp - 1) == 0 and D % (64 * dp) == 0


def solution(mesh):
    body = local_rows if by_rows(mesh) else local_plain
    return jax.shard_map(
        body,
        mesh=mesh,
        in_specs=(
            P("dp", None),
            P(("dp", "mp"), None),
            P("dp", None),
            P(None, "dp", "mp"),
            P(None, "dp", "mp"),
            P(None, "dp", "mp"),
            P("dp", "mp"),
            P("dp", "mp"),
            P("dp", "mp"),
            P("dp", "mp"),
            P("dp", "mp"),
            P("dp", "mp"),
            P("dp", "mp"),
            P("dp", "mp"),
            P("dp", "mp"),
            P(None, ("dp", "mp")),
            P(None, ("dp", "mp")),
            P(None, ("dp", "mp")),
        ),
        out_specs=(
            P(("dp", "mp"), None),
            P(("dp", "mp"), None),
            P(None, "dp", "mp"),
            P(None, "dp", "mp"),
            P(None, "dp", "mp"),
            P(None, "dp", "mp"),
            P("dp", "mp"),
            P("dp", "mp"),
            P("dp", "mp"),
            P("dp", "mp"),
            P("dp", "mp"),
            P("dp", "mp"),
            P("dp", "mp"),
            P("dp", "mp"),
            P("dp", "mp"),
            P("dp", "mp"),
            P("dp", "mp"),
            P("dp", "mp"),
            P(None, ("dp", "mp")),
            P(None, ("dp", "mp")),
            P(None, ("dp", "mp")),
            P(None, ("dp", "mp")),
        ),
        check_vma=False,
    )
```

```python
import functools

import jax
import jax.numpy as jnp
from jax import lax
from jax.experimental import pallas as pl
from jax.experimental.pallas import tpu as pltpu
from jax.sharding import PartitionSpec as P

D = 1024
HEAD_DIM = 64
FF = 4096
STEP = 3


EPS_NORM = 1e-12
NEG_FILL = -1e30
BETA_ONE = 0.5
BETA_TWO = 0.5
ADAM_EPS = 1e-08
DECAY_RATE = 0.01


def layer_norm(values, norm_gain, norm_shift):
    center = values - jnp.mean(values, axis=-1, keepdims=True)
    spread = jnp.mean(center * center, axis=-1, keepdims=True)
    return center * lax.rsqrt(spread + EPS_NORM) * norm_gain + norm_shift


def exact_gelu(values):
    return jax.nn.gelu(values, approximate=False)


def adam_step(gradient, weight, first_old, second, step_rate):
    correct_one = 1.0 - BETA_ONE**STEP
    correct_two = 1.0 - BETA_TWO**STEP
    moment = BETA_ONE * first_old + (1.0 - BETA_ONE) * gradient
    square = BETA_TWO * second + (1.0 - BETA_TWO) * gradient * gradient
    normed = moment / correct_one / (jnp.sqrt(square / correct_two) + ADAM_EPS)
    updated = weight - step_rate * (normed + DECAY_RATE * weight)
    return (gradient, moment, square, updated)


def local_plain(
    tokens_in,
    cotangent,
    segment_ids,
    project_weight,
    project_momentum,
    project_squares,
    output_weight,
    output_momentum,
    output_squares,
    up_weight,
    up_momentum,
    up_squares,
    down_weight,
    down_momentum,
    down_squares,
    norm_params,
    norm_momentum,
    norm_squares,
):
    gathered = (
        lax.all_gather(project_weight.astype(jnp.bfloat16), "dp", axis=1, tiled=True),
        lax.all_gather(output_weight.astype(jnp.bfloat16), "dp", axis=0, tiled=True),
        lax.all_gather(up_weight.astype(jnp.bfloat16), "dp", axis=0, tiled=True),
        lax.all_gather(down_weight.astype(jnp.bfloat16), "dp", axis=0, tiled=True),
    )
    proj_copy, out_copy, up_copy, down_copy = gathered
    norm_full = lax.all_gather(
        norm_params.astype(jnp.bfloat16), ("dp", "mp"), axis=1, tiled=True
    ).astype(jnp.float32)
    rows_here = segment_ids.shape[0]
    seq_len = segment_ids.shape[1]
    local_width = proj_copy.shape[2]
    heads_here = local_width // HEAD_DIM
    score_scale = HEAD_DIM ** (-0.5)
    projected = jnp.einsum(
        "tc,scn->stn", tokens_in, proj_copy, preferred_element_type=jnp.float32
    ).astype(jnp.bfloat16)
    heads_split = projected.reshape(3, rows_here, seq_len, heads_here, HEAD_DIM)

    def masked_scores(query_rows, key_rows, row_segments):
        scores = (
            jnp.einsum("qhd,khd->hqk", query_rows, key_rows, preferred_element_type=jnp.float32)
            * score_scale
        )
        same_doc = row_segments[:, None] == row_segments[None, :]
        return jnp.where(same_doc[None], scores, NEG_FILL)

    def row_forward(packed):
        query_rows, key_rows, value_rows, row_segments = packed
        scores = masked_scores(query_rows, key_rows, row_segments)
        row_max = jnp.max(scores, axis=-1, keepdims=True)
        row_exp = jnp.exp(scores - row_max)
        row_total = jnp.sum(row_exp, axis=-1, keepdims=True)
        row_probs = (row_exp / row_total).astype(jnp.bfloat16)
        mixed = jnp.einsum(
            "hqk,khd->qhd", row_probs, value_rows, preferred_element_type=jnp.float32
        )
        row_lse = (row_max + jnp.log(row_total))[..., 0]
        return (mixed.astype(jnp.bfloat16).reshape(seq_len, local_width), row_lse)

    context_rows, lse_rows = lax.map(
        row_forward, (heads_split[0], heads_split[1], heads_split[2], segment_ids)
    )
    context = context_rows.reshape(rows_here * seq_len, local_width)
    attn_part = jnp.einsum("tn,dn->td", context, out_copy, preferred_element_type=jnp.float32)
    attn_share = lax.psum_scatter(
        attn_part.astype(jnp.bfloat16), "mp", scatter_dimension=0, tiled=True
    ).astype(jnp.float32)
    share_rows = attn_share.shape[0]
    share_start = lax.axis_index("mp") * share_rows
    token_share = lax.dynamic_slice_in_dim(tokens_in, share_start, share_rows, 0).astype(
        jnp.float32
    )
    hidden_one, norm_one_back = jax.vjp(
        layer_norm, token_share + attn_share, norm_full[0], norm_full[1]
    )
    hidden_low = lax.all_gather(hidden_one.astype(jnp.bfloat16), "mp", axis=0, tiled=True)
    pre_act = jnp.dot(hidden_low, up_copy, preferred_element_type=jnp.float32)
    act_full, gelu_back = jax.vjp(exact_gelu, pre_act)
    act_low = act_full.astype(jnp.bfloat16)
    ffn_part = jnp.einsum("tf,df->td", act_low, down_copy, preferred_element_type=jnp.float32)
    ffn_share = lax.psum_scatter(
        ffn_part.astype(jnp.bfloat16), "mp", scatter_dimension=0, tiled=True
    ).astype(jnp.float32)
    result, norm_two_back = jax.vjp(layer_norm, hidden_one + ffn_share, norm_full[2], norm_full[3])
    layer_out = result.astype(jnp.bfloat16)
    regathered = (
        lax.all_gather(project_weight.astype(jnp.bfloat16), "dp", axis=1, tiled=True),
        lax.all_gather(output_weight.astype(jnp.bfloat16), "dp", axis=0, tiled=True),
        lax.all_gather(up_weight.astype(jnp.bfloat16), "dp", axis=0, tiled=True),
        lax.all_gather(down_weight.astype(jnp.bfloat16), "dp", axis=0, tiled=True),
    )
    proj_copy, out_copy, up_copy, down_copy = regathered
    d_resid_two, d_gain_two, d_shift_two = norm_two_back(cotangent.astype(jnp.float32))
    d_ffn = lax.all_gather(d_resid_two.astype(jnp.bfloat16), "mp", axis=0, tiled=True)
    down_grad = jnp.einsum("td,tf->df", d_ffn, act_low, preferred_element_type=jnp.float32)
    d_act = jnp.dot(d_ffn, down_copy, preferred_element_type=jnp.float32)
    d_pre = gelu_back(d_act)[0].astype(jnp.bfloat16)
    up_grad = jnp.einsum("tc,tf->cf", hidden_low, d_pre, preferred_element_type=jnp.float32)
    d_hidden_part = jnp.einsum("tf,cf->tc", d_pre, up_copy, preferred_element_type=jnp.float32)
    d_hidden = d_resid_two + lax.psum_scatter(
        d_hidden_part.astype(jnp.bfloat16), "mp", scatter_dimension=0, tiled=True
    ).astype(jnp.float32)
    d_resid_one, d_gain_one, d_shift_one = norm_one_back(d_hidden)
    d_attn = lax.all_gather(d_resid_one.astype(jnp.bfloat16), "mp", axis=0, tiled=True)
    output_grad = jnp.einsum("td,tn->dn", d_attn, context, preferred_element_type=jnp.float32)
    d_context = jnp.dot(d_attn, out_copy, preferred_element_type=jnp.float32).astype(jnp.bfloat16)

    def row_backward(packed):
        query_rows, key_rows, value_rows, row_segments, row_lse, row_grad = packed
        scores = masked_scores(query_rows, key_rows, row_segments)
        row_probs = jnp.exp(scores - row_lse[..., None])
        grad_heads = row_grad.reshape(seq_len, heads_here, HEAD_DIM)
        d_probs = jnp.einsum(
            "qhd,khd->hqk", grad_heads, value_rows, preferred_element_type=jnp.float32
        )
        row_inner = jnp.sum(d_probs * row_probs, axis=-1, keepdims=True)
        d_scores = (row_probs * (d_probs - row_inner)).astype(jnp.bfloat16)
        d_value = jnp.einsum(
            "hqk,qhd->khd",
            row_probs.astype(jnp.bfloat16),
            grad_heads,
            preferred_element_type=jnp.float32,
        )
        d_query = (
            jnp.einsum("hqk,khd->qhd", d_scores, key_rows, preferred_element_type=jnp.float32)
            * score_scale
        )
        d_key = (
            jnp.einsum("hqk,qhd->khd", d_scores, query_rows, preferred_element_type=jnp.float32)
            * score_scale
        )
        return (
            d_query.astype(jnp.bfloat16).reshape(seq_len, local_width),
            d_key.astype(jnp.bfloat16).reshape(seq_len, local_width),
            d_value.astype(jnp.bfloat16).reshape(seq_len, local_width),
        )

    grad_context_rows = d_context.reshape(rows_here, seq_len, local_width)
    d_rows = lax.map(
        row_backward,
        (heads_split[0], heads_split[1], heads_split[2], segment_ids, lse_rows, grad_context_rows),
    )
    d_proj = jnp.stack(d_rows).reshape(3, rows_here * seq_len, local_width)
    project_grad = jnp.einsum("tc,stn->scn", tokens_in, d_proj, preferred_element_type=jnp.float32)
    d_input_part = jnp.einsum("stn,scn->tc", d_proj, proj_copy, preferred_element_type=jnp.float32)
    input_grad = d_resid_one + lax.psum_scatter(
        d_input_part.astype(jnp.bfloat16), "mp", scatter_dimension=0, tiled=True
    ).astype(jnp.float32)
    norm_local = jnp.stack([d_gain_one, d_shift_one, d_gain_two, d_shift_two])
    norm_red = lax.psum_scatter(norm_local, ("dp", "mp"), scatter_dimension=1, tiled=True)
    proj_red, out_red, up_red, down_red = (
        lax.psum_scatter(
            project_grad.astype(jnp.bfloat16), "dp", scatter_dimension=1, tiled=True
        ).astype(jnp.float32),
        lax.psum_scatter(
            output_grad.astype(jnp.bfloat16), "dp", scatter_dimension=0, tiled=True
        ).astype(jnp.float32),
        lax.psum_scatter(
            up_grad.astype(jnp.bfloat16), "dp", scatter_dimension=0, tiled=True
        ).astype(jnp.float32),
        lax.psum_scatter(
            down_grad.astype(jnp.bfloat16), "dp", scatter_dimension=0, tiled=True
        ).astype(jnp.float32),
    )
    proj_new = adam_step(proj_red, project_weight, project_momentum, project_squares, D ** (-0.5))
    out_new = adam_step(out_red, output_weight, output_momentum, output_squares, 4.0 * D ** (-0.5))
    up_new = adam_step(up_red, up_weight, up_momentum, up_squares, D ** (-0.5))
    down_new = adam_step(down_red, down_weight, down_momentum, down_squares, FF ** (-0.5))
    norm_new = adam_step(norm_red, norm_params, norm_momentum, norm_squares, 0.3)
    return (
        layer_out,
        input_grad,
        proj_new[0],
        proj_new[1],
        proj_new[2],
        proj_new[3],
        out_new[0],
        out_new[1],
        out_new[2],
        out_new[3],
        up_new[0],
        up_new[1],
        up_new[2],
        up_new[3],
        down_new[0],
        down_new[1],
        down_new[2],
        down_new[3],
        norm_new[0],
        norm_new[1],
        norm_new[2],
        norm_new[3],
    )


MESH = pl.DeviceIdType.MESH
BF16 = jnp.bfloat16
F32 = jnp.float32
ANY = pl.BlockSpec(memory_space=pl.ANY)
VMEM = pl.BlockSpec(memory_space=pltpu.VMEM)
DMA = pltpu.SemaphoreType.DMA

HOP_X, HOP_Y, HOP_C, OWN = (0, 1, 0, 0), (0, 0, 0, 1), (0, 0, 1, 0), (0, 0, 0, 0)


def hop_z(mask):
    return (mask, 0, 0, 0)


def position():
    dp = lax.axis_index("dp")
    return (dp // 4, (dp // 2) % 2, dp % 2, lax.axis_index("mp"))


def moved(me, hop):
    return tuple(m ^ h if h else m for m, h in zip(me, hop))


def device_at(me, hop):
    z, x, c, y = moved(me, hop)
    return (z * 4 + x * 2 + c, y)


def entry_barrier(me, nz):
    barrier = pltpu.get_barrier_semaphore()
    hops = [HOP_X, HOP_Y, HOP_C] + [hop_z(a) for a in range(1, nz)]
    for hop in hops:
        pl.semaphore_signal(barrier, inc=1, device_id=device_at(me, hop), device_id_type=MESH)
    pl.semaphore_wait(barrier, len(hops))


def view_rows(ref, pos):
    z, x, c, y = pos
    half = ref.shape[4] // 2
    return ref.at[z, x, c, :, pl.ds(pl.multiple_of(y * half, half), half)]


class Gather:
    def __init__(self, me, nz, out, view, send_sem, recv_sem, base):
        self.me, self.nz, self.out, self.view = me, nz, out, view
        self.send_sem, self.recv_sem, self.base = send_sem, recv_sem, base
        self.sent = []

    def slot(self, rel):
        a, b, d, e = rel
        return self.base + ((a * 2 + b) * 2 + d) * 2 + e

    def piece(self, rel):
        return self.view(self.out, moved(self.me, rel))

    def copy(self, rel, hop):
        arrives = self.slot(tuple(r ^ h for r, h in zip(rel, hop)))
        return pltpu.make_async_remote_copy(
            src_ref=self.piece(rel),
            dst_ref=self.piece(rel),
            send_sem=self.send_sem.at[arrives],
            recv_sem=self.recv_sem.at[arrives],
            device_id=device_at(self.me, hop),
            device_id_type=MESH,
        )

    def send(self, rel, *hops):
        for hop in hops:
            self.copy(rel, hop).start()
            self.sent.append((rel, hop))

    def wait(self, rel):
        self.copy(tuple(r ^ h for r, h in zip(rel, HOP_C)), HOP_C).wait_recv()

    def first_square(self):
        self.send(OWN, HOP_X, HOP_Y, HOP_C)

    def first_column(self, *levels):
        self.send(OWN, *[hop_z(a) for a in levels])

    def level(self, a):
        self.wait(hop_z(a))
        self.send(hop_z(a), HOP_X, HOP_Y, HOP_C)

    def square(self, a):
        self.wait((a, 1, 0, 0))
        if a % 4 == 0:
            self.send((a, 1, 0, 0), HOP_Y)
        self.wait((a, 0, 0, 1))
        if a % 4 == 2:
            self.send((a, 0, 0, 1), HOP_X)
        self.send((a, 1, 0, 0), HOP_C)
        self.send((a, 0, 0, 1), HOP_C)

    def diagonal(self, a):
        self.wait((a, 1, 0, 1))
        if a % 2 == 0:
            self.send((a, 1, 0, 1), hop_z(1))
        self.send((a, 1, 0, 1), HOP_C)

    def whole(self, a):
        for b in range(2):
            for e in range(2):
                self.wait((a, b, 1, e))

    def drain(self):
        for rel, hop in self.sent:
            self.copy(rel, hop).wait_send()


def sum_hops(nz):
    hops, mask = [HOP_C, HOP_X, HOP_Y], 1
    while mask < nz:
        hops.append(hop_z(mask))
        mask *= 2
    return hops


class SmallSum:
    def __init__(self, me, nz, parts, came, send_sem, recv_sem):
        self.me, self.hops, self.parts, self.came = me, sum_hops(nz), parts, came
        self.send_sem, self.recv_sem = send_sem, recv_sem

    def copy(self, i):
        return pltpu.make_async_remote_copy(
            src_ref=self.parts.at[i],
            dst_ref=self.came.at[i],
            send_sem=self.send_sem.at[i],
            recv_sem=self.recv_sem.at[i],
            device_id=device_at(self.me, self.hops[i]),
            device_id_type=MESH,
        )

    def start(self, i):
        self.copy(i).start()

    def finish(self, i):
        self.copy(i).wait()
        self.parts[i + 1] = self.parts[i] + self.came[i]


LOG2_E = 1.4426950408889634
PDF_SCALE = 0.3989422804014327


def gelu_pair(u):
    phi = 0.5 + 0.5 * lax.erf(u * 0.5**0.5)
    bell = jnp.exp2(u * u * (-0.5 * LOG2_E))
    return u * phi, phi + u * PDF_SCALE * bell


def dot_nn(a, b):
    return jnp.dot(a, b, preferred_element_type=F32)


def dot_nt(a, b):
    return lax.dot_general(a, b, (((1,), (1,)), ((), ())), preferred_element_type=F32)


def normed(rows):
    center = rows - jnp.mean(rows, axis=-1, keepdims=True)
    scale = lax.rsqrt(jnp.mean(center * center, axis=-1, keepdims=True) + EPS_NORM)
    return center * scale, scale


def norm_backward(grad, n, scale):
    inner = jnp.mean(grad * n, axis=-1, keepdims=True)
    return scale * (grad - jnp.mean(grad, axis=-1, keepdims=True) - n * inner)


def at_slots(i, plan):
    for k in sorted(plan):
        @pl.when(i == k)
        def _(k=k):
            for call in plan[k]:
                call()


def phase(count, parts, plan):
    def step(i, carry):
        for k, part in enumerate(parts):
            at_slots(i, {slot // len(parts): plan[slot] for slot in plan if slot % len(parts) == k})
            part(i)
        return carry

    lax.fori_loop(0, count, step, 0)


ACTORS = "qkvoud"
METHODS = (
    "first_square", "first_column", "level", "square", "diagonal", "whole",
    "exchange", "fetch", "join", "bend", "column",
)


def script_plans(script, actors):
    plans = {}
    for place, slots in script:
        for slot, numbers in slots:
            calls = plans.setdefault(place, {}).setdefault(slot, [])
            for number in numbers:
                actor = actors[ACTORS[number // 1000]]
                method, level = METHODS[number // 10 % 100], number % 10
                if method == "fetch":
                    actor.take_side(level)
                calls.append(functools.partial(getattr(actor, method), *(() if method == "first_square" else (level,))))
    return plans


def run_calls(plans, name):
    for call in plans.get(name, {}).get(-1, []):
        call()


def forward_kernel(nz, tokens, cotangent, seg_col, seg_row, proj, out, up, down, norm,
                   proj_all, out_all, up_all, down_all, norm_all, qkv_out, ctx_out, lse,
                   resid_out, hidden_out, act_out, slope_out, layer_out, dres_out, dffn_out, dnorm,
                   tok, cot, w_small, w_up, w_down, qkv, ctx, bias, res, hidden, act, pre, slope,
                   send_sem, recv_sem, parts, came, sum_send, sum_recv, io_sem):
    me = position()
    t_here, seq = tok.shape[0], seg_row.shape[2]
    rows_here, pairs = t_here // seq, D // 128
    copies = {}

    def begin(key, src, dst, sem):
        copies[key] = pltpu.make_async_copy(src, dst, io_sem.at[sem])
        copies[key].start()

    mine = pl.ds(pl.multiple_of(me[3] * t_here, t_here), t_here)
    begin("tok", tokens.at[mine, :], tok, 0)
    begin("cot", cotangent, cot, 1)
    parts[0] = norm[...]
    fulls = [w_small.at[i] for i in range(4)] + [w_up, w_down]
    owns = [proj.at[i] for i in range(3)] + [out, up, down]
    gathers = {
        name: Gather(me, nz, fulls[i], view_rows, send_sem, recv_sem, 8 * nz * i) for i, name in enumerate("qkvoud")
    }
    for g, own in zip(gathers.values(), owns):
        g.piece(OWN)[...] = own[...].astype(BF16)
    entry_barrier(me, nz)
    small = SmallSum(me, nz, parts, came, sum_send, sum_recv)
    plans = script_plans(FORWARD_SCRIPT, gathers)
    run_calls(plans, "start")
    small.start(0)
    for i in range(len(small.hops)):
        calls = plans.setdefault("attn", {}).setdefault(2 * i, [])
        calls.append(functools.partial(small.finish, i))
        if i + 1 < len(small.hops):
            calls.append(functools.partial(small.start, i + 1))

    def bias_step(r):
        rows = pl.ds(pl.multiple_of(r * seq, seq), seq)
        same = seg_col[rows, 0:1] == seg_row[r]
        bias[r] = jnp.where(same, 0.0, NEG_FILL)

    phase(rows_here, [bias_step], {})
    copies["tok"].wait()
    n_q, n_a, n_o, n_u = D // 256, rows_here * pairs, t_here // 256, FF // 256
    for s, name in enumerate("qkv"):
        run_calls(plans, name)

        def project_step(j, s=s):
            col = pl.ds(pl.multiple_of(j * 256, 256), 256)
            qkv[s, :, col] = dot_nn(tok[...], w_small[s, :, :, :, :, col].reshape(D, 256)).astype(BF16)

        phase(n_q, [project_step], plans.get(name + "m", {}))
    begin("proj", w_small.at[pl.ds(0, 3)], proj_all, 2)
    begin("qkv", qkv, qkv_out, 3)
    head_of = lax.broadcasted_iota(jnp.int32, (seq, 128), 1) // HEAD_DIM
    ones = jnp.ones((16, seq), BF16)

    def attend_step(u):
        r, p = u // pairs, u % pairs
        col = pl.ds(pl.multiple_of(p * 128, 128), 128)
        whole = pl.ds(pl.multiple_of(r * seq, seq), seq)
        keys, values = qkv[1, whole, col], qkv[2, whole, col].T
        keys = [jnp.where(head_of == h, keys, jnp.zeros_like(keys)) for h in range(2)]
        values = [jnp.concatenate([values[h * HEAD_DIM : (h + 1) * HEAD_DIM], ones]) for h in range(2)]
        blocks = [(low, h) for low in range(0, seq, 256) for h in range(2)]

        def score(low, h):
            q = qkv[0, pl.ds(pl.multiple_of(r * seq + low, 256), 256), col] * jnp.asarray(HEAD_DIM**-0.5, BF16)
            return dot_nt(keys[h], q) + bias[r, :, low : low + 256]

        waiting, mixed = [score(*blocks[0])], []
        for n, (low, h) in enumerate(blocks):
            if n + 1 < len(blocks):
                waiting.append(score(*blocks[n + 1]))
            scores = waiting.pop(0)
            top = jnp.max(scores, axis=0, keepdims=True)
            weights = jnp.exp(scores - top).astype(BF16)
            sums = dot_nn(values[h], weights)
            total = sums[HEAD_DIM : HEAD_DIM + 1]
            mixed.append(sums[:HEAD_DIM] * (1.0 / total))
            lse[u, h : h + 1, low : low + 256] = top + jnp.log(total)
        for n, low in enumerate(range(0, seq, 256)):
            rows = pl.ds(pl.multiple_of(r * seq + low, 256), 256)
            ctx[rows, col] = jnp.concatenate(mixed[2 * n : 2 * n + 2]).T.astype(BF16)

    phase(n_a, [attend_step], plans["attn"])
    run_calls(plans, "o")
    norm_all[...] = parts[len(small.hops)]
    begin("out", w_small.at[3], out_all, 4)
    begin("ctx", ctx, ctx_out, 5)

    def out_step(m):
        rows = pl.ds(pl.multiple_of(m * 256, 256), 256)
        attended = dot_nt(ctx[rows, :], w_small[3].reshape(D, D))
        total = tok[rows, :].astype(F32) + attended
        res[rows, :] = total
        unit, _ = normed(total)
        hidden[rows, :] = (unit * norm_all[0:1, :] + norm_all[1:2, :]).astype(BF16)

    phase(n_o, [out_step], plans.get("out", {}))
    begin("res", res, resid_out, 6)
    begin("hidden", hidden, hidden_out, 7)
    run_calls(plans, "u")
    begin("up", w_up, up_all, 8)

    n_half = 2 * FF // 256
    rows_half = t_here // 2

    def half_of(i):
        col = pl.ds(pl.multiple_of((i // 2) * 256, 256), 256)
        rows = pl.ds(pl.multiple_of((i % 2) * rows_half, rows_half), rows_half)
        return rows, col

    def up_dot(i, dst):
        rows, col = half_of(i)
        dst[...] = dot_nn(hidden[rows, :], w_up[:, :, :, :, col].reshape(D, 256))

    def up_act(i, src):
        rows, col = half_of(i)
        for k in range(0, rows_half, 64):
            part = pl.ds(pl.multiple_of((i % 2) * rows_half + k, 64), 64)
            value, tangent = gelu_pair(src[k : k + 64, :])
            act[part, col] = value.astype(BF16)
            slope[(i // 2) % 2, part, :] = tangent.astype(BF16)

    def slope_copy(j):
        col = pl.ds(pl.multiple_of(j * 256, 256), 256)
        return pltpu.make_async_copy(slope.at[j % 2], slope_out.at[:, col], io_sem.at[9 + j % 2])

    up_dot(0, pre.at[0])

    def up_step(j):
        @pl.when(j >= 2)
        def _():
            slope_copy(j - 2).wait()

        up_dot(2 * j + 1, pre.at[1])
        up_act(2 * j, pre.at[0])

    def up_next(j):
        up_dot((2 * j + 2) % n_half, pre.at[0])
        up_act(2 * j + 1, pre.at[1])
        slope_copy(j).start()

    phase(n_u, [up_step, up_next], plans.get("up", {}))
    begin("act", act, act_out, 11)
    for j in (n_u - 2, n_u - 1):
        slope_copy(j).wait()
    for key in ("cot", "res", "hidden"):
        copies[key].wait()
    dnorm[...] = jnp.zeros_like(dnorm)

    def hidden_step(m):
        rows = pl.ds(pl.multiple_of(m * 128, 128), 128)
        unit, _ = normed(res[rows, :])
        res[rows, :] = unit * norm_all[0:1, :] + norm_all[1:2, :]

    phase(t_here // 128, [hidden_step], {})
    for a in DOWN_LEVELS:
        run_calls(plans, "d%d" % a)
        level = me[0] ^ a
        width = D // nz
        col = pl.ds(pl.multiple_of(level * width, width), width)

        def down_step(m):
            rows = pl.ds(pl.multiple_of(m * 512, 512), 512)
            res[rows, col] += dot_nt(act[rows, :], w_down[level].reshape(width, FF))

        phase(t_here // 512, [down_step], {})
    begin("down", w_down, down_all, 12)

    def norm_step(m):
        rows = pl.ds(pl.multiple_of(m * 128, 128), 128)
        unit, scale = normed(res[rows, :])
        tok[rows, :] = (unit * norm_all[2:3, :] + norm_all[3:4, :]).astype(BF16)
        grad = cot[rows, :].astype(F32)
        dnorm[0:1, :] = dnorm[0:1, :] + jnp.sum(grad * unit, axis=0, keepdims=True)
        dnorm[1:2, :] = dnorm[1:2, :] + jnp.sum(grad, axis=0, keepdims=True)
        dres = norm_backward(grad * norm_all[2:3, :], unit, scale)
        res[rows, :] = dres
        hidden[rows, :] = dres.astype(BF16)

    phase(t_here // 128, [norm_step], {})
    begin("layer", tok, layer_out, 13)
    begin("dres", res, dres_out, 14)
    begin("dffn", hidden, dffn_out, 15)
    for g in gathers.values():
        g.drain()
    for key in ("proj", "out", "up", "down", "qkv", "ctx", "act", "layer", "dres", "dffn"):
        copies[key].wait()


FORWARD_SCRIPT = (
    ("start", (
        (-1, (12, 11, 1000, 0, 1013, 1012, 13, 3011, 3000, 2000, 3012,)),
    )),
    ("q", (
        (-1, (30, 2012, 22, 21, 2011, 4011, 1023, 2030, 1022, 3021, 1011, 4012, 32, 3022, 2022, 1030, 2021,
            2040, 3032, 4000, 1032, 40, 42, 23, 1040, 3013, 3030, 2013, 2032, 3042, 52, 41, 1021, 1042, 4030,
            31, 1033, 3040, 3052, 3023, 1041, 2023, 33, 3043, 43, 1031, 1043, 2042, 4022, 2050, 4013, 5011,
            1052, 5000, 4021, 53, 2041, 1051, 3041, 3031, 1053, 2031, 50, 3050, 2052, 51,)),
    )),
    ("qm", (
        (0, (1050,)),
        (3, (2043,)),
    )),
    ("k", (
        (-1, ()),
    )),
    ("km", (
        (1, (3051, 3033, 2051,)),
        (2, (2033, 5012,)),
    )),
    ("v", (
        (-1, (3053, 5013, 4040, 2053,)),
    )),
    ("attn", (
        (1, (4032,)),
        (5, (5030,)),
        (10, (4041, 4042, 4023,)),
        (13, (5022, 5021, 5040,)),
    )),
    ("o", (
        (-1, ()),
    )),
    ("out", (
        (0, (5050, 4031, 4052,)),
        (1, (4033, 4043,)),
    )),
    ("u", (
        (-1, (5041, 4050, 4053, 4051,)),
    )),
    ("up", (
        (1, (5032, 5023,)),
        (17, (5042, 5031,)),
        (26, (5033,)),
        (29, (5043, 5052, 5051,)),
    )),
    ("d0", (
        (-1, ()),
    )),
    ("d1", (
        (-1, ()),
    )),
    ("d2", (
        (-1, ()),
    )),
    ("d3", (
        (-1, (5053,)),
    )),
)
DOWN_LEVELS = (0, 1, 2, 3)


def run_forward(nz, tokens_in, cotangent, segments, proj, out, up, down, norm):
    t_here = cotangent.shape[0]
    rows_here, seq = segments.shape
    n_sum = len(sum_hops(nz))
    rows = D // (4 * nz)
    full = lambda cols: jax.ShapeDtypeStruct((nz, 2, 2, rows, cols), BF16)
    flat = lambda cols, kind: jax.ShapeDtypeStruct((t_here, cols), kind)
    seg_col = jnp.broadcast_to(segments.reshape(t_here, 1), (t_here, 128))
    seg_row = segments.reshape(rows_here, 1, seq)
    return pl.pallas_call(
        functools.partial(forward_kernel, nz),
        out_shape=[
            jax.ShapeDtypeStruct((3, nz, 2, 2, rows, D), BF16),
            full(D),
            full(FF),
            full(FF),
            jax.ShapeDtypeStruct(norm.shape, F32),
            jax.ShapeDtypeStruct((3, t_here, D), BF16),
            flat(D, BF16),
            jax.ShapeDtypeStruct((rows_here * (D // 128), 8, seq), F32),
            flat(D, F32),
            flat(D, BF16),
            flat(FF, BF16),
            flat(FF, BF16),
            flat(D, BF16),
            flat(D, F32),
            flat(D, BF16),
            jax.ShapeDtypeStruct((8, D), F32),
        ],
        in_specs=[ANY, ANY] + [VMEM] * 7,
        out_specs=[ANY] * 4 + [VMEM, ANY, ANY, VMEM] + [ANY] * 7 + [VMEM],
        scratch_shapes=[
            pltpu.VMEM((t_here, D), BF16),
            pltpu.VMEM((t_here, D), BF16),
            pltpu.VMEM((4, nz, 2, 2, rows, D), BF16),
            pltpu.VMEM((nz, 2, 2, rows, FF), BF16),
            pltpu.VMEM((nz, 2, 2, rows, FF), BF16),
            pltpu.VMEM((3, t_here, D), BF16),
            pltpu.VMEM((t_here, D), BF16),
            pltpu.VMEM((rows_here, seq, seq), F32),
            pltpu.VMEM((t_here, D), F32),
            pltpu.VMEM((t_here, D), BF16),
            pltpu.VMEM((t_here, FF), BF16),
            pltpu.VMEM((2, t_here // 2, 256), F32),
            pltpu.VMEM((2, t_here, 256), BF16),
            DMA((48 * nz,)),
            DMA((48 * nz,)),
            pltpu.VMEM((n_sum + 1,) + norm.shape, F32),
            pltpu.VMEM((n_sum,) + norm.shape, F32),
            DMA((n_sum,)),
            DMA((n_sum,)),
            DMA((16,)),
        ],
        compiler_params=pltpu.CompilerParams(
            collective_id=0, has_side_effects=True, vmem_limit_bytes=62 << 20
        ),
        name="forward",
    )(tokens_in, cotangent, seg_col, seg_row, proj, out, up, down, norm)


def view_flat(ref, pos):
    z, x, c, y = pos
    rows, half = 64, ref.shape[1] // 2
    row = (z * 4 + x * 2 + c) * rows
    return ref.at[pl.ds(pl.multiple_of(row, rows), rows), pl.ds(pl.multiple_of(y * half, half), half)]


def add_rows(dst, terms, rows=16):
    def body(i, carry):
        block = pl.ds(pl.multiple_of(i * rows, rows), rows)
        total = terms[0][block, :].astype(F32)
        for term in terms[1:]:
            total = total + term[block, :].astype(F32)
        dst[block, :] = total.astype(dst.dtype)
        return carry

    lax.fori_loop(0, dst.shape[0] // rows, body, 0)


def add_pair(dst, other, rows=16):
    def body(i, carry):
        block = pl.ds(pl.multiple_of(i * rows, rows), rows)
        dst[block, :] = dst[block, :] + other[block, :]
        return carry

    lax.fori_loop(0, dst.shape[0] // rows, body, 0)


class Scatter:
    def __init__(self, me, nz, index, grad, from_c, cut, held, swap, came, result, sems, counter, before=()):
        self.me, self.nz, self.index, self.grad, self.from_c = me, nz, index, grad, from_c
        self.cut, self.held, self.swap, self.came, self.result = cut, held, swap, came, result
        self.load_sem, self.send_sem, self.recv_sem = sems
        self.counter, self.side, self.before = counter, {}, before

    def where(self, a, b, e):
        return (a * 2 + b) * 2 + e

    def part(self, ref, i):
        return ref.at[i, :, pl.ds(*self.cut)]

    def remote(self, src, dst, slot, hop):
        sem = self.index * 8 * self.nz + slot
        return pltpu.make_async_remote_copy(
            src_ref=src, dst_ref=dst, send_sem=self.send_sem.at[sem], recv_sem=self.recv_sem.at[sem],
            device_id=device_at(self.me, hop), device_id_type=MESH,
        )

    def core_copy(self, a, b, e):
        i = self.where(a, b, e)
        return self.remote(view_flat(self.grad, moved(self.me, (a, b, 1, e))), self.from_c.at[i], i, HOP_C)

    def hop_copy(self, kind, a):
        b, e = {"w": (1, 1), "d": (1, 1), "x": (1, 0), "y": (0, 1), "z": (0, 0)}[kind]
        hop = {"w": hop_z(1), "d": HOP_Y if a % 4 == 0 else HOP_X, "x": HOP_X, "y": HOP_Y, "z": hop_z(a)}[kind]
        slot = {"w": a // 2, "d": self.nz // 2 + a // 2, "x": self.nz + a, "y": 2 * self.nz + a, "z": 3 * self.nz + a}[kind]
        return self.remote(
            self.part(self.held, self.where(a, b, e)), self.part(self.came, slot), 4 * self.nz + slot, hop
        )

    def took(self, kind, a):
        copy = self.hop_copy(kind, a)
        copy.wait_recv()
        return copy.dst_ref

    def mine(self, a, b, e):
        return self.part(self.held, self.where(a, b, e))

    def pairs(self, a):
        return [(self.where(a, b, e), b * 2 + e, (a, b, 0, e)) for b in range(2) for e in range(2)]

    def loads(self, a):
        out, side = [], self.side[a]
        for i, k, rel in self.pairs(a):
            out.append(pltpu.make_async_copy(
                view_flat(self.grad, moved(self.me, rel)), self.part(self.held, i), self.load_sem.at[side * 8 + k]
            ))
            out.append(pltpu.make_async_copy(
                self.from_c.at[i], self.part(self.swap, side * 4 + k), self.load_sem.at[side * 8 + 4 + k]
            ))
        return out

    def exchange(self, a):
        for b, e in ((1, 1), (1, 0), (0, 1), (0, 0)):
            self.core_copy(a, b, e).start()

    def take_side(self, a):
        self.side[a] = len(self.counter) % 2
        self.counter.append(a)

    def fetch(self, a):
        for other in self.before:
            other.release(a)
        for b, e in ((1, 1), (1, 0), (0, 1), (0, 0)):
            self.core_copy(a, b, e).wait_recv()
        for load in self.loads(a):
            load.start()

    def join(self, a):
        for load in self.loads(a):
            load.wait()
        for i, k, _ in self.pairs(a):
            add_pair(self.part(self.held, i), self.part(self.swap, self.side[a] * 4 + k))
        if a % 2:
            self.hop_copy("w", a).start()
        if a % 4 != 0:
            self.hop_copy("x", a).start()
        if a % 4 != 2:
            self.hop_copy("y", a).start()

    def bend(self, a):
        add_pair(self.mine(a, 1, 1), self.took("w", a))
        self.hop_copy("d", a).start()

    def square(self, a):
        kind, b, e = ("x", 1, 0) if a % 4 == 0 else ("y", 0, 1)
        add_pair(self.mine(a, b, e), self.took("d", a))
        self.hop_copy(kind, a).start()

    def column(self, a):
        terms = [self.mine(a, 0, 0), self.took("x", a), self.took("y", a)]
        if a:
            add_rows(terms[0], terms)
            self.hop_copy("z", a).start()
        else:
            add_rows(self.result, terms + [self.took("z", k) for k in range(1, self.nz)])

    def release(self, a):
        for b in range(2):
            for e in range(2):
                self.core_copy(a, b, e).wait_send()
        for kind in ("w", "x", "y", "z") if a % 2 else ("d", "x", "y", "z") if a else ("d", "x", "y"):
            self.hop_copy(kind, a).wait_send()


def transpose_into(dst, src):
    def body(i, carry):
        block = pl.ds(pl.multiple_of(i * 128, 128), 128)
        dst[:, block] = src[block, :].T
        return carry

    lax.fori_loop(0, src.shape[0] // 128, body, 0)


def backward_kernel(nz, tokens, seg_col, seg_row, proj, out, up, down, norm, qkv_in, ctx_in, lse,
                    resid, hidden, act, slope, dres, dffn, dnorm_two,
                    input_grad, *refs):
    red, norm_sum, grads, swaps, refs = refs[:6], refs[6], refs[7:13], refs[13:19], refs[19:]
    down_grad, up_grad, out_grad = grads[:3]
    (tiles, buf_a, buf_b, buf_c, total, dpre, stage, ctx, dqkv, resid_tile, dq,
     held, held_mix, swap, came_down, came_up, came_mix,
     load_sem, send_sem, recv_sem, io_sem, parts, came, sum_send, sum_recv) = refs
    me = position()
    t_here, seq = total.shape[0], seg_row.shape[2]
    rows_here, pairs = t_here // seq, D // 128
    n_ff = FF // 512
    copies = {}

    def begin(key, src, dst, sem):
        copies[key] = pltpu.make_async_copy(src, dst, io_sem.at[sem])
        copies[key].start()

    def col512(j):
        return pl.ds(pl.multiple_of(j * 512, 512), 512)

    def tile_copy(src, j, base, sem):
        return pltpu.make_async_copy(src.at[:, col512(j)], tiles.at[base + j % 2], io_sem.at[sem + j % 2])

    def stage_copy(dst, col, slot):
        return pltpu.make_async_copy(stage.at[slot], dst.at[:, col], io_sem.at[8 + slot])

    def put_stage(i, value, dst, col):
        slot = i % 2

        @pl.when(i >= 2)
        def _():
            stage_copy(dst, col, slot).wait()

        stage[slot] = value.astype(BF16)
        stage_copy(dst, col, slot).start()

    def flush_stage(dst):
        for slot in range(2):
            stage_copy(dst, pl.ds(0, 512), slot).wait()

    begin("dffn", dffn, buf_a, 10)
    begin("hidden", hidden, ctx, 11)
    begin("dres", dres, total, 12)
    tile_copy(act, 0, 0, 0).start()
    entry_barrier(me, nz)
    sems = (load_sem, send_sem, recv_sem)
    counter = []
    half = D // 2
    cuts = [(0, FF // 2)] * 2 + [(i * half, half) for i in (3, 0, 1, 2)]
    arrivals = (came_down, came_up) + (came_mix,) * 4
    scatters = {}
    for i, name in enumerate("duoqkv"):
        before = {"u": "d"}.get(name)
        scatters[name] = Scatter(
            me, nz, i, grads[i], swaps[i], cuts[i], held if name in "du" else held_mix, swap, arrivals[i], red[i],
            sems, counter,
            [scatters[before]] if before else [],
        )
    small = SmallSum(me, nz, parts, came, sum_send, sum_recv)
    n_small = len(small.hops)
    n_attn, n_m = rows_here * pairs, t_here // 256
    plans = script_plans(BACKWARD_SCRIPT, scatters)
    for i in range(n_small):
        calls = plans.setdefault("attn", {}).setdefault(2 * i + 1, [])
        calls.append(functools.partial(small.finish, i))
        if i + 1 < n_small:
            calls.append(functools.partial(small.start, i + 1))

    copies["dffn"].wait()
    transpose_into(buf_b, buf_a)

    def down_step(j):
        @pl.when(j + 1 < n_ff)
        def _():
            tile_copy(act, j + 1, 0, 0).start()

        tile_copy(act, j, 0, 0).wait()
        put_stage(j, dot_nn(buf_b[...], tiles[j % 2]), down_grad, col512(j))

    phase(n_ff, [down_step], {})
    for src, base in ((down, 2), (slope, 4), (up, 6)):
        tile_copy(src, 0, base, base).start()
    copies["hidden"].wait()
    transpose_into(buf_c, ctx)
    begin("ctx", ctx_in, ctx, 11)
    for j in range(2):
        begin(("w_out", j), out.at[:, pl.ds(j * 512, 512)], dqkv.at[j], 13 + 6 * j)
    flush_stage(down_grad)
    copies["dres"].wait()

    def pre_step(j):
        @pl.when(j + 1 < n_ff)
        def _():
            for src, base in ((down, 2), (slope, 4), (up, 6)):
                tile_copy(src, j + 1, base, base).start()

        for src, base in ((down, 2), (slope, 4), (up, 6)):
            tile_copy(src, j, base, base).wait()
        dpre[...] = (dot_nn(buf_a[...], tiles[2 + j % 2]) * tiles[4 + j % 2].astype(F32)).astype(BF16)

    def up_grad_step(j):
        put_stage(j, dot_nn(buf_c[...], dpre[...]), up_grad, col512(j))

    def hidden_step(j):
        total[...] += dot_nt(dpre[...], tiles[6 + j % 2])

    phase(n_ff, [pre_step, up_grad_step, hidden_step], plans.get("ffn", {}))
    flush_stage(up_grad)
    for i in range(6):
        begin(("qkv", i), qkv_in.at[i // 2, :, pl.ds((i % 2) * 512, 512)], tiles.at[i], i)
    norm_sum[...] = jnp.zeros_like(norm_sum)

    def resid_copy(m):
        rows = pl.ds(pl.multiple_of(m * 256, 256), 256)
        return pltpu.make_async_copy(resid.at[rows, :], resid_tile.at[m % 2], io_sem.at[14 + m % 2])

    resid_copy(0).start()

    def norm_step(m):
        @pl.when(m + 1 < n_m)
        def _():
            resid_copy(m + 1).start()

        resid_copy(m).wait()
        rows = pl.ds(pl.multiple_of(m * 256, 256), 256)
        unit, scale = normed(resid_tile[m % 2])
        grad = total[rows, :]
        norm_sum[0:1, :] = norm_sum[0:1, :] + jnp.sum(grad * unit, axis=0, keepdims=True)
        norm_sum[1:2, :] = norm_sum[1:2, :] + jnp.sum(grad, axis=0, keepdims=True)
        moved_grad = norm_backward(grad * norm[0:1, :], unit, scale)
        total[rows, :] = moved_grad
        buf_b[rows, :] = moved_grad.astype(BF16)

    phase(n_m, [norm_step], plans.get("ln", {}))
    norm_sum[2:4, :] = dnorm_two[0:2, :]
    parts[0] = norm_sum[...]
    small.start(0)
    transpose_into(buf_a, buf_b)
    copies["ctx"].wait()
    for j in range(2):
        copies[("w_out", j)].wait()

    def out_grad_step(j):
        put_stage(j, dot_nn(buf_a[...], ctx[:, col512(j)]), out_grad, col512(j))

    phase(2, [out_grad_step], plans.get("out", {}))
    flush_stage(out_grad)

    def ctx_step(j):
        buf_a[:, col512(j)] = dot_nn(buf_b[...], dqkv[j]).astype(BF16)

    phase(2, [ctx_step], plans.get("ctx", {}))
    mine = pl.ds(pl.multiple_of(me[3] * t_here, t_here), t_here)
    begin("tok", tokens.at[mine, :], buf_b, 10)

    bias = resid_tile

    def bias_step(r):
        for k in range(2):
            rows = pl.ds(pl.multiple_of(r * seq + k * (seq // 2), seq // 2), seq // 2)
            bias[r, :, k * seq : (k + 1) * seq] = jnp.where(seg_col[rows, 0:1] == seg_row[r], 0.0, NEG_FILL)

    phase(rows_here, [bias_step], {})
    for i in range(6):
        copies[("qkv", i)].wait()
    head_of = lax.broadcasted_iota(jnp.int32, (128, 128), 1) // HEAD_DIM
    head_pick = (
        lax.broadcasted_iota(jnp.int32, (8, 128), 1) // HEAD_DIM == lax.broadcasted_iota(jnp.int32, (8, 128), 0)
    ).astype(BF16)
    shrink = jnp.asarray(HEAD_DIM**-0.5, BF16)

    def per_head(block):
        return jnp.concatenate([jnp.where(head_of == h, block, jnp.zeros_like(block)) for h in range(2)])

    def attend_step(u):
        r, p = u // pairs, u % pairs
        side = p // 4
        col = pl.ds(pl.multiple_of(p * 128, 128), 128)
        near = pl.ds(pl.multiple_of((p % 4) * 128, 128), 128)
        whole = pl.ds(pl.multiple_of(r * seq, seq), seq)
        product = buf_a[whole, col].astype(F32) * ctx[whole, col].astype(F32)
        coarse = product.astype(BF16)
        fine = (product - coarse.astype(F32)).astype(BF16)
        delta = dot_nt(head_pick, coarse) + dot_nt(head_pick, fine)
        dq[...] = jnp.zeros_like(dq)
        n_blocks = seq // 128

        def block_of(kb):
            low, high = max(0, kb - 2) * 128, min(n_blocks, kb + 3) * 128
            k_rows = pl.ds(pl.multiple_of(r * seq + kb * 128, 128), 128)
            q_rows = pl.ds(pl.multiple_of(r * seq + low, 128), high - low)
            return low, high, k_rows, q_rows

        def products(kb):
            low, high, k_rows, q_rows = block_of(kb)
            q = tiles[side, q_rows, near] * shrink
            keys = per_head(tiles[2 + side, k_rows, near])
            return keys, q, dot_nt(keys, q), dot_nt(per_head(tiles[4 + side, k_rows, near]), buf_a[q_rows, col])

        waiting = [products(0)]
        for kb in range(n_blocks):
            if kb + 1 < n_blocks:
                waiting.append(products(kb + 1))
            keys, q, scores, d_probs = waiting.pop(0)
            low, high, k_rows, q_rows = block_of(kb)
            top, left = kb * 128 % (seq // 2), kb * 128 // (seq // 2) * seq
            block = bias[r, top : top + 128, left + low : left + high]
            probs, d_scores = [], []
            for h in range(2):
                part = slice(h * 128, h * 128 + 128)
                prob = jnp.exp(scores[part] + block - lse[u, h : h + 1, low:high])
                probs.append(prob.astype(BF16))
                d_scores.append((prob * (d_probs[part] - delta[h : h + 1, low:high])).astype(BF16))
            probs, d_scores = jnp.concatenate(probs), jnp.concatenate(d_scores)
            d_value = dot_nn(probs, buf_a[q_rows, col])
            d_key = dot_nn(d_scores, q)
            dqkv[4 + side, k_rows, near] = jnp.where(head_of == 0, d_value[:128], d_value[128:]).astype(BF16)
            dqkv[2 + side, k_rows, near] = jnp.where(head_of == 0, d_key[:128], d_key[128:]).astype(BF16)
            dq[:, low:high] += dot_nn(keys.T, d_scores)
        dqkv[side, whole, near] = (dq[...].T * HEAD_DIM**-0.5).astype(BF16)

    phase(n_attn, [attend_step], plans["attn"])
    for i in range(6):
        begin(("proj", i), proj.at[i // 2, :, pl.ds((i % 2) * 512, 512)], tiles.at[i], i)
    copies["tok"].wait()
    transpose_into(buf_c, buf_b)

    for s, name in enumerate("qkv"):

        def project_step(i, s=s):
            put_stage(i, dot_nn(buf_c[...], dqkv[2 * s + i]), grads[3 + s], col512(i))

        phase(2, [project_step], plans.get("p" + name, {}))
        flush_stage(grads[3 + s])
    for i in range(6):
        copies[("proj", i)].wait()
    def in_copy(m):
        rows = pl.ds(pl.multiple_of(m * 256, 256), 256)
        return pltpu.make_async_copy(total.at[rows, :], input_grad.at[rows, :], io_sem.at[16 + m])

    def input_step(m):
        rows = pl.ds(pl.multiple_of(m * 256, 256), 256)
        value = total[rows, :]
        for i in range(6):
            value = value + dot_nt(dqkv[i, rows, :], tiles[i])
        total[rows, :] = value

    phase(n_m, [input_step], plans.get("in", {}))
    for m in range(n_m):
        in_copy(m).start()
    run_calls(plans, "end")
    for name in "uoqkv":
        for a in range(nz):
            scatters[name].release(a)
    for m in range(n_m):
        in_copy(m).wait()
    norm_sum[...] = parts[n_small]


BACKWARD_SCRIPT = (
    ("ffn", (
        (0, (5061, 5062,)),
        (4, (5071, 5063, 5060,)),
        (6, (5081,)),
        (7, (5073, 5072,)),
        (9, (5083, 5082, 5070,)),
        (11, (5080, 5090,)),
        (14, (5092,)),
        (15, (5103,)),
        (23, (5030, 5032,)),
    )),
    ("ln", (
        (1, (4063, 4061, 5101, 4062, 4060,)),
    )),
    ("out", (
        (0, (4073,)),
        (1, (5102,)),
    )),
    ("ctx", (
        (1, (3061, 4071, 3062, 4083, 3060, 3063,)),
    )),
    ("attn", (
        (0, (4081, 4072,)),
        (2, (4082, 3071, 3072,)),
        (3, (4103, 3081, 3082, 3070, 3073, 5100,)),
        (4, (4092, 3080, 3083, 4070,)),
        (6, (4080,)),
        (9, (3101, 4090,)),
        (10, (3090, 4101,)),
        (13, (4032, 3092,)),
        (14, (3103,)),
    )),
    ("pq", (
        (0, (3032, 4030, 3030,)),
    )),
    ("pk", (
        (0, (4102,)),
        (1, (3102, 63, 61, 62, 60,)),
    )),
    ("pv", (
        (0, (73,)),
        (1, (83, 71, 1063, 72, 1062, 1061, 1060, 81, 82, 70,)),
    )),
    ("in", (
        (0, (103, 80, 1071, 92, 2063, 1072, 2061, 101, 1081, 4100, 1070, 1082, 1073, 2060, 90, 1080, 2073,
            1083, 2071, 32, 2062, 2083,)),
        (1, (1101, 30, 1090, 2081, 2072, 2070, 1092, 3100,)),
        (2, (2082, 2092, 1103, 2080, 102,)),
        (3, (1030, 1032, 2090, 2103,)),
    )),
    ("end", (
        (-1, (2101, 2032, 1102, 2030, 100, 2102, 1100, 2100,)),
    )),
)


def run_backward(nz, tokens_in, segments, proj, out, up, down, norm, qkv, ctx, lse,
                 resid, hidden, act, slope, dres, dffn, dnorm_two):
    t_here = dffn.shape[0]
    rows_here, seq = segments.shape
    n_sum = len(sum_hops(nz))
    piece = (64, FF // 2)
    seg_col = jnp.broadcast_to(segments.reshape(t_here, 1), (t_here, 128))
    seg_row = segments.reshape(rows_here, 1, seq)
    widths = (FF // 2,) * 2 + (D // 2,) * 4
    reduced = [jax.ShapeDtypeStruct((64, w), F32) for w in widths]
    grads = [jax.ShapeDtypeStruct((D, 2 * w), BF16) for w in widths]
    swapped = [jax.ShapeDtypeStruct((4 * nz, 64, w), BF16) for w in widths]
    results = pl.pallas_call(
        functools.partial(backward_kernel, nz),
        out_shape=[jax.ShapeDtypeStruct((t_here, D), F32)] + reduced + [jax.ShapeDtypeStruct(norm.shape, F32)]
        + grads + swapped,
        in_specs=[ANY, VMEM, VMEM] + [ANY] * 4 + [VMEM, ANY, ANY, VMEM] + [ANY] * 6 + [VMEM],
        out_specs=[ANY] + [VMEM] * 7 + [ANY] * 12,
        scratch_shapes=[
            pltpu.VMEM((8, t_here, 512), BF16),
            pltpu.VMEM((t_here, D), BF16),
            pltpu.VMEM((t_here, D), BF16),
            pltpu.VMEM((t_here, D), BF16),
            pltpu.VMEM((t_here, D), F32),
            pltpu.VMEM((t_here, 512), BF16),
            pltpu.VMEM((2, t_here, 512), BF16),
            pltpu.VMEM((t_here, D), BF16),
            pltpu.VMEM((6, t_here, 512), BF16),
            pltpu.VMEM((2, 256, D), F32),
            pltpu.VMEM((128, seq), F32),
            pltpu.VMEM((4 * nz,) + piece, BF16),
            pltpu.VMEM((4 * nz,) + piece, BF16),
            pltpu.VMEM((8,) + piece, BF16),
            pltpu.VMEM((4 * nz,) + piece, BF16),
            pltpu.VMEM((4 * nz,) + piece, BF16),
            pltpu.VMEM((4 * nz,) + piece, BF16),
            DMA((16,)),
            DMA((48 * nz,)),
            DMA((48 * nz,)),
            DMA((20,)),
            pltpu.VMEM((n_sum + 1,) + norm.shape, F32),
            pltpu.VMEM((n_sum,) + norm.shape, F32),
            DMA((n_sum,)),
            DMA((n_sum,)),
        ],
        compiler_params=pltpu.CompilerParams(
            collective_id=1, has_side_effects=True, vmem_limit_bytes=62 << 20
        ),
        name="backward",
    )(tokens_in, seg_col, seg_row, proj, out, up, down, norm, qkv, ctx, lse,
      resid, hidden, act, slope, dres, dffn, dnorm_two)
    return results[:8]


def local_rows(
    tokens_in,
    cotangent,
    segment_ids,
    project_weight,
    project_momentum,
    project_squares,
    output_weight,
    output_momentum,
    output_squares,
    up_weight,
    up_momentum,
    up_squares,
    down_weight,
    down_momentum,
    down_squares,
    norm_params,
    norm_momentum,
    norm_squares,
):
    nz = lax.axis_size("dp") // 4
    dp, mp = lax.axis_index("dp"), lax.axis_index("mp")
    norm_cols = norm_params.shape[1]
    norm_start = (dp * 2 + mp) * norm_cols
    norm_wide = lax.dynamic_update_slice(
        jnp.zeros((8, D), F32), norm_params.astype(BF16).astype(F32), (0, norm_start)
    )
    rows_here = segment_ids.shape[0] // 2
    segments = lax.dynamic_slice_in_dim(segment_ids, mp * rows_here, rows_here, 0)
    (proj_w, out_w, up_w, down_w, norm_full, qkv, context, lse, resid_one, hidden_low, act_low, slope,
     layer_out, d_resid_two, d_ffn, d_norm_two) = run_forward(
        nz,
        tokens_in,
        cotangent,
        segments,
        project_weight,
        output_weight,
        up_weight,
        down_weight,
        norm_wide,
    )
    input_grad, down_red, up_red, out_red, *proj_red, norm_sum = run_backward(
        nz,
        tokens_in,
        segments,
        proj_w.reshape(3, D, D),
        out_w.reshape(D, D),
        up_w.reshape(D, FF),
        down_w.reshape(D, FF),
        norm_full,
        qkv,
        context,
        lse,
        resid_one,
        hidden_low,
        act_low,
        slope,
        d_resid_two,
        d_ffn,
        d_norm_two,
    )
    proj_red = jnp.stack(proj_red)
    norm_red = lax.dynamic_slice(norm_sum, (0, norm_start), (4, norm_cols))
    return (
        layer_out,
        input_grad,
        *adam_step(proj_red, project_weight, project_momentum, project_squares, D ** (-0.5)),
        *adam_step(out_red, output_weight, output_momentum, output_squares, 4.0 * D ** (-0.5)),
        *adam_step(up_red, up_weight, up_momentum, up_squares, D ** (-0.5)),
        *adam_step(down_red, down_weight, down_momentum, down_squares, FF ** (-0.5)),
        *adam_step(norm_red, norm_params, norm_momentum, norm_squares, 0.3),
    )


def by_rows(mesh):
    dp, mp = mesh.shape["dp"], mesh.shape["mp"]
    return mp == 2 and dp >= 8 and dp & (dp - 1) == 0 and D % (64 * dp) == 0


def solution(mesh):
    body = local_rows if by_rows(mesh) else local_plain
    return jax.shard_map(
        body,
        mesh=mesh,
        in_specs=(
            P("dp", None),
            P(("dp", "mp"), None),
            P("dp", None),
            P(None, "dp", "mp"),
            P(None, "dp", "mp"),
            P(None, "dp", "mp"),
            P("dp", "mp"),
            P("dp", "mp"),
            P("dp", "mp"),
            P("dp", "mp"),
            P("dp", "mp"),
            P("dp", "mp"),
            P("dp", "mp"),
            P("dp", "mp"),
            P("dp", "mp"),
            P(None, ("dp", "mp")),
            P(None, ("dp", "mp")),
            P(None, ("dp", "mp")),
        ),
        out_specs=(
            P(("dp", "mp"), None),
            P(("dp", "mp"), None),
            P(None, "dp", "mp"),
            P(None, "dp", "mp"),
            P(None, "dp", "mp"),
            P(None, "dp", "mp"),
            P("dp", "mp"),
            P("dp", "mp"),
            P("dp", "mp"),
            P("dp", "mp"),
            P("dp", "mp"),
            P("dp", "mp"),
            P("dp", "mp"),
            P("dp", "mp"),
            P("dp", "mp"),
            P("dp", "mp"),
            P("dp", "mp"),
            P("dp", "mp"),
            P(None, ("dp", "mp")),
            P(None, ("dp", "mp")),
            P(None, ("dp", "mp")),
            P(None, ("dp", "mp")),
        ),
        check_vma=False,
    )
```

```python
import functools

import jax
import jax.numpy as jnp
from jax import lax
from jax.experimental import pallas as pl
from jax.experimental.pallas import tpu as pltpu
from jax.sharding import PartitionSpec as P

D = 1024
HEAD_DIM = 64
FF = 4096
STEP = 3


EPS_NORM = 1e-12
NEG_FILL = -1e30
BETA_ONE = 0.5
BETA_TWO = 0.5
ADAM_EPS = 1e-08
DECAY_RATE = 0.01


def layer_norm(values, norm_gain, norm_shift):
    center = values - jnp.mean(values, axis=-1, keepdims=True)
    spread = jnp.mean(center * center, axis=-1, keepdims=True)
    return center * lax.rsqrt(spread + EPS_NORM) * norm_gain + norm_shift


def exact_gelu(values):
    return jax.nn.gelu(values, approximate=False)


def adam_step(gradient, weight, first_old, second, step_rate):
    correct_one = 1.0 - BETA_ONE**STEP
    correct_two = 1.0 - BETA_TWO**STEP
    moment = BETA_ONE * first_old + (1.0 - BETA_ONE) * gradient
    square = BETA_TWO * second + (1.0 - BETA_TWO) * gradient * gradient
    normed = moment / correct_one / (jnp.sqrt(square / correct_two) + ADAM_EPS)
    updated = weight - step_rate * (normed + DECAY_RATE * weight)
    return (gradient, moment, square, updated)


def local_plain(
    tokens_in,
    cotangent,
    segment_ids,
    project_weight,
    project_momentum,
    project_squares,
    output_weight,
    output_momentum,
    output_squares,
    up_weight,
    up_momentum,
    up_squares,
    down_weight,
    down_momentum,
    down_squares,
    norm_params,
    norm_momentum,
    norm_squares,
):
    gathered = (
        lax.all_gather(project_weight.astype(jnp.bfloat16), "dp", axis=1, tiled=True),
        lax.all_gather(output_weight.astype(jnp.bfloat16), "dp", axis=0, tiled=True),
        lax.all_gather(up_weight.astype(jnp.bfloat16), "dp", axis=0, tiled=True),
        lax.all_gather(down_weight.astype(jnp.bfloat16), "dp", axis=0, tiled=True),
    )
    proj_copy, out_copy, up_copy, down_copy = gathered
    norm_full = lax.all_gather(
        norm_params.astype(jnp.bfloat16), ("dp", "mp"), axis=1, tiled=True
    ).astype(jnp.float32)
    rows_here = segment_ids.shape[0]
    seq_len = segment_ids.shape[1]
    local_width = proj_copy.shape[2]
    heads_here = local_width // HEAD_DIM
    score_scale = HEAD_DIM ** (-0.5)
    projected = jnp.einsum(
        "tc,scn->stn", tokens_in, proj_copy, preferred_element_type=jnp.float32
    ).astype(jnp.bfloat16)
    heads_split = projected.reshape(3, rows_here, seq_len, heads_here, HEAD_DIM)

    def masked_scores(query_rows, key_rows, row_segments):
        scores = (
            jnp.einsum("qhd,khd->hqk", query_rows, key_rows, preferred_element_type=jnp.float32)
            * score_scale
        )
        same_doc = row_segments[:, None] == row_segments[None, :]
        return jnp.where(same_doc[None], scores, NEG_FILL)

    def row_forward(packed):
        query_rows, key_rows, value_rows, row_segments = packed
        scores = masked_scores(query_rows, key_rows, row_segments)
        row_max = jnp.max(scores, axis=-1, keepdims=True)
        row_exp = jnp.exp(scores - row_max)
        row_total = jnp.sum(row_exp, axis=-1, keepdims=True)
        row_probs = (row_exp / row_total).astype(jnp.bfloat16)
        mixed = jnp.einsum(
            "hqk,khd->qhd", row_probs, value_rows, preferred_element_type=jnp.float32
        )
        row_lse = (row_max + jnp.log(row_total))[..., 0]
        return (mixed.astype(jnp.bfloat16).reshape(seq_len, local_width), row_lse)

    context_rows, lse_rows = lax.map(
        row_forward, (heads_split[0], heads_split[1], heads_split[2], segment_ids)
    )
    context = context_rows.reshape(rows_here * seq_len, local_width)
    attn_part = jnp.einsum("tn,dn->td", context, out_copy, preferred_element_type=jnp.float32)
    attn_share = lax.psum_scatter(
        attn_part.astype(jnp.bfloat16), "mp", scatter_dimension=0, tiled=True
    ).astype(jnp.float32)
    share_rows = attn_share.shape[0]
    share_start = lax.axis_index("mp") * share_rows
    token_share = lax.dynamic_slice_in_dim(tokens_in, share_start, share_rows, 0).astype(
        jnp.float32
    )
    hidden_one, norm_one_back = jax.vjp(
        layer_norm, token_share + attn_share, norm_full[0], norm_full[1]
    )
    hidden_low = lax.all_gather(hidden_one.astype(jnp.bfloat16), "mp", axis=0, tiled=True)
    pre_act = jnp.dot(hidden_low, up_copy, preferred_element_type=jnp.float32)
    act_full, gelu_back = jax.vjp(exact_gelu, pre_act)
    act_low = act_full.astype(jnp.bfloat16)
    ffn_part = jnp.einsum("tf,df->td", act_low, down_copy, preferred_element_type=jnp.float32)
    ffn_share = lax.psum_scatter(
        ffn_part.astype(jnp.bfloat16), "mp", scatter_dimension=0, tiled=True
    ).astype(jnp.float32)
    result, norm_two_back = jax.vjp(layer_norm, hidden_one + ffn_share, norm_full[2], norm_full[3])
    layer_out = result.astype(jnp.bfloat16)
    regathered = (
        lax.all_gather(project_weight.astype(jnp.bfloat16), "dp", axis=1, tiled=True),
        lax.all_gather(output_weight.astype(jnp.bfloat16), "dp", axis=0, tiled=True),
        lax.all_gather(up_weight.astype(jnp.bfloat16), "dp", axis=0, tiled=True),
        lax.all_gather(down_weight.astype(jnp.bfloat16), "dp", axis=0, tiled=True),
    )
    proj_copy, out_copy, up_copy, down_copy = regathered
    d_resid_two, d_gain_two, d_shift_two = norm_two_back(cotangent.astype(jnp.float32))
    d_ffn = lax.all_gather(d_resid_two.astype(jnp.bfloat16), "mp", axis=0, tiled=True)
    down_grad = jnp.einsum("td,tf->df", d_ffn, act_low, preferred_element_type=jnp.float32)
    d_act = jnp.dot(d_ffn, down_copy, preferred_element_type=jnp.float32)
    d_pre = gelu_back(d_act)[0].astype(jnp.bfloat16)
    up_grad = jnp.einsum("tc,tf->cf", hidden_low, d_pre, preferred_element_type=jnp.float32)
    d_hidden_part = jnp.einsum("tf,cf->tc", d_pre, up_copy, preferred_element_type=jnp.float32)
    d_hidden = d_resid_two + lax.psum_scatter(
        d_hidden_part.astype(jnp.bfloat16), "mp", scatter_dimension=0, tiled=True
    ).astype(jnp.float32)
    d_resid_one, d_gain_one, d_shift_one = norm_one_back(d_hidden)
    d_attn = lax.all_gather(d_resid_one.astype(jnp.bfloat16), "mp", axis=0, tiled=True)
    output_grad = jnp.einsum("td,tn->dn", d_attn, context, preferred_element_type=jnp.float32)
    d_context = jnp.dot(d_attn, out_copy, preferred_element_type=jnp.float32).astype(jnp.bfloat16)

    def row_backward(packed):
        query_rows, key_rows, value_rows, row_segments, row_lse, row_grad = packed
        scores = masked_scores(query_rows, key_rows, row_segments)
        row_probs = jnp.exp(scores - row_lse[..., None])
        grad_heads = row_grad.reshape(seq_len, heads_here, HEAD_DIM)
        d_probs = jnp.einsum(
            "qhd,khd->hqk", grad_heads, value_rows, preferred_element_type=jnp.float32
        )
        row_inner = jnp.sum(d_probs * row_probs, axis=-1, keepdims=True)
        d_scores = (row_probs * (d_probs - row_inner)).astype(jnp.bfloat16)
        d_value = jnp.einsum(
            "hqk,qhd->khd",
            row_probs.astype(jnp.bfloat16),
            grad_heads,
            preferred_element_type=jnp.float32,
        )
        d_query = (
            jnp.einsum("hqk,khd->qhd", d_scores, key_rows, preferred_element_type=jnp.float32)
            * score_scale
        )
        d_key = (
            jnp.einsum("hqk,qhd->khd", d_scores, query_rows, preferred_element_type=jnp.float32)
            * score_scale
        )
        return (
            d_query.astype(jnp.bfloat16).reshape(seq_len, local_width),
            d_key.astype(jnp.bfloat16).reshape(seq_len, local_width),
            d_value.astype(jnp.bfloat16).reshape(seq_len, local_width),
        )

    grad_context_rows = d_context.reshape(rows_here, seq_len, local_width)
    d_rows = lax.map(
        row_backward,
        (heads_split[0], heads_split[1], heads_split[2], segment_ids, lse_rows, grad_context_rows),
    )
    d_proj = jnp.stack(d_rows).reshape(3, rows_here * seq_len, local_width)
    project_grad = jnp.einsum("tc,stn->scn", tokens_in, d_proj, preferred_element_type=jnp.float32)
    d_input_part = jnp.einsum("stn,scn->tc", d_proj, proj_copy, preferred_element_type=jnp.float32)
    input_grad = d_resid_one + lax.psum_scatter(
        d_input_part.astype(jnp.bfloat16), "mp", scatter_dimension=0, tiled=True
    ).astype(jnp.float32)
    norm_local = jnp.stack([d_gain_one, d_shift_one, d_gain_two, d_shift_two])
    norm_red = lax.psum_scatter(norm_local, ("dp", "mp"), scatter_dimension=1, tiled=True)
    proj_red, out_red, up_red, down_red = (
        lax.psum_scatter(
            project_grad.astype(jnp.bfloat16), "dp", scatter_dimension=1, tiled=True
        ).astype(jnp.float32),
        lax.psum_scatter(
            output_grad.astype(jnp.bfloat16), "dp", scatter_dimension=0, tiled=True
        ).astype(jnp.float32),
        lax.psum_scatter(
            up_grad.astype(jnp.bfloat16), "dp", scatter_dimension=0, tiled=True
        ).astype(jnp.float32),
        lax.psum_scatter(
            down_grad.astype(jnp.bfloat16), "dp", scatter_dimension=0, tiled=True
        ).astype(jnp.float32),
    )
    proj_new = adam_step(proj_red, project_weight, project_momentum, project_squares, D ** (-0.5))
    out_new = adam_step(out_red, output_weight, output_momentum, output_squares, 4.0 * D ** (-0.5))
    up_new = adam_step(up_red, up_weight, up_momentum, up_squares, D ** (-0.5))
    down_new = adam_step(down_red, down_weight, down_momentum, down_squares, FF ** (-0.5))
    norm_new = adam_step(norm_red, norm_params, norm_momentum, norm_squares, 0.3)
    return (
        layer_out,
        input_grad,
        proj_new[0],
        proj_new[1],
        proj_new[2],
        proj_new[3],
        out_new[0],
        out_new[1],
        out_new[2],
        out_new[3],
        up_new[0],
        up_new[1],
        up_new[2],
        up_new[3],
        down_new[0],
        down_new[1],
        down_new[2],
        down_new[3],
        norm_new[0],
        norm_new[1],
        norm_new[2],
        norm_new[3],
    )


MESH = pl.DeviceIdType.MESH
BF16 = jnp.bfloat16
F32 = jnp.float32
ANY = pl.BlockSpec(memory_space=pl.ANY)
VMEM = pl.BlockSpec(memory_space=pltpu.VMEM)
DMA = pltpu.SemaphoreType.DMA

HOP_X, HOP_Y, HOP_C, OWN = (0, 1, 0, 0), (0, 0, 0, 1), (0, 0, 1, 0), (0, 0, 0, 0)


def hop_z(mask):
    return (mask, 0, 0, 0)


def position():
    dp = lax.axis_index("dp")
    return (dp // 4, (dp // 2) % 2, dp % 2, lax.axis_index("mp"))


def moved(me, hop):
    return tuple(m ^ h if h else m for m, h in zip(me, hop))


def device_at(me, hop):
    z, x, c, y = moved(me, hop)
    return (z * 4 + x * 2 + c, y)


def entry_barrier(me, nz):
    barrier = pltpu.get_barrier_semaphore()
    hops = [HOP_X, HOP_Y, HOP_C] + [hop_z(a) for a in range(1, nz)]
    for hop in hops:
        pl.semaphore_signal(barrier, inc=1, device_id=device_at(me, hop), device_id_type=MESH)
    pl.semaphore_wait(barrier, len(hops))


def view_rows(ref, pos):
    z, x, c, y = pos
    half = ref.shape[4] // 2
    return ref.at[z, x, c, :, pl.ds(pl.multiple_of(y * half, half), half)]


class Gather:
    def __init__(self, me, nz, out, view, send_sem, recv_sem, base):
        self.me, self.nz, self.out, self.view = me, nz, out, view
        self.send_sem, self.recv_sem, self.base = send_sem, recv_sem, base
        self.sent = []

    def slot(self, rel):
        a, b, d, e = rel
        return self.base + ((a * 2 + b) * 2 + d) * 2 + e

    def piece(self, rel):
        return self.view(self.out, moved(self.me, rel))

    def copy(self, rel, hop):
        arrives = self.slot(tuple(r ^ h for r, h in zip(rel, hop)))
        return pltpu.make_async_remote_copy(
            src_ref=self.piece(rel),
            dst_ref=self.piece(rel),
            send_sem=self.send_sem.at[arrives],
            recv_sem=self.recv_sem.at[arrives],
            device_id=device_at(self.me, hop),
            device_id_type=MESH,
        )

    def send(self, rel, *hops):
        for hop in hops:
            self.copy(rel, hop).start()
            self.sent.append((rel, hop))

    def wait(self, rel):
        self.copy(tuple(r ^ h for r, h in zip(rel, HOP_C)), HOP_C).wait_recv()

    def first_square(self):
        self.send(OWN, HOP_X, HOP_Y, HOP_C)

    def first_column(self, *levels):
        self.send(OWN, *[hop_z(a) for a in levels])

    def level(self, a):
        self.wait(hop_z(a))
        self.send(hop_z(a), HOP_X, HOP_Y, HOP_C)

    def square(self, a):
        self.wait((a, 1, 0, 0))
        if a % 4 == 0:
            self.send((a, 1, 0, 0), HOP_Y)
        self.wait((a, 0, 0, 1))
        if a % 4 == 2:
            self.send((a, 0, 0, 1), HOP_X)
        self.send((a, 1, 0, 0), HOP_C)
        self.send((a, 0, 0, 1), HOP_C)

    def diagonal(self, a):
        self.wait((a, 1, 0, 1))
        if a % 2 == 0:
            self.send((a, 1, 0, 1), hop_z(1))
        self.send((a, 1, 0, 1), HOP_C)

    def whole(self, a):
        for b in range(2):
            for e in range(2):
                self.wait((a, b, 1, e))

    def drain(self):
        for rel, hop in self.sent:
            self.copy(rel, hop).wait_send()


def sum_hops(nz):
    hops, mask = [HOP_C, HOP_X, HOP_Y], 1
    while mask < nz:
        hops.append(hop_z(mask))
        mask *= 2
    return hops


class SmallSum:
    def __init__(self, me, nz, parts, came, send_sem, recv_sem):
        self.me, self.hops, self.parts, self.came = me, sum_hops(nz), parts, came
        self.send_sem, self.recv_sem = send_sem, recv_sem

    def copy(self, i):
        return pltpu.make_async_remote_copy(
            src_ref=self.parts.at[i],
            dst_ref=self.came.at[i],
            send_sem=self.send_sem.at[i],
            recv_sem=self.recv_sem.at[i],
            device_id=device_at(self.me, self.hops[i]),
            device_id_type=MESH,
        )

    def start(self, i):
        self.copy(i).start()

    def finish(self, i):
        self.copy(i).wait()
        self.parts[i + 1] = self.parts[i] + self.came[i]


LOG2_E = 1.4426950408889634
PDF_SCALE = 0.3989422804014327


def gelu_pair(u):
    phi = 0.5 + 0.5 * lax.erf(u * 0.5**0.5)
    bell = jnp.exp2(u * u * (-0.5 * LOG2_E))
    return u * phi, phi + u * PDF_SCALE * bell


def dot_nn(a, b):
    return jnp.dot(a, b, preferred_element_type=F32)


def dot_nt(a, b):
    return lax.dot_general(a, b, (((1,), (1,)), ((), ())), preferred_element_type=F32)


def normed(rows):
    center = rows - jnp.mean(rows, axis=-1, keepdims=True)
    scale = lax.rsqrt(jnp.mean(center * center, axis=-1, keepdims=True) + EPS_NORM)
    return center * scale, scale


def norm_backward(grad, n, scale):
    inner = jnp.mean(grad * n, axis=-1, keepdims=True)
    return scale * (grad - jnp.mean(grad, axis=-1, keepdims=True) - n * inner)


def at_slots(i, plan):
    for k in sorted(plan):
        @pl.when(i == k)
        def _(k=k):
            for call in plan[k]:
                call()


def phase(count, parts, plan):
    def step(i, carry):
        for k, part in enumerate(parts):
            at_slots(i, {slot // len(parts): plan[slot] for slot in plan if slot % len(parts) == k})
            part(i)
        return carry

    lax.fori_loop(0, count, step, 0)


ACTORS = "qkvoud"
METHODS = (
    "first_square", "first_column", "level", "square", "diagonal", "whole",
    "exchange", "fetch", "join", "bend", "column",
)


def script_plans(script, actors):
    plans = {}
    for place, slots in script:
        for slot, numbers in slots:
            calls = plans.setdefault(place, {}).setdefault(slot, [])
            for number in numbers:
                actor = actors[ACTORS[number // 1000]]
                method, level = METHODS[number // 10 % 100], number % 10
                if method == "fetch":
                    actor.take_side(level)
                calls.append(functools.partial(getattr(actor, method), *(() if method == "first_square" else (level,))))
    return plans


def run_calls(plans, name):
    for call in plans.get(name, {}).get(-1, []):
        call()


def forward_kernel(nz, tokens, cotangent, seg_col, seg_row, proj, out, up, down, norm,
                   proj_all, out_all, up_all, down_all, norm_all, qkv_out, ctx_out, lse,
                   resid_out, hidden_out, act_out, slope_out, layer_out, dres_out, dffn_out, dnorm,
                   tok, cot, w_small, w_up, w_down, qkv, ctx, bias, res, hidden, act, pre, slope,
                   send_sem, recv_sem, parts, came, sum_send, sum_recv, io_sem):
    me = position()
    t_here, seq = tok.shape[0], seg_row.shape[2]
    rows_here, pairs = t_here // seq, D // 128
    copies = {}

    def begin(key, src, dst, sem):
        copies[key] = pltpu.make_async_copy(src, dst, io_sem.at[sem])
        copies[key].start()

    mine = pl.ds(pl.multiple_of(me[3] * t_here, t_here), t_here)
    begin("tok", tokens.at[mine, :], tok, 0)
    begin("cot", cotangent, cot, 1)
    parts[0] = norm[...]
    fulls = [w_small.at[i] for i in range(4)] + [w_up, w_down]
    owns = [proj.at[i] for i in range(3)] + [out, up, down]
    gathers = {
        name: Gather(me, nz, fulls[i], view_rows, send_sem, recv_sem, 8 * nz * i) for i, name in enumerate("qkvoud")
    }
    for g, own in zip(gathers.values(), owns):
        g.piece(OWN)[...] = own[...].astype(BF16)
    entry_barrier(me, nz)
    small = SmallSum(me, nz, parts, came, sum_send, sum_recv)
    plans = script_plans(FORWARD_SCRIPT, gathers)
    run_calls(plans, "start")
    small.start(0)
    for i in range(len(small.hops)):
        calls = plans.setdefault("attn", {}).setdefault(2 * i, [])
        calls.append(functools.partial(small.finish, i))
        if i + 1 < len(small.hops):
            calls.append(functools.partial(small.start, i + 1))

    def bias_step(r):
        rows = pl.ds(pl.multiple_of(r * seq, seq), seq)
        same = seg_col[rows, 0:1] == seg_row[r]
        bias[r] = jnp.where(same, 0.0, NEG_FILL)

    phase(rows_here, [bias_step], {})
    copies["tok"].wait()
    n_q, n_a, n_o, n_u = D // 256, rows_here * pairs, t_here // 256, FF // 256
    for s, name in enumerate("qkv"):
        run_calls(plans, name)

        def project_step(j, s=s):
            col = pl.ds(pl.multiple_of(j * 256, 256), 256)
            qkv[s, :, col] = dot_nn(tok[...], w_small[s, :, :, :, :, col].reshape(D, 256)).astype(BF16)

        phase(n_q, [project_step], plans.get(name + "m", {}))
    begin("proj", w_small.at[pl.ds(0, 3)], proj_all, 2)
    begin("qkv", qkv, qkv_out, 3)
    head_of = lax.broadcasted_iota(jnp.int32, (seq, 128), 1) // HEAD_DIM
    ones = jnp.ones((16, seq), BF16)

    def attend_step(u):
        r, p = u // pairs, u % pairs
        col = pl.ds(pl.multiple_of(p * 128, 128), 128)
        whole = pl.ds(pl.multiple_of(r * seq, seq), seq)
        keys, values = qkv[1, whole, col], qkv[2, whole, col].T
        keys = [jnp.where(head_of == h, keys, jnp.zeros_like(keys)) for h in range(2)]
        values = [jnp.concatenate([values[h * HEAD_DIM : (h + 1) * HEAD_DIM], ones]) for h in range(2)]
        blocks = [(low, h) for low in range(0, seq, 256) for h in range(2)]

        def score(low, h):
            q = qkv[0, pl.ds(pl.multiple_of(r * seq + low, 256), 256), col] * jnp.asarray(HEAD_DIM**-0.5, BF16)
            return dot_nt(keys[h], q) + bias[r, :, low : low + 256]

        waiting, mixed = [score(*blocks[0])], []
        for n, (low, h) in enumerate(blocks):
            if n + 1 < len(blocks):
                waiting.append(score(*blocks[n + 1]))
            scores = waiting.pop(0)
            top = jnp.max(scores, axis=0, keepdims=True)
            weights = jnp.exp(scores - top).astype(BF16)
            sums = dot_nn(values[h], weights)
            total = sums[HEAD_DIM : HEAD_DIM + 1]
            mixed.append(sums[:HEAD_DIM] * (1.0 / total))
            lse[u, h : h + 1, low : low + 256] = top + jnp.log(total)
        for n, low in enumerate(range(0, seq, 256)):
            rows = pl.ds(pl.multiple_of(r * seq + low, 256), 256)
            ctx[rows, col] = jnp.concatenate(mixed[2 * n : 2 * n + 2]).T.astype(BF16)

    phase(n_a, [attend_step], plans["attn"])
    run_calls(plans, "o")
    norm_all[...] = parts[len(small.hops)]
    begin("out", w_small.at[3], out_all, 4)
    begin("ctx", ctx, ctx_out, 5)

    def out_step(m):
        rows = pl.ds(pl.multiple_of(m * 256, 256), 256)
        attended = dot_nt(ctx[rows, :], w_small[3].reshape(D, D))
        total = tok[rows, :].astype(F32) + attended
        res[rows, :] = total
        unit, _ = normed(total)
        hidden[rows, :] = (unit * norm_all[0:1, :] + norm_all[1:2, :]).astype(BF16)

    phase(n_o, [out_step], plans.get("out", {}))
    begin("res", res, resid_out, 6)
    begin("hidden", hidden, hidden_out, 7)
    run_calls(plans, "u")
    begin("up", w_up, up_all, 8)

    n_half = 2 * FF // 256
    rows_half = t_here // 2

    def half_of(i):
        col = pl.ds(pl.multiple_of((i // 2) * 256, 256), 256)
        rows = pl.ds(pl.multiple_of((i % 2) * rows_half, rows_half), rows_half)
        return rows, col

    def up_dot(i, dst):
        rows, col = half_of(i)
        dst[...] = dot_nn(hidden[rows, :], w_up[:, :, :, :, col].reshape(D, 256))

    def up_act(i, src):
        rows, col = half_of(i)
        for k in range(0, rows_half, 64):
            part = pl.ds(pl.multiple_of((i % 2) * rows_half + k, 64), 64)
            value, tangent = gelu_pair(src[k : k + 64, :])
            act[part, col] = value.astype(BF16)
            slope[(i // 2) % 2, part, :] = tangent.astype(BF16)

    def slope_copy(j):
        col = pl.ds(pl.multiple_of(j * 256, 256), 256)
        return pltpu.make_async_copy(slope.at[j % 2], slope_out.at[:, col], io_sem.at[9 + j % 2])

    up_dot(0, pre.at[0])

    def up_step(j):
        @pl.when(j >= 2)
        def _():
            slope_copy(j - 2).wait()

        up_dot(2 * j + 1, pre.at[1])
        up_act(2 * j, pre.at[0])

    def up_next(j):
        up_dot((2 * j + 2) % n_half, pre.at[0])
        up_act(2 * j + 1, pre.at[1])
        slope_copy(j).start()

    phase(n_u, [up_step, up_next], plans.get("up", {}))
    begin("act", act, act_out, 11)
    for j in (n_u - 2, n_u - 1):
        slope_copy(j).wait()
    for key in ("cot", "res", "hidden"):
        copies[key].wait()
    dnorm[...] = jnp.zeros_like(dnorm)

    def hidden_step(m):
        rows = pl.ds(pl.multiple_of(m * 128, 128), 128)
        unit, _ = normed(res[rows, :])
        res[rows, :] = unit * norm_all[0:1, :] + norm_all[1:2, :]

    phase(t_here // 128, [hidden_step], {})
    for a in DOWN_LEVELS:
        run_calls(plans, "d%d" % a)
        level = me[0] ^ a
        width = D // nz
        col = pl.ds(pl.multiple_of(level * width, width), width)

        def down_step(m):
            rows = pl.ds(pl.multiple_of(m * 512, 512), 512)
            res[rows, col] += dot_nt(act[rows, :], w_down[level].reshape(width, FF))

        phase(t_here // 512, [down_step], {})
    begin("down", w_down, down_all, 12)

    def norm_step(m):
        rows = pl.ds(pl.multiple_of(m * 128, 128), 128)
        unit, scale = normed(res[rows, :])
        tok[rows, :] = (unit * norm_all[2:3, :] + norm_all[3:4, :]).astype(BF16)
        grad = cot[rows, :].astype(F32)
        dnorm[0:1, :] = dnorm[0:1, :] + jnp.sum(grad * unit, axis=0, keepdims=True)
        dnorm[1:2, :] = dnorm[1:2, :] + jnp.sum(grad, axis=0, keepdims=True)
        dres = norm_backward(grad * norm_all[2:3, :], unit, scale)
        res[rows, :] = dres
        hidden[rows, :] = dres.astype(BF16)

    phase(t_here // 128, [norm_step], {})
    begin("layer", tok, layer_out, 13)
    begin("dres", res, dres_out, 14)
    begin("dffn", hidden, dffn_out, 15)
    for g in gathers.values():
        g.drain()
    for key in ("proj", "out", "up", "down", "qkv", "ctx", "act", "layer", "dres", "dffn"):
        copies[key].wait()


FORWARD_SCRIPT = (
    ("start", (
        (-1, (12, 11, 1000, 0, 1013, 1012, 13, 3011, 3000, 2000, 3012,)),
    )),
    ("q", (
        (-1, (30, 2012, 22, 21, 2011, 4011, 1023, 2030, 1022, 3021, 1011, 4012, 32, 3022, 2022, 1030, 2021,
            2040, 3032, 4000, 1032, 40, 42, 23, 1040, 3013, 3030, 2013, 2032, 3042, 52, 41, 1021, 1042, 4030,
            31, 1033, 3040, 3052, 3023, 1041, 2023, 33, 3043, 43, 1031, 1043, 2042, 4022, 2050, 4013, 5011,
            1052, 5000, 4021, 53, 2041, 1051, 3041, 3031, 1053, 2031, 50, 3050, 2052, 51,)),
    )),
    ("qm", (
        (0, (1050,)),
        (3, (2043,)),
    )),
    ("k", (
        (-1, ()),
    )),
    ("km", (
        (1, (3051, 3033, 2051,)),
        (2, (2033, 5012,)),
    )),
    ("v", (
        (-1, (3053, 5013, 4040, 2053,)),
    )),
    ("attn", (
        (1, (4032,)),
        (5, (5030,)),
        (10, (4041, 4042, 4023,)),
        (13, (5022, 5021, 5040,)),
    )),
    ("o", (
        (-1, ()),
    )),
    ("out", (
        (0, (5050, 4031, 4052,)),
        (1, (4033, 4043,)),
    )),
    ("u", (
        (-1, (5041, 4050, 4053, 4051,)),
    )),
    ("up", (
        (1, (5032, 5023,)),
        (17, (5042, 5031,)),
        (26, (5033,)),
        (29, (5043, 5052, 5051,)),
    )),
    ("d0", (
        (-1, ()),
    )),
    ("d1", (
        (-1, ()),
    )),
    ("d2", (
        (-1, ()),
    )),
    ("d3", (
        (-1, (5053,)),
    )),
)
DOWN_LEVELS = (0, 1, 2, 3)


def run_forward(nz, tokens_in, cotangent, segments, proj, out, up, down, norm):
    t_here = cotangent.shape[0]
    rows_here, seq = segments.shape
    n_sum = len(sum_hops(nz))
    rows = D // (4 * nz)
    full = lambda cols: jax.ShapeDtypeStruct((nz, 2, 2, rows, cols), BF16)
    flat = lambda cols, kind: jax.ShapeDtypeStruct((t_here, cols), kind)
    seg_col = jnp.broadcast_to(segments.reshape(t_here, 1), (t_here, 128))
    seg_row = segments.reshape(rows_here, 1, seq)
    return pl.pallas_call(
        functools.partial(forward_kernel, nz),
        out_shape=[
            jax.ShapeDtypeStruct((3, nz, 2, 2, rows, D), BF16),
            full(D),
            full(FF),
            full(FF),
            jax.ShapeDtypeStruct(norm.shape, F32),
            jax.ShapeDtypeStruct((3, t_here, D), BF16),
            flat(D, BF16),
            jax.ShapeDtypeStruct((rows_here * (D // 128), 8, seq), F32),
            flat(D, F32),
            flat(D, BF16),
            flat(FF, BF16),
            flat(FF, BF16),
            flat(D, BF16),
            flat(D, F32),
            flat(D, BF16),
            jax.ShapeDtypeStruct((8, D), F32),
        ],
        in_specs=[ANY, ANY] + [VMEM] * 7,
        out_specs=[ANY] * 4 + [VMEM, ANY, ANY, VMEM] + [ANY] * 7 + [VMEM],
        scratch_shapes=[
            pltpu.VMEM((t_here, D), BF16),
            pltpu.VMEM((t_here, D), BF16),
            pltpu.VMEM((4, nz, 2, 2, rows, D), BF16),
            pltpu.VMEM((nz, 2, 2, rows, FF), BF16),
            pltpu.VMEM((nz, 2, 2, rows, FF), BF16),
            pltpu.VMEM((3, t_here, D), BF16),
            pltpu.VMEM((t_here, D), BF16),
            pltpu.VMEM((rows_here, seq, seq), F32),
            pltpu.VMEM((t_here, D), F32),
            pltpu.VMEM((t_here, D), BF16),
            pltpu.VMEM((t_here, FF), BF16),
            pltpu.VMEM((2, t_here // 2, 256), F32),
            pltpu.VMEM((2, t_here, 256), BF16),
            DMA((48 * nz,)),
            DMA((48 * nz,)),
            pltpu.VMEM((n_sum + 1,) + norm.shape, F32),
            pltpu.VMEM((n_sum,) + norm.shape, F32),
            DMA((n_sum,)),
            DMA((n_sum,)),
            DMA((16,)),
        ],
        compiler_params=pltpu.CompilerParams(
            collective_id=0, has_side_effects=True, vmem_limit_bytes=62 << 20
        ),
        name="forward",
    )(tokens_in, cotangent, seg_col, seg_row, proj, out, up, down, norm)


def view_flat(ref, pos):
    z, x, c, y = pos
    rows, half = 64, ref.shape[1] // 2
    row = (z * 4 + x * 2 + c) * rows
    return ref.at[pl.ds(pl.multiple_of(row, rows), rows), pl.ds(pl.multiple_of(y * half, half), half)]


def add_rows(dst, terms, rows=16):
    def body(i, carry):
        block = pl.ds(pl.multiple_of(i * rows, rows), rows)
        total = terms[0][block, :].astype(F32)
        for term in terms[1:]:
            total = total + term[block, :].astype(F32)
        dst[block, :] = total.astype(dst.dtype)
        return carry

    lax.fori_loop(0, dst.shape[0] // rows, body, 0)


def add_pair(dst, other, rows=16):
    def body(i, carry):
        block = pl.ds(pl.multiple_of(i * rows, rows), rows)
        dst[block, :] = dst[block, :] + other[block, :]
        return carry

    lax.fori_loop(0, dst.shape[0] // rows, body, 0)


class Scatter:
    def __init__(self, me, nz, index, grad, from_c, cut, held, swap, came, result, sems, counter, before=()):
        self.me, self.nz, self.index, self.grad, self.from_c = me, nz, index, grad, from_c
        self.cut, self.held, self.swap, self.came, self.result = cut, held, swap, came, result
        self.load_sem, self.send_sem, self.recv_sem = sems
        self.counter, self.side, self.before = counter, {}, before

    def where(self, a, b, e):
        return (a * 2 + b) * 2 + e

    def part(self, ref, i):
        return ref.at[i, :, pl.ds(*self.cut)]

    def remote(self, src, dst, slot, hop):
        sem = self.index * 8 * self.nz + slot
        return pltpu.make_async_remote_copy(
            src_ref=src, dst_ref=dst, send_sem=self.send_sem.at[sem], recv_sem=self.recv_sem.at[sem],
            device_id=device_at(self.me, hop), device_id_type=MESH,
        )

    def core_copy(self, a, b, e):
        i = self.where(a, b, e)
        return self.remote(view_flat(self.grad, moved(self.me, (a, b, 1, e))), self.from_c.at[i], i, HOP_C)

    def hop_copy(self, kind, a):
        b, e = {"w": (1, 1), "d": (1, 1), "x": (1, 0), "y": (0, 1), "z": (0, 0)}[kind]
        hop = {"w": hop_z(1), "d": HOP_Y if a % 4 == 0 else HOP_X, "x": HOP_X, "y": HOP_Y, "z": hop_z(a)}[kind]
        slot = {"w": a // 2, "d": self.nz // 2 + a // 2, "x": self.nz + a, "y": 2 * self.nz + a, "z": 3 * self.nz + a}[kind]
        return self.remote(
            self.part(self.held, self.where(a, b, e)), self.part(self.came, slot), 4 * self.nz + slot, hop
        )

    def took(self, kind, a):
        copy = self.hop_copy(kind, a)
        copy.wait_recv()
        return copy.dst_ref

    def mine(self, a, b, e):
        return self.part(self.held, self.where(a, b, e))

    def pairs(self, a):
        return [(self.where(a, b, e), b * 2 + e, (a, b, 0, e)) for b in range(2) for e in range(2)]

    def loads(self, a):
        out, side = [], self.side[a]
        for i, k, rel in self.pairs(a):
            out.append(pltpu.make_async_copy(
                view_flat(self.grad, moved(self.me, rel)), self.part(self.held, i), self.load_sem.at[side * 8 + k]
            ))
            out.append(pltpu.make_async_copy(
                self.from_c.at[i], self.part(self.swap, side * 4 + k), self.load_sem.at[side * 8 + 4 + k]
            ))
        return out

    def exchange(self, a):
        for b, e in ((1, 1), (1, 0), (0, 1), (0, 0)):
            self.core_copy(a, b, e).start()

    def take_side(self, a):
        self.side[a] = len(self.counter) % 2
        self.counter.append(a)

    def fetch(self, a):
        for other in self.before:
            other.release(a)
        for b, e in ((1, 1), (1, 0), (0, 1), (0, 0)):
            self.core_copy(a, b, e).wait_recv()
        for load in self.loads(a):
            load.start()

    def join(self, a):
        for load in self.loads(a):
            load.wait()
        for i, k, _ in self.pairs(a):
            add_pair(self.part(self.held, i), self.part(self.swap, self.side[a] * 4 + k))
        if a % 2:
            self.hop_copy("w", a).start()
        if a % 4 != 0:
            self.hop_copy("x", a).start()
        if a % 4 != 2:
            self.hop_copy("y", a).start()

    def bend(self, a):
        add_pair(self.mine(a, 1, 1), self.took("w", a))
        self.hop_copy("d", a).start()

    def square(self, a):
        kind, b, e = ("x", 1, 0) if a % 4 == 0 else ("y", 0, 1)
        add_pair(self.mine(a, b, e), self.took("d", a))
        self.hop_copy(kind, a).start()

    def column(self, a):
        terms = [self.mine(a, 0, 0), self.took("x", a), self.took("y", a)]
        if a:
            add_rows(terms[0], terms)
            self.hop_copy("z", a).start()
        else:
            add_rows(self.result, terms + [self.took("z", k) for k in range(1, self.nz)])

    def release(self, a):
        for b in range(2):
            for e in range(2):
                self.core_copy(a, b, e).wait_send()
        for kind in ("w", "x", "y", "z") if a % 2 else ("d", "x", "y", "z") if a else ("d", "x", "y"):
            self.hop_copy(kind, a).wait_send()


def transpose_into(dst, src):
    def body(i, carry):
        block = pl.ds(pl.multiple_of(i * 128, 128), 128)
        dst[:, block] = src[block, :].T
        return carry

    lax.fori_loop(0, src.shape[0] // 128, body, 0)


def backward_kernel(nz, tokens, seg_col, seg_row, proj, out, up, down, norm, qkv_in, ctx_in, lse,
                    resid, hidden, act, slope, dres, dffn, dnorm_two,
                    input_grad, *refs):
    red, norm_sum, grads, swaps, refs = refs[:6], refs[6], refs[7:13], refs[13:19], refs[19:]
    down_grad, up_grad, out_grad = grads[:3]
    (tiles, buf_a, buf_b, buf_c, total, dpre, stage, ctx, dqkv, resid_tile, dq,
     held, held_mix, swap, came_down, came_up, came_mix,
     load_sem, send_sem, recv_sem, io_sem, parts, came, sum_send, sum_recv) = refs
    me = position()
    t_here, seq = total.shape[0], seg_row.shape[2]
    rows_here, pairs = t_here // seq, D // 128
    n_ff = FF // 512
    copies = {}

    def begin(key, src, dst, sem):
        copies[key] = pltpu.make_async_copy(src, dst, io_sem.at[sem])
        copies[key].start()

    def col512(j):
        return pl.ds(pl.multiple_of(j * 512, 512), 512)

    def tile_copy(src, j, base, sem):
        return pltpu.make_async_copy(src.at[:, col512(j)], tiles.at[base + j % 2], io_sem.at[sem + j % 2])

    def stage_copy(dst, col, slot):
        return pltpu.make_async_copy(stage.at[slot], dst.at[:, col], io_sem.at[8 + slot])

    def put_stage(i, value, dst, col):
        slot = i % 2

        @pl.when(i >= 2)
        def _():
            stage_copy(dst, col, slot).wait()

        stage[slot] = value.astype(BF16)
        stage_copy(dst, col, slot).start()

    def flush_stage(dst):
        for slot in range(2):
            stage_copy(dst, pl.ds(0, 512), slot).wait()

    begin("dffn", dffn, buf_a, 10)
    begin("hidden", hidden, ctx, 11)
    begin("dres", dres, total, 12)
    tile_copy(act, 0, 0, 0).start()
    entry_barrier(me, nz)
    sems = (load_sem, send_sem, recv_sem)
    counter = []
    half = D // 2
    cuts = [(0, FF // 2)] * 2 + [(i * half, half) for i in (3, 0, 1, 2)]
    arrivals = (came_down, came_up) + (came_mix,) * 4
    scatters = {}
    for i, name in enumerate("duoqkv"):
        before = {"u": "d"}.get(name)
        scatters[name] = Scatter(
            me, nz, i, grads[i], swaps[i], cuts[i], held if name in "du" else held_mix, swap, arrivals[i], red[i],
            sems, counter,
            [scatters[before]] if before else [],
        )
    small = SmallSum(me, nz, parts, came, sum_send, sum_recv)
    n_small = len(small.hops)
    n_attn, n_m = rows_here * pairs, t_here // 256
    plans = script_plans(BACKWARD_SCRIPT, scatters)
    for i in range(n_small):
        calls = plans.setdefault("attn", {}).setdefault(2 * i + 1, [])
        calls.append(functools.partial(small.finish, i))
        if i + 1 < n_small:
            calls.append(functools.partial(small.start, i + 1))

    copies["dffn"].wait()
    transpose_into(buf_b, buf_a)

    def down_step(j):
        @pl.when(j + 1 < n_ff)
        def _():
            tile_copy(act, j + 1, 0, 0).start()

        tile_copy(act, j, 0, 0).wait()
        put_stage(j, dot_nn(buf_b[...], tiles[j % 2]), down_grad, col512(j))

    phase(n_ff, [down_step], {})
    for src, base in ((down, 2), (slope, 4), (up, 6)):
        tile_copy(src, 0, base, base).start()
    copies["hidden"].wait()
    transpose_into(buf_c, ctx)
    begin("ctx", ctx_in, ctx, 11)
    for j in range(2):
        begin(("w_out", j), out.at[:, pl.ds(j * 512, 512)], dqkv.at[j], 13 + 6 * j)
    flush_stage(down_grad)
    copies["dres"].wait()

    def pre_step(j):
        @pl.when(j + 1 < n_ff)
        def _():
            for src, base in ((down, 2), (slope, 4), (up, 6)):
                tile_copy(src, j + 1, base, base).start()

        for src, base in ((down, 2), (slope, 4), (up, 6)):
            tile_copy(src, j, base, base).wait()
        dpre[...] = (dot_nn(buf_a[...], tiles[2 + j % 2]) * tiles[4 + j % 2].astype(F32)).astype(BF16)

    def up_grad_step(j):
        put_stage(j, dot_nn(buf_c[...], dpre[...]), up_grad, col512(j))

    def hidden_step(j):
        total[...] += dot_nt(dpre[...], tiles[6 + j % 2])

    phase(n_ff, [pre_step, up_grad_step, hidden_step], plans.get("ffn", {}))
    flush_stage(up_grad)
    for i in range(6):
        begin(("qkv", i), qkv_in.at[i // 2, :, pl.ds((i % 2) * 512, 512)], tiles.at[i], i)
    norm_sum[...] = jnp.zeros_like(norm_sum)

    def resid_copy(m):
        rows = pl.ds(pl.multiple_of(m * 256, 256), 256)
        return pltpu.make_async_copy(resid.at[rows, :], resid_tile.at[m % 2], io_sem.at[14 + m % 2])

    resid_copy(0).start()

    def norm_step(m):
        @pl.when(m + 1 < n_m)
        def _():
            resid_copy(m + 1).start()

        resid_copy(m).wait()
        rows = pl.ds(pl.multiple_of(m * 256, 256), 256)
        unit, scale = normed(resid_tile[m % 2])
        grad = total[rows, :]
        norm_sum[0:1, :] = norm_sum[0:1, :] + jnp.sum(grad * unit, axis=0, keepdims=True)
        norm_sum[1:2, :] = norm_sum[1:2, :] + jnp.sum(grad, axis=0, keepdims=True)
        moved_grad = norm_backward(grad * norm[0:1, :], unit, scale)
        total[rows, :] = moved_grad
        buf_b[rows, :] = moved_grad.astype(BF16)

    phase(n_m, [norm_step], plans.get("ln", {}))
    norm_sum[2:4, :] = dnorm_two[0:2, :]
    parts[0] = norm_sum[...]
    small.start(0)
    transpose_into(buf_a, buf_b)
    copies["ctx"].wait()
    for j in range(2):
        copies[("w_out", j)].wait()

    def out_grad_step(j):
        put_stage(j, dot_nn(buf_a[...], ctx[:, col512(j)]), out_grad, col512(j))

    phase(2, [out_grad_step], plans.get("out", {}))
    flush_stage(out_grad)

    def ctx_step(j):
        buf_a[:, col512(j)] = dot_nn(buf_b[...], dqkv[j]).astype(BF16)

    phase(2, [ctx_step], plans.get("ctx", {}))
    mine = pl.ds(pl.multiple_of(me[3] * t_here, t_here), t_here)
    begin("tok", tokens.at[mine, :], buf_b, 10)

    bias = resid_tile

    def bias_step(r):
        for k in range(2):
            rows = pl.ds(pl.multiple_of(r * seq + k * (seq // 2), seq // 2), seq // 2)
            bias[r, :, k * seq : (k + 1) * seq] = jnp.where(seg_col[rows, 0:1] == seg_row[r], 0.0, NEG_FILL)

    phase(rows_here, [bias_step], {})
    for i in range(6):
        copies[("qkv", i)].wait()
    head_of = lax.broadcasted_iota(jnp.int32, (128, 128), 1) // HEAD_DIM
    head_pick = (
        lax.broadcasted_iota(jnp.int32, (8, 128), 1) // HEAD_DIM == lax.broadcasted_iota(jnp.int32, (8, 128), 0)
    ).astype(BF16)
    shrink = jnp.asarray(HEAD_DIM**-0.5, BF16)

    def per_head(block):
        return jnp.concatenate([jnp.where(head_of == h, block, jnp.zeros_like(block)) for h in range(2)])

    def attend_step(u):
        r, p = u // pairs, u % pairs
        side = p // 4
        col = pl.ds(pl.multiple_of(p * 128, 128), 128)
        near = pl.ds(pl.multiple_of((p % 4) * 128, 128), 128)
        whole = pl.ds(pl.multiple_of(r * seq, seq), seq)
        product = buf_a[whole, col].astype(F32) * ctx[whole, col].astype(F32)
        coarse = product.astype(BF16)
        fine = (product - coarse.astype(F32)).astype(BF16)
        delta = dot_nt(head_pick, coarse) + dot_nt(head_pick, fine)
        dq[...] = jnp.zeros_like(dq)
        n_blocks = seq // 128

        def block_of(kb):
            low, high = max(0, kb - 2) * 128, min(n_blocks, kb + 3) * 128
            k_rows = pl.ds(pl.multiple_of(r * seq + kb * 128, 128), 128)
            q_rows = pl.ds(pl.multiple_of(r * seq + low, 128), high - low)
            return low, high, k_rows, q_rows

        def products(kb):
            low, high, k_rows, q_rows = block_of(kb)
            q = tiles[side, q_rows, near] * shrink
            keys = per_head(tiles[2 + side, k_rows, near])
            return keys, q, dot_nt(keys, q), dot_nt(per_head(tiles[4 + side, k_rows, near]), buf_a[q_rows, col])

        waiting = [products(0)]
        for kb in range(n_blocks):
            if kb + 1 < n_blocks:
                waiting.append(products(kb + 1))
            keys, q, scores, d_probs = waiting.pop(0)
            low, high, k_rows, q_rows = block_of(kb)
            top, left = kb * 128 % (seq // 2), kb * 128 // (seq // 2) * seq
            block = bias[r, top : top + 128, left + low : left + high]
            probs, d_scores = [], []
            for h in range(2):
                part = slice(h * 128, h * 128 + 128)
                prob = jnp.exp(scores[part] + block - lse[u, h : h + 1, low:high])
                probs.append(prob.astype(BF16))
                d_scores.append((prob * (d_probs[part] - delta[h : h + 1, low:high])).astype(BF16))
            probs, d_scores = jnp.concatenate(probs), jnp.concatenate(d_scores)
            d_value = dot_nn(probs, buf_a[q_rows, col])
            d_key = dot_nn(d_scores, q)
            dqkv[4 + side, k_rows, near] = jnp.where(head_of == 0, d_value[:128], d_value[128:]).astype(BF16)
            dqkv[2 + side, k_rows, near] = jnp.where(head_of == 0, d_key[:128], d_key[128:]).astype(BF16)
            dq[:, low:high] += dot_nn(keys.T, d_scores)
        dqkv[side, whole, near] = (dq[...].T * HEAD_DIM**-0.5).astype(BF16)

    phase(n_attn, [attend_step], plans["attn"])
    for i in range(6):
        begin(("proj", i), proj.at[i // 2, :, pl.ds((i % 2) * 512, 512)], tiles.at[i], i)
    copies["tok"].wait()
    transpose_into(buf_c, buf_b)

    for s, name in enumerate("qkv"):

        def project_step(i, s=s):
            put_stage(i, dot_nn(buf_c[...], dqkv[2 * s + i]), grads[3 + s], col512(i))

        phase(2, [project_step], plans.get("p" + name, {}))
        flush_stage(grads[3 + s])
    for i in range(6):
        copies[("proj", i)].wait()
    def in_copy(m):
        rows = pl.ds(pl.multiple_of(m * 256, 256), 256)
        return pltpu.make_async_copy(total.at[rows, :], input_grad.at[rows, :], io_sem.at[16 + m])

    def input_step(m):
        rows = pl.ds(pl.multiple_of(m * 256, 256), 256)
        value = total[rows, :]
        for i in range(6):
            value = value + dot_nt(dqkv[i, rows, :], tiles[i])
        total[rows, :] = value

    phase(n_m, [input_step], plans.get("in", {}))
    for m in range(n_m):
        in_copy(m).start()
    run_calls(plans, "end")
    for name in "uoqkv":
        for a in range(nz):
            scatters[name].release(a)
    for m in range(n_m):
        in_copy(m).wait()
    norm_sum[...] = parts[n_small]


BACKWARD_SCRIPT = (
    ("ffn", (
        (0, (5061, 5062,)),
        (4, (5071, 5063, 5060,)),
        (6, (5081,)),
        (7, (5073, 5072,)),
        (9, (5083, 5082, 5070,)),
        (11, (5080, 5090,)),
        (14, (5092, 5103,)),
        (23, (5030, 5032,)),
    )),
    ("ln", (
        (1, (4063, 4061, 5101, 4062, 4060,)),
    )),
    ("out", (
        (0, (4073,)),
        (1, (5102,)),
    )),
    ("ctx", (
        (1, (3061, 4071, 3062, 4083, 3060, 3063,)),
    )),
    ("attn", (
        (0, (4081, 4072,)),
        (2, (4082, 3071, 3072,)),
        (3, (4103, 3081, 3082, 3070, 3073, 5100, 4092, 3080, 3083, 4070,)),
        (5, (4080,)),
        (9, (3101, 4090, 3090, 4101,)),
        (13, (4032, 3092, 3103,)),
    )),
    ("pq", (
        (0, (3032, 4030, 3030,)),
    )),
    ("pk", (
        (0, (4102, 3102, 63, 61, 62, 60,)),
    )),
    ("pv", (
        (0, (73,)),
        (1, (83, 71, 1063, 72, 1062, 1061, 1060, 81, 82, 70,)),
    )),
    ("in", (
        (0, (103, 80, 1071, 92, 2063, 1072, 2061, 101, 1081, 4100, 1070, 1082, 1073, 2060, 90, 1080, 2073,
            1083, 2071, 32, 2062, 2083,)),
        (1, (1101, 30, 1090, 2081, 2072, 2070, 1092, 3100,)),
        (2, (2082, 2092, 1103, 2080, 102,)),
        (3, (1030, 1032, 2090, 2103, 2101,)),
    )),
    ("end", (
        (-1, (2032, 1102, 2030, 100, 2102, 1100, 2100,)),
    )),
)


def run_backward(nz, tokens_in, segments, proj, out, up, down, norm, qkv, ctx, lse,
                 resid, hidden, act, slope, dres, dffn, dnorm_two):
    t_here = dffn.shape[0]
    rows_here, seq = segments.shape
    n_sum = len(sum_hops(nz))
    piece = (64, FF // 2)
    seg_col = jnp.broadcast_to(segments.reshape(t_here, 1), (t_here, 128))
    seg_row = segments.reshape(rows_here, 1, seq)
    widths = (FF // 2,) * 2 + (D // 2,) * 4
    reduced = [jax.ShapeDtypeStruct((64, w), F32) for w in widths]
    grads = [jax.ShapeDtypeStruct((D, 2 * w), BF16) for w in widths]
    swapped = [jax.ShapeDtypeStruct((4 * nz, 64, w), BF16) for w in widths]
    results = pl.pallas_call(
        functools.partial(backward_kernel, nz),
        out_shape=[jax.ShapeDtypeStruct((t_here, D), F32)] + reduced + [jax.ShapeDtypeStruct(norm.shape, F32)]
        + grads + swapped,
        in_specs=[ANY, VMEM, VMEM] + [ANY] * 4 + [VMEM, ANY, ANY, VMEM] + [ANY] * 6 + [VMEM],
        out_specs=[ANY] + [VMEM] * 7 + [ANY] * 12,
        scratch_shapes=[
            pltpu.VMEM((8, t_here, 512), BF16),
            pltpu.VMEM((t_here, D), BF16),
            pltpu.VMEM((t_here, D), BF16),
            pltpu.VMEM((t_here, D), BF16),
            pltpu.VMEM((t_here, D), F32),
            pltpu.VMEM((t_here, 512), BF16),
            pltpu.VMEM((2, t_here, 512), BF16),
            pltpu.VMEM((t_here, D), BF16),
            pltpu.VMEM((6, t_here, 512), BF16),
            pltpu.VMEM((2, 256, D), F32),
            pltpu.VMEM((128, seq), F32),
            pltpu.VMEM((4 * nz,) + piece, BF16),
            pltpu.VMEM((4 * nz,) + piece, BF16),
            pltpu.VMEM((8,) + piece, BF16),
            pltpu.VMEM((4 * nz,) + piece, BF16),
            pltpu.VMEM((4 * nz,) + piece, BF16),
            pltpu.VMEM((4 * nz,) + piece, BF16),
            DMA((16,)),
            DMA((48 * nz,)),
            DMA((48 * nz,)),
            DMA((20,)),
            pltpu.VMEM((n_sum + 1,) + norm.shape, F32),
            pltpu.VMEM((n_sum,) + norm.shape, F32),
            DMA((n_sum,)),
            DMA((n_sum,)),
        ],
        compiler_params=pltpu.CompilerParams(
            collective_id=1, has_side_effects=True, vmem_limit_bytes=62 << 20
        ),
        name="backward",
    )(tokens_in, seg_col, seg_row, proj, out, up, down, norm, qkv, ctx, lse,
      resid, hidden, act, slope, dres, dffn, dnorm_two)
    return results[:8]


def local_rows(
    tokens_in,
    cotangent,
    segment_ids,
    project_weight,
    project_momentum,
    project_squares,
    output_weight,
    output_momentum,
    output_squares,
    up_weight,
    up_momentum,
    up_squares,
    down_weight,
    down_momentum,
    down_squares,
    norm_params,
    norm_momentum,
    norm_squares,
):
    nz = lax.axis_size("dp") // 4
    dp, mp = lax.axis_index("dp"), lax.axis_index("mp")
    norm_cols = norm_params.shape[1]
    norm_start = (dp * 2 + mp) * norm_cols
    norm_wide = lax.dynamic_update_slice(
        jnp.zeros((8, D), F32), norm_params.astype(BF16).astype(F32), (0, norm_start)
    )
    rows_here = segment_ids.shape[0] // 2
    segments = lax.dynamic_slice_in_dim(segment_ids, mp * rows_here, rows_here, 0)
    (proj_w, out_w, up_w, down_w, norm_full, qkv, context, lse, resid_one, hidden_low, act_low, slope,
     layer_out, d_resid_two, d_ffn, d_norm_two) = run_forward(
        nz,
        tokens_in,
        cotangent,
        segments,
        project_weight,
        output_weight,
        up_weight,
        down_weight,
        norm_wide,
    )
    input_grad, down_red, up_red, out_red, *proj_red, norm_sum = run_backward(
        nz,
        tokens_in,
        segments,
        proj_w.reshape(3, D, D),
        out_w.reshape(D, D),
        up_w.reshape(D, FF),
        down_w.reshape(D, FF),
        norm_full,
        qkv,
        context,
        lse,
        resid_one,
        hidden_low,
        act_low,
        slope,
        d_resid_two,
        d_ffn,
        d_norm_two,
    )
    proj_red = jnp.stack(proj_red)
    norm_red = lax.dynamic_slice(norm_sum, (0, norm_start), (4, norm_cols))
    return (
        layer_out,
        input_grad,
        *adam_step(proj_red, project_weight, project_momentum, project_squares, D ** (-0.5)),
        *adam_step(out_red, output_weight, output_momentum, output_squares, 4.0 * D ** (-0.5)),
        *adam_step(up_red, up_weight, up_momentum, up_squares, D ** (-0.5)),
        *adam_step(down_red, down_weight, down_momentum, down_squares, FF ** (-0.5)),
        *adam_step(norm_red, norm_params, norm_momentum, norm_squares, 0.3),
    )


def by_rows(mesh):
    dp, mp = mesh.shape["dp"], mesh.shape["mp"]
    return mp == 2 and dp >= 8 and dp & (dp - 1) == 0 and D % (64 * dp) == 0


def solution(mesh):
    body = local_rows if by_rows(mesh) else local_plain
    return jax.shard_map(
        body,
        mesh=mesh,
        in_specs=(
            P("dp", None),
            P(("dp", "mp"), None),
            P("dp", None),
            P(None, "dp", "mp"),
            P(None, "dp", "mp"),
            P(None, "dp", "mp"),
            P("dp", "mp"),
            P("dp", "mp"),
            P("dp", "mp"),
            P("dp", "mp"),
            P("dp", "mp"),
            P("dp", "mp"),
            P("dp", "mp"),
            P("dp", "mp"),
            P("dp", "mp"),
            P(None, ("dp", "mp")),
            P(None, ("dp", "mp")),
            P(None, ("dp", "mp")),
        ),
        out_specs=(
            P(("dp", "mp"), None),
            P(("dp", "mp"), None),
            P(None, "dp", "mp"),
            P(None, "dp", "mp"),
            P(None, "dp", "mp"),
            P(None, "dp", "mp"),
            P("dp", "mp"),
            P("dp", "mp"),
            P("dp", "mp"),
            P("dp", "mp"),
            P("dp", "mp"),
            P("dp", "mp"),
            P("dp", "mp"),
            P("dp", "mp"),
            P("dp", "mp"),
            P("dp", "mp"),
            P("dp", "mp"),
            P("dp", "mp"),
            P(None, ("dp", "mp")),
            P(None, ("dp", "mp")),
            P(None, ("dp", "mp")),
            P(None, ("dp", "mp")),
        ),
        check_vma=False,
    )
```
